128 devices in a mesh: gx: 16 (over x, y), gy: 8 (over z, core).
Axes of the slice: x: 4, y: 4, z: 4, core: 2. Of those that a mesh axis runs over, the one named last changes fastest.
Arguments:
- state_in: float32 [4, 32768, 16, 128], P(None, ('gx', 'gy')), may hold values from -6 to 6
- stiffness: float32 [16, 16, 32768], P(None, None, ('gx', 'gy')), may hold values from -1.5 to 1.5
- elem_cell: int32 [32768], P(('gx', 'gy')), may hold values from 0 to 32767, as said below
- group_column: int32 [131072], P(('gx', 'gy')), may hold values from 0 to 131071, as said below
- group_inverse: bfloat16 [8192, 128, 128], P(('gx', 'gy')), may hold values from 0 to 0.875
Outputs:
- state_out: float32 [4, 32768, 16, 128], P(None, ('gx', 'gy'))
The draws below stay inside these ranges and needn't reach their ends.
Inputs may be any that keep to these rules, and one draw needn't show every extreme that they name: `elem_cell`: device i * 8 + j (index i along gx, j along gy) holds in its 256 slots, in some order, exactly the cells with x from i * 16 to (i + 1) * 16 - 1 and y from j * 16 to (j + 1) * 16 - 1; every cell is held once. `group_column`: every column is named once. Column c lies on device c // 1024, slot p on device p // 1024; the 1024 slots of each device name exactly 8 columns of each device.
All inputs are finite; a program needn't handle non-finite values.
Results may differ from the reference program's by a relative error of at most 0.0031.
Values may be sent and summed in bfloat16 or wider, within the bound.
A program may use at most 128 MiB of HBM per device.

```python
import math
import jax
import jax.numpy as jnp
from jax import lax

LEV = 128
NF = 4
NP = 16
GROUP_COLS = 16
EXD = 16
EYD = 16
COL_DEV = 1024
EX = 256
EY = 128
NELEM = 32768
NCOL = 131072
GROUPS = 8192
N_GX = 16
N_GY = 8


def draw_elem_cell(key, part):
    devices = N_GX * N_GY
    per_device = EXD * EYD
    keys = jax.random.split(key, devices)
    orders = jax.vmap(lambda single: jax.random.permutation(single, per_device))(keys).astype(jnp.int32)
    device_ids = jnp.arange(devices, dtype=jnp.int32)[:, None]
    cell_x = device_ids // N_GY * EXD + orders // EYD
    cell_y = device_ids % N_GY * EYD + orders % EYD
    return (cell_x * EY + cell_y).reshape(-1).astype(jnp.int32)


def draw_group_column(key, part):
    devices = N_GX * N_GY
    per_peer = COL_DEV // devices
    first_key, second_key = jax.random.split(key)
    chosen = jax.vmap(lambda single: jax.random.permutation(single, COL_DEV))(jax.random.split(first_key, devices)).astype(jnp.int32)
    slot_draw = jax.vmap(lambda single: jax.random.permutation(single, COL_DEV))(jax.random.split(second_key, devices)).astype(jnp.int32)
    source = slot_draw // per_peer
    within = slot_draw % per_peer
    dest_ids = jnp.arange(devices, dtype=jnp.int32)[:, None]
    local_index = chosen[source, dest_ids * per_peer + within]
    return (source * COL_DEV + local_index).reshape(-1).astype(jnp.int32)


def draw_group_inverse(key, part):
    first_key, second_key = jax.random.split(key)
    length_scale = jnp.exp(jax.random.uniform(first_key, (GROUPS, 1, 1), jnp.float32, 0.0, math.log(16.0)))
    factor = jax.random.uniform(second_key, (GROUPS, LEV, LEV), jnp.float32, 0.5, 1.5)
    levels_row = jnp.arange(LEV, dtype=jnp.float32)[:, None]
    levels_col = jnp.arange(LEV, dtype=jnp.float32)[None, :]
    distance = jnp.abs(levels_row - levels_col)[None, :, :]
    values = factor * jnp.exp(-distance / length_scale) / (1.0 + 2.0 * length_scale)
    return values.astype(jnp.bfloat16)


def block_scale(key, shape, cuts, least, top_value):
    factor_of, own = 1.0, jax.random.fold_in(key, 6)
    for dim, shards_of in cuts:
        draws = jnp.exp(jax.random.uniform(jax.random.fold_in(own, dim), (shards_of,), jnp.float32, least / len(cuts), top_value / len(cuts)))
        factor_of = factor_of * jnp.repeat(draws, shape[dim] // shards_of).reshape([-1 if axis == dim else 1 for axis in range(len(shape))])
    return factor_of


def bell_draw(key, extent, deviation, most, shards=(), kind=jnp.bfloat16):
    loudness = block_scale(key, extent, shards, -0.22, 0.18) if shards else 1.0
    values = jax.random.normal(key, extent, jnp.float32) * deviation * loudness
    return jnp.minimum(jnp.maximum(values, -most), most).astype(kind)


def setup_inputs(seed: int = 0) -> dict:
    splits = jax.random.split(jax.random.key(seed), 6)
    state_in = bell_draw(splits[0], (NF, NELEM, NP, LEV), 1.0, 6.0, ((1, 128),), jnp.float32)
    stiffness = bell_draw(splits[1], (NP, NP, NELEM), NP ** -0.5, 1.5, ((2, 128),), jnp.float32)
    elem_cell = draw_elem_cell(jax.random.fold_in(splits[5], 71), 0)
    group_column = draw_group_column(jax.random.fold_in(splits[5], 71), 0)
    group_inverse = draw_group_inverse(jax.random.fold_in(splits[5], 71), 0)
    return dict(state_in=state_in, stiffness=stiffness, elem_cell=elem_cell, group_column=group_column, group_inverse=group_inverse)


exact_mode = lax.Precision.HIGHEST

def lagrange_value(node_index, position, gll_nodes):
    running = 1.0
    for other_index in range(4):
        if other_index != node_index:
            running = running * (position - gll_nodes[other_index]) / (gll_nodes[node_index] - gll_nodes[other_index])
    return running

def half_tables():
    gll_nodes = [-1.0, -1.0 / math.sqrt(5.0), 1.0 / math.sqrt(5.0), 1.0]
    halves = [[0.0] * 4, [0.0] * 4]
    for half_index, bounds in enumerate(((-1.0, 0.0), (0.0, 1.0))):
        lower_end, upper_end = bounds
        centre_point = 0.5 * (lower_end + upper_end)
        offset_gauss = 0.5 * (upper_end - lower_end) / math.sqrt(3.0)
        for node_index in range(4):
            first_value = lagrange_value(node_index, centre_point - offset_gauss, gll_nodes)
            second_value = lagrange_value(node_index, centre_point + offset_gauss, gll_nodes)
            halves[half_index][node_index] = 0.5 * (upper_end - lower_end) * (first_value + second_value)
    product = [[sum((halves[row_index][k_index] * halves[col_index][k_index] for k_index in range(4))) for col_index in range(2)] for row_index in range(2)]
    determinant = product[0][0] * product[1][1] - product[0][1] * product[1][0]
    inverse = [[product[1][1] / determinant, -product[0][1] / determinant], [-product[1][0] / determinant, product[0][0] / determinant]]
    spread = [[sum((halves[k_index][node_index] * inverse[k_index][col_index] for k_index in range(2))) for col_index in range(2)] for node_index in range(4)]
    return (jnp.asarray(halves, jnp.float32), jnp.asarray(spread, jnp.float32))

def assemble(element_grid):
    from_west = jnp.roll(element_grid[:, :, 3], 1, axis=0)
    from_east = jnp.roll(element_grid[:, :, 0], -1, axis=0)
    across = element_grid.at[:, :, 0].add(from_west).at[:, :, 3].add(from_east)
    from_south = jnp.roll(across[:, :, :, 3], 1, axis=1)
    from_north = jnp.roll(across[:, :, :, 0], -1, axis=1)
    summed = across.at[:, :, :, 0].add(from_south).at[:, :, :, 3].add(from_north)
    sharing = jnp.array([2.0, 1.0, 1.0, 2.0], jnp.float32)
    return summed / (sharing[:, None] * sharing[None, :])[:, :, None]

def reference(state_in, stiffness, elem_cell, group_column, group_inverse):
    halves, spread = half_tables()
    slot_of_cell = jnp.zeros((NELEM,), jnp.int32).at[elem_cell].set(jnp.arange(NELEM, dtype=jnp.int32))
    column_of_slot = jnp.zeros((NCOL,), jnp.int32).at[group_column].set(jnp.arange(NCOL, dtype=jnp.int32))
    inverse_wide = group_inverse.astype(jnp.float32)

    def one_field(one_state):
        local_term = jnp.einsum('nme,eml->enl', stiffness, one_state, precision=exact_mode)
        combined = one_state + local_term
        element_grid = combined[slot_of_cell].reshape(EX, EY, 4, 4, LEV)
        dynamics = assemble(element_grid)
        columns = jnp.einsum('ia,jb,xyabl->xyijl', halves, halves, dynamics, precision=exact_mode).astype(jnp.bfloat16)
        columns = columns.reshape(NELEM, 4, LEV)[elem_cell].reshape(NCOL, LEV)
        physics = columns[group_column].reshape(GROUPS, GROUP_COLS, LEV).astype(jnp.float32)
        smoothed = jnp.einsum('gkl,gjl->gjk', inverse_wide, physics, precision=exact_mode)
        tendency = (smoothed - physics).astype(jnp.bfloat16).reshape(NCOL, LEV)
        returned = tendency[column_of_slot]
        back_grid = returned.reshape(NELEM, 2, 2, LEV)[slot_of_cell].astype(jnp.float32)
        on_nodes = jnp.einsum('ai,bj,eijl->eabl', spread, spread, back_grid, precision=exact_mode)
        updated = dynamics + assemble(on_nodes.reshape(EX, EY, 4, 4, LEV))
        return updated.reshape(NELEM, 16, LEV)[elem_cell]
    return lax.map(one_field, state_in)
```

```python
import functools
import math

import jax
import jax.numpy as jnp
import ml_dtypes
import numpy as np
from jax import lax
from jax.experimental import pallas as pl
from jax.experimental.pallas import tpu as pltpu
from jax.sharding import PartitionSpec as P

F32, BF16, I32 = jnp.float32, jnp.bfloat16, jnp.int32
MESH = pl.DeviceIdType.MESH
NX, NY = 16, 8
ND = NX * NY
TX = TY = 16
NE = TX * TY
NC = 4 * NE
LEV = 128
NH = 2
WEST, EAST, SOUTH, NORTH = 0, 18, 36, 52
NHALO = 68
RX = 80
RROWS = 18 * RX + 16
CORNERS = (
    (1, 1, 4, 15, 15, 15),
    (-1, 1, 5, 0, 15, 3),
    (1, -1, 6, 15, 0, 12),
    (-1, -1, 7, 0, 0, 0),
)


def lagrange_value(node, position, nodes):
    value = 1.0
    for other in range(4):
        if other != node:
            value *= (position - nodes[other]) / (nodes[node] - nodes[other])
    return value


def tables():
    nodes = [-1.0, -1.0 / math.sqrt(5.0), 1.0 / math.sqrt(5.0), 1.0]
    halves = np.zeros((2, 4))
    for i, (low, high) in enumerate(((-1.0, 0.0), (0.0, 1.0))):
        centre, offset = 0.5 * (low + high), 0.5 * (high - low) / math.sqrt(3.0)
        for a in range(4):
            halves[i, a] = (
                0.5
                * (high - low)
                * (
                    lagrange_value(a, centre - offset, nodes)
                    + lagrange_value(a, centre + offset, nodes)
                )
            )
    spread = halves.T @ np.linalg.inv(halves @ halves.T)
    return halves.astype(np.float32).astype(np.float64), spread.astype(np.float32).astype(np.float64)


def split_bf16(table):
    high = table.astype(ml_dtypes.bfloat16)
    low = (table - high.astype(np.float64)).astype(ml_dtypes.bfloat16)
    return high, low


def constant_tables():
    halves, spread = tables()
    cols = np.einsum("ia,jb,yz->iyjzab", halves, halves, np.eye(TY)).reshape(64, 256)
    col_high, col_low = split_bf16(cols)
    along = np.zeros((4, 3, 2))
    along[:, 1, :] = spread
    along[0, 0, :] += spread[3]
    along[3, 2, :] += spread[0]
    along[0] *= 0.5
    along[3] *= 0.5
    along_y = np.zeros((TY, 4, 40))
    for y in range(TY):
        for step in range(3):
            other = y + step - 1
            base = 32 if other < 0 else 34 if other >= TY else 2 * other
            along_y[y, :, base : base + 2] += along[:, step, :]
    update = np.zeros((256, 256))
    update[:, :240] = np.einsum("asi,ybr->yabsir", along, along_y).reshape(256, 240)
    up_high, up_low = split_bf16(update)
    return np.concatenate([col_high, col_low], 0), np.concatenate([up_high, up_low], 0)


def iota(shape, dim):
    return lax.broadcasted_iota(I32, shape, dim)


def dot(left, right):
    return jnp.dot(left, right, preferred_element_type=F32)


def dot_nt(left, right):
    return lax.dot_general(left, right, (((1,), (1,)), ((), ())), preferred_element_type=F32)


class Peers:
    def __init__(self, gx, gy):
        self.x, self.y = lax.div(gx, 4), lax.rem(gx, 4)
        self.z, self.core = lax.div(gy, 2), lax.rem(gy, 2)
        self.xs = [lax.rem(self.x + a, 4) * 4 for a in range(4)]
        self.zs = [lax.rem(self.z + d, 4) * 2 for d in range(4)]
        self.cores = [self.core, 1 - self.core]

    def block(self, b, with_self=False):
        ys = [lax.rem(self.y + b + a, 4) for a in range(4)]
        back_b = lax.rem(4 - b, 4) if not isinstance(b, int) else -b % 4
        found = []
        for d in range(4):
            for a in range(4):
                for c in range(2):
                    if isinstance(b, int) and b == d == a == c == 0 and not with_self:
                        continue
                    tgx = self.xs[a] + ys[a]
                    tgy = self.zs[(d + a) % 4] + self.cores[c]
                    inner = d * 8 + a * 2 + c
                    back = -d % 4 * 8 + -a % 4 * 2 + c
                    found.append((tgx, tgy, b * 32 + inner, back_b * 32 + back))
        return found

    def position(self, source):
        a = ((source >> 5) - self.x) & 3
        b = (((source >> 3) & 3) - self.y - a) & 3
        d = (((source >> 1) & 3) - self.z - a) & 3
        c = ((source & 1) - self.core) & 1
        return b * 32 + d * 8 + a * 2 + c


def combine_kernel(cell_ref, state_hbm, stiff_hbm, out_ref, st, xs, w, stiff_sem, state_sem):
    stiff_copy = pltpu.make_async_copy(stiff_hbm, xs, stiff_sem)
    stiff_copy.start()
    loads = []
    for part in range(8):
        rows = pl.ds(part * 512, 512)
        copy = pltpu.make_async_copy(state_hbm.at[:, rows], st.at[:, rows], state_sem.at[part])
        copy.start()
        loads.append(copy)
    stiff_copy.wait()
    flipped = xs[...].T.astype(BF16)
    row_i, col_i = iota((256, 256), 0), iota((256, 256), 1)
    same_m = (row_i & 15) == (col_i & 15)
    diagonal = (row_i & 15) == (col_i >> 4)
    for n in range(16):
        pick = jnp.where(same_m & ((row_i >> 4) == n), 1.0, 0.0).astype(BF16)
        block = jnp.where(diagonal, dot(flipped, pick), 0.0)
        for u in range(2):
            w[u, pl.ds(n, 256, stride=16), :] = block[:, u * 128 : (u + 1) * 128]

    def step(g, carry):
        rows = pl.ds(pl.multiple_of(g * 256, 256), 256)
        state = jnp.concatenate([st[f, rows, :] for f in range(4)], axis=1)
        oper = jnp.concatenate([w[0, rows, :], w[1, rows, :]], axis=1).astype(BF16)
        state = state + dot(oper, state.astype(BF16))
        for e in range(16):
            cell = cell_ref[g * 16 + e]
            tile = ((cell >> 7) & 15) * 16 + (cell & 15)
            target = pl.ds(pl.multiple_of(tile * 16, 16), 16)
            for f in range(4):
                out_ref[f, target, :] = state[e * 16 : e * 16 + 16, f * 128 : f * 128 + 128]
        return carry

    for part in range(8):
        loads[part].wait()
        lax.fori_loop(part * 2, part * 2 + 2, step, 0)


def exchange_kernel(
    st, cell_ref, gcol_ref, inv, coltab_ref,
    dyn, gridb,
    halo, wv, wq, mid, req, qrow, crow,
    sel, sel_t, place, place_t,
    dyn_high, dyn_low, cols, outb, incb, backb, rcvb, flat, tend, grid,
    sx, sy, sc, rx, ry, rc,
    tx, ty, tc, ux, uy, uc,
    wsend, wrecv, vsend, vrecv, loc_sem,
    fsend, frecv, bsend, brecv, hsend, hrecv, gsend, grecv,
):
    gx, gy = lax.axis_index("gx"), lax.axis_index("gy")
    peers = Peers(gx, gy)
    barrier = pltpu.get_barrier_semaphore()

    def other_x(k):
        return lax.rem(gx + k, NX)

    def other_y(k):
        return lax.rem(gy + k, NY)

    for dgx, dgy, _, _, _, _ in CORNERS:
        pl.semaphore_signal(
            barrier, inc=1, device_id=(other_x(NX + dgx), other_y(NY + dgy)), device_id_type=MESH
        )

    def greet_x(k, carry):
        pl.semaphore_signal(barrier, inc=1, device_id=(other_x(k), gy), device_id_type=MESH)
        return carry

    def greet_y(k, carry):
        pl.semaphore_signal(barrier, inc=1, device_id=(gx, other_y(k)), device_id_type=MESH)
        return carry

    lax.fori_loop(1, NX, greet_x, 0)
    lax.fori_loop(1, NY, greet_y, 0)


    lane = iota((128, 128), 1)
    sub = iota((128, 128), 0)
    eye = lane == sub

    def to_col(row):
        return jnp.sum(jnp.where(eye, jnp.broadcast_to(row, (128, 128)), 0.0), axis=1, keepdims=True)

    def to_row(col):
        return jnp.sum(jnp.where(eye, jnp.broadcast_to(col, (128, 128)), 0.0), axis=0, keepdims=True)

    upper = jnp.where(sub < lane, 1.0, 0.0).astype(BF16)
    seen = jnp.zeros((128, 1), F32)
    want_high = jnp.zeros((128, 128), F32)
    want_low = jnp.zeros((128, 128), F32)
    for block in range(8):
        named = gcol_ref[block : block + 1, :]
        source, local = named >> 10, named & 1023
        hit = jnp.broadcast_to(source, (128, 128)) == sub
        onehot = jnp.where(hit, 1.0, 0.0)
        before = dot(onehot.astype(BF16), upper) + seen
        seen = seen + jnp.sum(onehot, axis=1, keepdims=True)
        rank = jnp.sum(jnp.where(hit, before, 0.0), axis=0, keepdims=True)
        qrow[block : block + 1, :] = peers.position(source).astype(F32) * 8.0 + rank
        ranked = jnp.broadcast_to(rank, (128, 128)) == sub.astype(F32)
        high = (local >> 5).astype(F32)
        low = (local & 31).astype(F32)
        zero = jnp.zeros((128, 128), F32)
        chosen_high = jnp.where(ranked, jnp.broadcast_to(high, (128, 128)), zero).astype(BF16)
        chosen_low = jnp.where(ranked, jnp.broadcast_to(low, (128, 128)), zero).astype(BF16)
        onehot = onehot.astype(BF16)
        want_high = want_high + dot_nt(onehot, chosen_high)
        want_low = want_low + dot_nt(onehot, chosen_low)
    wv[...] = want_high * 32.0 + want_low

    def row_out(s, carry):
        for y in range(NY):
            wq[s, y] = wv[pl.ds(s * NY + y, 1), :]
        return carry

    lax.fori_loop(0, NX, row_out, 0)
    pl.semaphore_wait(barrier, NX + NY - 2 + len(CORNERS))

    def ask_x(k, carry):
        pltpu.make_async_remote_copy(
            wq.at[other_x(k)], mid.at[gx], wsend, wrecv,
            device_id=(other_x(k), gy), device_id_type=MESH,
        ).start()
        return carry

    lax.fori_loop(1, NX, ask_x, 0)
    own_x = pltpu.make_async_copy(wq.at[gx], mid.at[gx], loc_sem.at[0])
    own_x.start()

    others_x = mid.at[pl.ds(0, NX - 1)]
    others_y = req.at[:, pl.ds(0, NY - 1)]

    def ask_y(k, carry):
        pltpu.make_async_remote_copy(
            mid.at[:, other_y(k)], req.at[:, gy], vsend, vrecv,
            device_id=(gx, other_y(k)), device_id_type=MESH,
        ).start()
        return carry

    def copy_to(src, dst, send, recv, dgx, dgy):
        return pltpu.make_async_remote_copy(
            src, dst, send, recv,
            device_id=((gx + dgx + NX) % NX, (gy + dgy + NY) % NY),
            device_id_type=MESH,
        )

    def send_halo(h):
        for f in range(2):
            field = 2 * h + f

            for k in range(16):
                part = pl.ds(k * 4, 4)
                sx[h, 0, f, part, :] = st[field, pl.ds((15 * 16 + k) * 16 + 12, 4), :]
                sx[h, 1, f, part, :] = st[field, pl.ds(k * 16, 4), :]
                sy[h, 0, f, part, :] = st[field, pl.ds((k * 16 + 15) * 16 + 3, 4, stride=4), :]
                sy[h, 1, f, part, :] = st[field, pl.ds(k * 256, 4, stride=4), :]
            for at, (_, _, _, x, y, n) in enumerate(CORNERS):
                sc[h, at, f : f + 1, :] = st[field, pl.ds((x * 16 + y) * 16 + n, 1), :]
        copies = [
            copy_to(sx.at[h, 0], rx.at[h, 0], hsend.at[h, 0], hrecv.at[h, 0], 1, 0),
            copy_to(sx.at[h, 1], rx.at[h, 1], hsend.at[h, 1], hrecv.at[h, 1], -1, 0),
            copy_to(sy.at[h, 0], ry.at[h, 0], hsend.at[h, 2], hrecv.at[h, 2], 0, 1),
            copy_to(sy.at[h, 1], ry.at[h, 1], hsend.at[h, 3], hrecv.at[h, 3], 0, -1),
        ]
        for at, (dgx, dgy, to, _, _, _) in enumerate(CORNERS):
            copies.append(
                copy_to(sc.at[h, at], rc.at[h, at], hsend.at[h, to], hrecv.at[h, to], dgx, dgy)
            )
        for copy in copies:
            copy.start()
        return copies

    def take_halo(h, copies):
        for copy in copies:
            copy.wait_recv()
        for f in range(2):
            field = 2 * h + f
            for k in range(16):
                part = pl.ds(k * 4, 4)
                halo[field, pl.ds((WEST + 1 + k) * 16 + 12, 4), :] = rx[h, 0, f, part, :]
                halo[field, pl.ds((EAST + 1 + k) * 16, 4), :] = rx[h, 1, f, part, :]
                halo[field, pl.ds((SOUTH + k) * 16 + 3, 4, stride=4), :] = ry[h, 0, f, part, :]
                halo[field, pl.ds((NORTH + k) * 16, 4, stride=4), :] = ry[h, 1, f, part, :]
            halo[field, pl.ds(WEST * 16 + 15, 1), :] = rc[h, 0, f : f + 1, :]
            halo[field, pl.ds(EAST * 16 + 3, 1), :] = rc[h, 1, f : f + 1, :]
            halo[field, pl.ds((WEST + 17) * 16 + 12, 1), :] = rc[h, 2, f : f + 1, :]
            halo[field, pl.ds((EAST + 17) * 16, 1), :] = rc[h, 3, f : f + 1, :]

    s8 = iota((8, 128), 0)
    b_at = s8 & 3
    is_b0, is_b3, first_a = b_at == 0, b_at == 3, s8 < 4
    b_scale = jnp.where(is_b0 | is_b3, 0.5, 1.0)
    scale0 = b_scale * jnp.where(first_a, 0.5, 1.0)
    scale1 = b_scale * jnp.where(first_a, 1.0, 0.5)

    def dynamics(h):
        def column(x, carry):
            fixed = isinstance(x, int)

            def rows(x, y, v):
                inside = 0 <= y < TY
                if fixed and x == -1:
                    return halo, (WEST + y + 1) * 16 + v * 8
                if fixed and x == TX:
                    return halo, (EAST + y + 1) * 16 + v * 8
                if not inside:
                    return halo, ((SOUTH if y < 0 else NORTH) + x) * 16 + v * 8
                return st, x * 256 + y * 16 + v * 8

            def load(field, x, y, v):
                ref, at = rows(x, y, v)
                return ref[field, pl.ds(at if fixed else pl.multiple_of(at, 8), 8), :]

            def along_x(y):
                found = []
                for f in range(2):
                    field = 2 * h + f
                    own0, own1 = load(field, x, y, 0), load(field, x, y, 1)
                    before, after = load(field, x - 1, y, 1), load(field, x + 1, y, 0)
                    found.append(own0 + jnp.where(first_a, pltpu.roll(before, 4, 0), 0.0))
                    found.append(own1 + jnp.where(first_a, 0.0, pltpu.roll(after, 4, 0)))
                return found

            south, here = along_x(-1), along_x(0)
            for y in range(TY):
                north = along_x(y + 1)
                for f in range(2):
                    parts = []
                    for v, scale in ((2 * f, scale0), (2 * f + 1, scale1)):
                        edge = jnp.where(is_b0, pltpu.roll(south[v], 5, 0), 0.0)
                        edge = jnp.where(is_b3, pltpu.roll(north[v], 3, 0), edge)
                        parts.append((here[v] + edge) * scale)
                    total = jnp.concatenate(parts, axis=0)
                    at = x * 256 + y * 16
                    dyn[2 * h + f, pl.ds(at if fixed else pl.multiple_of(at, 16), 16), :] = total
                    high = total.astype(BF16)
                    dyn_high[y * 16 : y * 16 + 16, f * 128 : f * 128 + 128] = high
                    low = (total - high.astype(F32)).astype(BF16)
                    dyn_low[y * 16 : y * 16 + 16, f * 128 : f * 128 + 128] = low
                south, here = here, north
            main = dot(coltab_ref[...], dyn_high[...])
            rest = dot(coltab_ref[0:64, :], dyn_low[...])
            total = main[0:64] + main[64:128] + rest
            cols[pl.ds(x * 64 if fixed else pl.multiple_of(x * 64, 64), 64), :] = total.astype(BF16)
            return carry

        column(0, 0)
        lax.fori_loop(1, TX - 1, column, 0)
        column(TX - 1, 0)

    wide = iota((128, 1024), 1)

    def selections():
        k_mask = iota((128, 128), 1) == (iota((128, 128), 0) & 7)

        def build(b, carry):
            found = peers.block(b, with_self=True)
            for part in range(2):
                asked = [
                    jnp.broadcast_to(req[tgx, tgy], (8, 128))
                    for tgx, tgy, _, _ in found[part * 16 : part * 16 + 16]
                ]
                asked = jnp.where(k_mask, jnp.concatenate(asked, axis=0), 0.0)
                asked = jnp.sum(asked, axis=1, keepdims=True).astype(I32)
                slot_at, piece = asked >> 2, asked & 3
                tile = jnp.zeros((128, 128), F32)
                for u in range(2):
                    cell = cell_ref[u : u + 1, :]
                    names = (((cell >> 7) & 15) * 16 + (cell & 15)).astype(F32)
                    names = jnp.broadcast_to(names, (128, 128))
                    tile = tile + jnp.where(slot_at == lane + 128 * u, names, 0.0)
                tile = jnp.sum(tile, axis=1, keepdims=True).astype(I32)
                at = (tile >> 4) * 64 + (piece >> 1) * 32 + (tile & 15) * 2 + (piece & 1)
                block = b * 2 + part
                rows = pl.ds(pl.multiple_of(block * 128, 128), 128)
                sel[rows, :] = jnp.where(wide == at, 1.0, 0.0).astype(BF16)
                crow[pl.ds(block, 1), :] = to_row(at.astype(F32))
            return carry

        lax.fori_loop(0, 4, build, 0)

    def transposed(row_ref, out_ref):
        def build(block, carry):
            rows = pl.ds(pl.multiple_of(block * 128, 128), 128)
            want = (sub + block * 128).astype(F32)
            for u in range(8):
                names = jnp.broadcast_to(row_ref[u : u + 1, :], (128, 128))
                out_ref[rows, u * 128 : (u + 1) * 128] = jnp.where(names == want, 1.0, 0.0).astype(BF16)
            return carry

        lax.fori_loop(0, 8, build, 0)

    def placing():
        def build(block, carry):
            rows = pl.ds(pl.multiple_of(block * 128, 128), 128)
            at = to_col(qrow[pl.ds(block, 1), :]).astype(I32)
            place[rows, :] = jnp.where(wide == at, 1.0, 0.0).astype(BF16)
            return carry

        lax.fori_loop(0, 8, build, 0)

    def permute_and_send(matrix, source, src, dst, h, send, recv, loc):
        def step(b):
            rows = pl.ds(pl.multiple_of(b * 256, 256), 256)
            moved = dot(matrix[rows, :], source[...])
            src[h, pl.ds(b * 32, 32)] = moved.reshape(32, 8, 256).astype(BF16)
            for tgx, tgy, at, back in peers.block(b):
                pltpu.make_async_remote_copy(
                    src.at[h, at], dst.at[h, back], send.at[h], recv.at[h],
                    device_id=(tgx, tgy), device_id_type=MESH,
                ).start()

        def loop_step(b, carry):
            step(b)
            return carry

        step(0)
        own = pltpu.make_async_copy(src.at[h, 0], dst.at[h, 0], loc_sem.at[loc])
        own.start()
        lax.fori_loop(1, 4, loop_step, 0)
        return own

    def wait_all(ref, h, sem):
        block = ref.at[h, pl.ds(0, ND - 1)]
        pltpu.make_async_copy(block, block, sem.at[h]).wait()

    def flatten(src, h):
        def step(block, carry):
            part = src[h, pl.ds(block * 16, 16)].astype(F32).reshape(128, 256)
            flat[pl.ds(pl.multiple_of(block * 128, 128), 128), :] = part.astype(BF16)
            return carry

        lax.fori_loop(0, 8, step, 0)

    halo_copies, forward, back_copies = [None] * NH, [None] * NH, [None] * NH
    halo_copies[0] = send_halo(0)
    own_x.wait()
    pltpu.make_async_copy(others_x, others_x, wrecv).wait()
    lax.fori_loop(1, NY, ask_y, 0)
    own_y = pltpu.make_async_copy(mid.at[:, gy], req.at[:, gy], loc_sem.at[0])
    own_y.start()
    halo_copies[1] = send_halo(1)
    for h in range(NH):
        take_halo(h, halo_copies[h])
        dynamics(h)
        if h == 0:
            own_y.wait()
            pltpu.make_async_copy(others_y, others_y, vrecv).wait()
            selections()
        forward[h] = permute_and_send(sel, cols, outb, incb, h, fsend, frecv, 1 + h)
        if h == 0:
            transposed(qrow, place_t)
            placing()

    transposed(crow, sel_t)

    def physics(h):
        def step(block, carry):
            rows = pl.ds(pl.multiple_of(block * 256, 256), 256)
            moved = dot(place[rows, :], flat[...])
            for g in range(16):
                part = moved[g * 16 : (g + 1) * 16, :]
                stacked = jnp.concatenate([part[:, :128], part[:, 128:]], axis=0)
                smooth = dot_nt(stacked.astype(BF16), inv[block * 16 + g])
                change = smooth - stacked
                change = jnp.concatenate([change[:16], change[16:]], axis=1)
                tend[pl.ds(pl.multiple_of(block * 256 + g * 16, 16), 16), :] = change.astype(BF16)
            return carry

        lax.fori_loop(0, 4, step, 0)

    for h in range(NH):
        forward[h].wait()
        wait_all(incb, h, frecv)
        flatten(incb, h)
        physics(h)
        back_copies[h] = permute_and_send(place_t, tend, backb, rcvb, h, bsend, brecv, 3 + h)

    grid[...] = jnp.zeros_like(grid)
    ring_copies = []
    for h in range(NH):
        back_copies[h].wait()
        wait_all(rcvb, h, brecv)
        flatten(rcvb, h)

        def ungroup(block, carry):
            rows = pl.ds(pl.multiple_of(block * 256, 256), 256)
            moved = dot(sel_t[rows, :], flat[...])
            for x in range(4):
                for i in range(2):
                    base = pl.multiple_of((block * 4 + x + 1) * RX + i * 40, 8)
                    piece = moved[x * 64 + i * 32 : x * 64 + i * 32 + 32, :]
                    for u in range(2):
                        grid[h, u, pl.ds(base, 32), :] = piece[:, u * 128 : (u + 1) * 128]
            return carry

        lax.fori_loop(0, 4, ungroup, 0)
        for u in range(2):
            for i in range(2):
                tx[h, 0, u, i * 32 : i * 32 + 32, :] = grid[h, u, 16 * RX + i * 40 : 16 * RX + i * 40 + 32, :]
                tx[h, 1, u, i * 32 : i * 32 + 32, :] = grid[h, u, RX + i * 40 : RX + i * 40 + 32, :]
            for j in range(2):
                ty[h, 0, u, j * 32 : j * 32 + 32, :] = grid[h, u, pl.ds(RX + 30 + j, 32, stride=40), :]
                ty[h, 1, u, j * 32 : j * 32 + 32, :] = grid[h, u, pl.ds(RX + j, 32, stride=40), :]
            for at, (_, _, _, x, y, _) in enumerate(CORNERS):
                for i in range(2):
                    base = (x + 1) * RX + i * 40 + 2 * y
                    tc[h, at, u * 4 + i * 2 : u * 4 + i * 2 + 2, :] = grid[h, u, base : base + 2, :]
        copies = [
            copy_to(tx.at[h, 0], ux.at[h, 0], gsend.at[h, 0], grecv.at[h, 0], 1, 0),
            copy_to(tx.at[h, 1], ux.at[h, 1], gsend.at[h, 1], grecv.at[h, 1], -1, 0),
            copy_to(ty.at[h, 0], uy.at[h, 0], gsend.at[h, 2], grecv.at[h, 2], 0, 1),
            copy_to(ty.at[h, 1], uy.at[h, 1], gsend.at[h, 3], grecv.at[h, 3], 0, -1),
        ]
        for at, (dgx, dgy, to, _, _, _) in enumerate(CORNERS):
            copies.append(
                copy_to(tc.at[h, at], uc.at[h, at], gsend.at[h, to], grecv.at[h, to], dgx, dgy)
            )
        for copy in copies:
            copy.start()
        ring_copies.append(copies)

    for h in range(NH):
        for copy in ring_copies[h]:
            copy.wait_recv()
        for u in range(2):
            for i in range(2):
                part = slice(i * 32, i * 32 + 32)
                grid[h, u, i * 40 : i * 40 + 32, :] = ux[h, 0, u, part, :]
                grid[h, u, 17 * RX + i * 40 : 17 * RX + i * 40 + 32, :] = ux[h, 1, u, part, :]
            for j in range(2):
                part = slice(j * 32, j * 32 + 32)
                grid[h, u, pl.ds(RX + 32 + j, 32, stride=40), :] = uy[h, 0, u, part, :]
                grid[h, u, pl.ds(RX + 34 + j, 32, stride=40), :] = uy[h, 1, u, part, :]
            for at, (big_x, base) in enumerate(((0, 32), (17, 32), (0, 34), (17, 34))):
                for i in range(2):
                    to = big_x * RX + i * 40 + base
                    grid[h, u, to : to + 2, :] = uc[h, at, u * 4 + i * 2 : u * 4 + i * 2 + 2, :]
            gridb[h, :, u * 128 : (u + 1) * 128] = grid[h, u].astype(BF16)

    pltpu.make_async_copy(others_x, others_x, wsend).wait()
    pltpu.make_async_copy(others_y, others_y, vsend).wait()
    for h in range(NH):
        wait_all(outb, h, fsend)
        wait_all(backb, h, bsend)
        for copy in halo_copies[h] + ring_copies[h]:
            copy.wait_send()


def finish_kernel(cell_ref, ret, table_ref, dyn, out_hbm, total, outv, out_sem):
    def add(x, carry):
        rows = pl.ds(pl.multiple_of(x * 256, 256), 256)
        for h in range(NH):
            near = ret[h, pl.ds(pl.multiple_of(x * RX, 16), 256), :]
            update = dot(table_ref[...], near)
            update = update[:256] + update[256:]
            for f in range(2):
                field = 2 * h + f
                total[field, rows, :] = dyn[field, rows, :] + update[:, f * 128 : (f + 1) * 128]
        return carry

    lax.fori_loop(0, TX, add, 0)

    def gather(s, carry):
        cell = cell_ref[s]
        tile = ((cell >> 7) & 15) * 16 + (cell & 15)
        source = pl.ds(pl.multiple_of(tile * 16, 16), 16)
        target = pl.ds(pl.multiple_of(s * 16, 16), 16)
        for field in range(4):
            outv[field, target, :] = total[field, source, :]
        return carry

    stores = []
    for part in range(8):
        lax.fori_loop(part * 32, part * 32 + 32, gather, 0, unroll=4)
        rows = pl.ds(part * 512, 512)
        copy = pltpu.make_async_copy(outv.at[:, rows], out_hbm.at[:, rows], out_sem.at[part])
        copy.start()
        stores.append(copy)
    for copy in stores:
        copy.wait()


def any_spec():
    return pl.BlockSpec(memory_space=pl.ANY)


def hbm_spec():
    return pl.BlockSpec(memory_space=pltpu.HBM)


def vmem_spec():
    return pl.BlockSpec(memory_space=pltpu.VMEM)


def smem_spec():
    return pl.BlockSpec(memory_space=pltpu.SMEM)


def per_device(coltab, uptab, state_in, stiffness, elem_cell, group_column, group_inverse):
    state = state_in.reshape(4, NE * 16, LEV)
    dma = pltpu.SemaphoreType.DMA
    vmem = pltpu.VMEM
    whole = jax.ShapeDtypeStruct((4, NE * 16, LEV), F32)
    combined = pl.pallas_call(
        combine_kernel,
        out_shape=whole,
        in_specs=[smem_spec(), hbm_spec(), hbm_spec()],
        out_specs=vmem_spec(),
        scratch_shapes=[
            vmem((4, NE * 16, LEV), F32),
            vmem((256, 256), F32),
            vmem((2, NE * 16, LEV), F32),
            dma,
            dma((8,)),
        ],
        compiler_params=pltpu.CompilerParams(vmem_limit_bytes=42 << 20),
        name="combine",
    )(elem_cell, state, stiffness.reshape(256, NE))
    scratch = [
        vmem((4, NHALO * 16, LEV), F32),
        vmem((128, 128), F32),
        vmem((NX, NY, 1, 128), F32),
        vmem((NX, NY, 1, 128), F32),
        vmem((NX, NY, 1, 128), F32),
        vmem((8, 128), F32),
        vmem((8, 128), F32),
        vmem((NC, NC), BF16),
        vmem((NC, NC), BF16),
        vmem((NC, NC), BF16),
        vmem((NC, NC), BF16),
        vmem((256, 256), BF16),
        vmem((256, 256), BF16),
        vmem((NC, 256), BF16),
        vmem((NH, ND, 8, 256), BF16),
        vmem((NH, ND, 8, 256), BF16),
        vmem((NH, ND, 8, 256), BF16),
        vmem((NH, ND, 8, 256), BF16),
        vmem((NC, 256), BF16),
        vmem((NC, 256), BF16),
        vmem((NH, 2, RROWS, LEV), F32),
        vmem((NH, 2, 2, 64, LEV), F32),
        vmem((NH, 2, 2, 64, LEV), F32),
        vmem((NH, 4, 8, LEV), F32),
        vmem((NH, 2, 2, 64, LEV), F32),
        vmem((NH, 2, 2, 64, LEV), F32),
        vmem((NH, 4, 8, LEV), F32),
        vmem((NH, 2, 2, 64, LEV), F32),
        vmem((NH, 2, 2, 64, LEV), F32),
        vmem((NH, 4, 8, LEV), F32),
        vmem((NH, 2, 2, 64, LEV), F32),
        vmem((NH, 2, 2, 64, LEV), F32),
        vmem((NH, 4, 8, LEV), F32),
        dma, dma, dma, dma, dma((5,)),
        dma((NH,)), dma((NH,)), dma((NH,)), dma((NH,)),
        dma((NH, 8)), dma((NH, 8)), dma((NH, 8)), dma((NH, 8)),
    ]
    dyn, ret = pl.pallas_call(
        exchange_kernel,
        out_shape=(whole, jax.ShapeDtypeStruct((NH, RROWS, 256), BF16)),
        in_specs=[vmem_spec()] * 5,
        out_specs=(vmem_spec(), vmem_spec()),
        scratch_shapes=scratch,
        compiler_params=pltpu.CompilerParams(
            collective_id=0, has_side_effects=True, vmem_limit_bytes=28 << 20
        ),
        name="exchange",
    )(combined, elem_cell.reshape(2, 128), group_column.reshape(8, 128), group_inverse, coltab)
    out = pl.pallas_call(
        finish_kernel,
        out_shape=whole,
        in_specs=[smem_spec(), vmem_spec(), vmem_spec(), vmem_spec()],
        out_specs=any_spec(),
        scratch_shapes=[vmem((4, NE * 16, LEV), F32), vmem((4, NE * 16, LEV), F32), dma((8,))],
        compiler_params=pltpu.CompilerParams(vmem_limit_bytes=32 << 20),
        name="finish",
    )(elem_cell, ret, uptab, dyn)
    return out.reshape(4, NE, 16, LEV)


def solution(mesh):
    coltab, uptab = constant_tables()
    placed = (
        P(None, ("gx", "gy"), None, None),
        P(None, None, ("gx", "gy")),
        P(("gx", "gy")),
        P(("gx", "gy")),
        P(("gx", "gy"), None, None),
    )

    def run(*args):
        body = functools.partial(per_device, jnp.asarray(coltab), jnp.asarray(uptab))
        return jax.shard_map(
            body,
            mesh=mesh,
            in_specs=placed,
            out_specs=P(None, ("gx", "gy"), None, None),
            check_vma=False,
        )(*args)

    return run
```

```python
import functools
import math

import jax
import jax.numpy as jnp
import ml_dtypes
import numpy as np
from jax import lax
from jax.experimental import pallas as pl
from jax.experimental.pallas import tpu as pltpu
from jax.sharding import PartitionSpec as P

F32, BF16, I32 = jnp.float32, jnp.bfloat16, jnp.int32
MESH = pl.DeviceIdType.MESH
NX, NY = 16, 8
ND = NX * NY
TX = TY = 16
NE = TX * TY
NC = 4 * NE
LEV = 128
NH = 2
WEST, EAST, SOUTH, NORTH = 0, 18, 36, 52
NHALO = 68
RX = 80
RROWS = 18 * RX + 16
CORNERS = (
    (1, 1, 4, 15, 15, 15),
    (-1, 1, 5, 0, 15, 3),
    (1, -1, 6, 15, 0, 12),
    (-1, -1, 7, 0, 0, 0),
)


def lagrange_value(node, position, nodes):
    value = 1.0
    for other in range(4):
        if other != node:
            value *= (position - nodes[other]) / (nodes[node] - nodes[other])
    return value


def tables():
    nodes = [-1.0, -1.0 / math.sqrt(5.0), 1.0 / math.sqrt(5.0), 1.0]
    halves = np.zeros((2, 4))
    for i, (low, high) in enumerate(((-1.0, 0.0), (0.0, 1.0))):
        centre, offset = 0.5 * (low + high), 0.5 * (high - low) / math.sqrt(3.0)
        for a in range(4):
            halves[i, a] = (
                0.5
                * (high - low)
                * (
                    lagrange_value(a, centre - offset, nodes)
                    + lagrange_value(a, centre + offset, nodes)
                )
            )
    spread = halves.T @ np.linalg.inv(halves @ halves.T)
    return halves.astype(np.float32).astype(np.float64), spread.astype(np.float32).astype(np.float64)


def split_bf16(table):
    high = table.astype(ml_dtypes.bfloat16)
    low = (table - high.astype(np.float64)).astype(ml_dtypes.bfloat16)
    return high, low


def constant_tables():
    halves, spread = tables()
    cols = np.einsum("ia,jb,yz->iyjzab", halves, halves, np.eye(TY)).reshape(64, 256)
    col_high, col_low = split_bf16(cols)
    along = np.zeros((4, 3, 2))
    along[:, 1, :] = spread
    along[0, 0, :] += spread[3]
    along[3, 2, :] += spread[0]
    along[0] *= 0.5
    along[3] *= 0.5
    along_y = np.zeros((TY, 4, 40))
    for y in range(TY):
        for step in range(3):
            other = y + step - 1
            base = 32 if other < 0 else 34 if other >= TY else 2 * other
            along_y[y, :, base : base + 2] += along[:, step, :]
    update = np.zeros((256, 256))
    update[:, :240] = np.einsum("asi,ybr->yabsir", along, along_y).reshape(256, 240)
    up_high, up_low = split_bf16(update)
    return np.concatenate([col_high, col_low], 0), np.concatenate([up_high, up_low], 0)


def iota(shape, dim):
    return lax.broadcasted_iota(I32, shape, dim)


def dot(left, right):
    return jnp.dot(left, right, preferred_element_type=F32)


def dot_nt(left, right):
    return lax.dot_general(left, right, (((1,), (1,)), ((), ())), preferred_element_type=F32)


class Peers:
    def __init__(self, gx, gy):
        self.x, self.y = lax.div(gx, 4), lax.rem(gx, 4)
        self.z, self.core = lax.div(gy, 2), lax.rem(gy, 2)
        self.xs = [lax.rem(self.x + a, 4) * 4 for a in range(4)]
        self.zs = [lax.rem(self.z + d, 4) * 2 for d in range(4)]
        self.cores = [self.core, 1 - self.core]

    def block(self, b, with_self=False):
        ys = [lax.rem(self.y + b + a, 4) for a in range(4)]
        back_b = lax.rem(4 - b, 4) if not isinstance(b, int) else -b % 4
        found = []
        for d in range(4):
            for a in range(4):
                for c in range(2):
                    if isinstance(b, int) and b == d == a == c == 0 and not with_self:
                        continue
                    tgx = self.xs[a] + ys[a]
                    tgy = self.zs[(d + a) % 4] + self.cores[c]
                    inner = d * 8 + a * 2 + c
                    back = -d % 4 * 8 + -a % 4 * 2 + c
                    found.append((tgx, tgy, b * 32 + inner, back_b * 32 + back))
        return found

    def position(self, source):
        a = ((source >> 5) - self.x) & 3
        b = (((source >> 3) & 3) - self.y - a) & 3
        d = (((source >> 1) & 3) - self.z - a) & 3
        c = ((source & 1) - self.core) & 1
        return b * 32 + d * 8 + a * 2 + c


def exchange_kernel(
    state_hbm, stiff_hbm, inv_hbm, cell_ref, gcol_ref, coltab_ref, uptab_ref,
    dyn,
    inv, st0, st1, xs, w16, slot_vmem, slots,
    halo, wv, wq, mid, req, qrow, crow,
    sel, sel_t, place, place_t,
    dyn_high, dyn_low, cols, outb, incb, backb, rcvb, flat, tend, grid, gridb,
    sx, sy, sc, rx, ry, rc,
    tx, ty, tc, ux, uy, uc,
    state_sem, in_sem, wsend, wrecv, vsend, vrecv, loc_sem,
    fsend, frecv, bsend, brecv, hsend, hrecv, gsend, grecv,
):
    st = (st0, st1)
    gx, gy = lax.axis_index("gx"), lax.axis_index("gy")
    peers = Peers(gx, gy)
    barrier = pltpu.get_barrier_semaphore()

    def other_x(k):
        return lax.rem(gx + k, NX)

    def other_y(k):
        return lax.rem(gy + k, NY)

    for dgx, dgy, _, _, _, _ in CORNERS:
        pl.semaphore_signal(
            barrier, inc=1, device_id=(other_x(NX + dgx), other_y(NY + dgy)), device_id_type=MESH
        )

    def greet_x(k, carry):
        pl.semaphore_signal(barrier, inc=1, device_id=(other_x(k), gy), device_id_type=MESH)
        return carry

    def greet_y(k, carry):
        pl.semaphore_signal(barrier, inc=1, device_id=(gx, other_y(k)), device_id_type=MESH)
        return carry

    lax.fori_loop(1, NX, greet_x, 0)
    lax.fori_loop(1, NY, greet_y, 0)


    stiff_copy = pltpu.make_async_copy(stiff_hbm, xs, in_sem.at[0])
    stiff_copy.start()
    state_copies = []
    for h in range(NH):
        row = []
        for part in range(4):
            elems = pl.ds(part * 64, 64)
            copy = pltpu.make_async_copy(
                state_hbm.at[pl.ds(2 * h, 2), elems], st[h].at[:, elems], state_sem.at[h, part]
            )
            copy.start()
            row.append(copy)
        state_copies.append(row)

    inv_copy = pltpu.make_async_copy(inv_hbm, inv, in_sem.at[2])
    inv_copy.start()

    lane = iota((128, 128), 1)
    sub = iota((128, 128), 0)
    eye = lane == sub

    def to_col(row):
        return jnp.sum(jnp.where(eye, jnp.broadcast_to(row, (128, 128)), 0.0), axis=1, keepdims=True)

    def to_row(col):
        return jnp.sum(jnp.where(eye, jnp.broadcast_to(col, (128, 128)), 0.0), axis=0, keepdims=True)

    def tiles(u):
        cell = cell_ref[u : u + 1, :]
        return (((cell >> 7) & 15) * 16 + (cell & 15)).astype(F32)

    for v in range(2):
        found = jnp.zeros((128, 128), F32)
        for u in range(2):
            at = to_col(tiles(u))
            number = (sub + 128 * u).astype(F32)
            found = jnp.maximum(found, jnp.where(at == (lane + 128 * v).astype(F32), number, 0.0))
        slot_vmem[v : v + 1, :] = jnp.max(found, axis=0, keepdims=True).astype(I32)
    slot_copy = pltpu.make_async_copy(slot_vmem, slots, in_sem.at[1])
    slot_copy.start()

    upper = jnp.where(sub < lane, 1.0, 0.0).astype(BF16)
    seen = jnp.zeros((128, 1), F32)
    want_high = jnp.zeros((128, 128), F32)
    want_low = jnp.zeros((128, 128), F32)
    for block in range(8):
        named = gcol_ref[block : block + 1, :]
        source, local = named >> 10, named & 1023
        hit = jnp.broadcast_to(source, (128, 128)) == sub
        onehot = jnp.where(hit, 1.0, 0.0)
        before = dot(onehot.astype(BF16), upper) + seen
        seen = seen + jnp.sum(onehot, axis=1, keepdims=True)
        rank = jnp.sum(jnp.where(hit, before, 0.0), axis=0, keepdims=True)
        qrow[block : block + 1, :] = peers.position(source).astype(F32) * 8.0 + rank
        ranked = jnp.broadcast_to(rank, (128, 128)) == sub.astype(F32)
        high = (local >> 5).astype(F32)
        low = (local & 31).astype(F32)
        zero = jnp.zeros((128, 128), F32)
        chosen_high = jnp.where(ranked, jnp.broadcast_to(high, (128, 128)), zero).astype(BF16)
        chosen_low = jnp.where(ranked, jnp.broadcast_to(low, (128, 128)), zero).astype(BF16)
        onehot = onehot.astype(BF16)
        want_high = want_high + dot_nt(onehot, chosen_high)
        want_low = want_low + dot_nt(onehot, chosen_low)
    wv[...] = want_high * 32.0 + want_low

    def row_out(s, carry):
        for y in range(NY):
            wq[s, y] = wv[pl.ds(s * NY + y, 1), :]
        return carry

    lax.fori_loop(0, NX, row_out, 0)
    stiff_copy.wait()
    flipped = xs[...].T.astype(BF16)
    row_i, col_i = iota((256, 256), 0), iota((256, 256), 1)
    same_m = (row_i & 15) == (col_i & 15)
    diagonal = (row_i & 15) == (col_i >> 4)
    for n in range(16):
        pick = jnp.where(same_m & ((row_i >> 4) == n), 1.0, 0.0).astype(BF16)
        block = jnp.where(diagonal, dot(flipped, pick), 0.0)
        for u in range(2):
            dyn[u, pl.ds(n, 256, stride=16), :] = block[:, u * 128 : (u + 1) * 128]

    pl.semaphore_wait(barrier, NX + NY - 2 + len(CORNERS))

    def ask_x(k, carry):
        pltpu.make_async_remote_copy(
            wq.at[other_x(k)], mid.at[gx], wsend, wrecv,
            device_id=(other_x(k), gy), device_id_type=MESH,
        ).start()
        return carry

    lax.fori_loop(1, NX, ask_x, 0)
    own_x = pltpu.make_async_copy(wq.at[gx], mid.at[gx], loc_sem.at[0])
    own_x.start()

    others_x = mid.at[pl.ds(0, NX - 1)]
    others_y = req.at[:, pl.ds(0, NY - 1)]

    def ask_y(k, carry):
        pltpu.make_async_remote_copy(
            mid.at[:, other_y(k)], req.at[:, gy], vsend, vrecv,
            device_id=(gx, other_y(k)), device_id_type=MESH,
        ).start()
        return carry

    def combine(h):
        def step(g, carry):
            rows = pl.ds(pl.multiple_of(g * 256, 256), 256)
            elems = pl.ds(g * 16, 16)
            both = jnp.concatenate([st[h][f, elems].reshape(256, LEV) for f in range(2)], axis=1)
            if h == 0:
                oper = jnp.concatenate([dyn[0, rows, :], dyn[1, rows, :]], axis=1).astype(BF16)
                w16[rows, :] = oper
            else:
                oper = w16[rows, :]
            both = both + dot(oper, both.astype(BF16))
            for f in range(2):
                st[h][f, elems] = both[:, f * LEV : (f + 1) * LEV].reshape(16, 16, LEV)
            return carry

        for part in range(4):
            state_copies[h][part].wait()
            lax.fori_loop(part * 4, part * 4 + 4, step, 0)

    def slot(x, y):
        if isinstance(x, int):
            return slots[x // 8, x % 8 * 16 + y] & (NE - 1)
        return slots[lax.div(x, 8), lax.rem(x, 8) * 16 + y] & (NE - 1)

    def copy_to(src, dst, send, recv, dgx, dgy):
        return pltpu.make_async_remote_copy(
            src, dst, send, recv,
            device_id=((gx + dgx + NX) % NX, (gy + dgy + NY) % NY),
            device_id_type=MESH,
        )

    def send_halo(h):
        for f in range(2):
            field = 2 * h + f

            for k in range(16):
                part = pl.ds(k * 4, 4)
                sx[h, 0, f, part, :] = st[h][f, slot(15, k), 8:16, :][4:8]
                sx[h, 1, f, part, :] = st[h][f, slot(0, k), 0:8, :][0:4]
                for side, y, b in ((0, 15, 3), (1, 0, 0)):
                    at = slot(k, y)
                    for v in range(2):
                        half = st[h][f, at, v * 8 : v * 8 + 8, :]
                        for a in range(2):
                            to = k * 4 + v * 2 + a
                            sy[h, side, f, to : to + 1, :] = half[a * 4 + b : a * 4 + b + 1]
            for at, (_, _, _, x, y, n) in enumerate(CORNERS):
                half = st[h][f, slot(x, y), n // 8 * 8 : n // 8 * 8 + 8, :]
                sc[h, at, f : f + 1, :] = half[n % 8 : n % 8 + 1]
        copies = [
            copy_to(sx.at[h, 0], rx.at[h, 0], hsend.at[h, 0], hrecv.at[h, 0], 1, 0),
            copy_to(sx.at[h, 1], rx.at[h, 1], hsend.at[h, 1], hrecv.at[h, 1], -1, 0),
            copy_to(sy.at[h, 0], ry.at[h, 0], hsend.at[h, 2], hrecv.at[h, 2], 0, 1),
            copy_to(sy.at[h, 1], ry.at[h, 1], hsend.at[h, 3], hrecv.at[h, 3], 0, -1),
        ]
        for at, (dgx, dgy, to, _, _, _) in enumerate(CORNERS):
            copies.append(
                copy_to(sc.at[h, at], rc.at[h, at], hsend.at[h, to], hrecv.at[h, to], dgx, dgy)
            )
        for copy in copies:
            copy.start()
        return copies

    def take_halo(h, copies):
        for copy in copies:
            copy.wait_recv()
        for f in range(2):
            field = 2 * h + f
            for k in range(16):
                part = pl.ds(k * 4, 4)
                halo[field, WEST + 1 + k, 12:16, :] = rx[h, 0, f, part, :]
                halo[field, EAST + 1 + k, 0:4, :] = rx[h, 1, f, part, :]
                halo[field, SOUTH + k, pl.ds(3, 4, stride=4), :] = ry[h, 0, f, part, :]
                halo[field, NORTH + k, pl.ds(0, 4, stride=4), :] = ry[h, 1, f, part, :]
            halo[field, WEST, 15:16, :] = rc[h, 0, f : f + 1, :]
            halo[field, EAST, 3:4, :] = rc[h, 1, f : f + 1, :]
            halo[field, WEST + 17, 12:13, :] = rc[h, 2, f : f + 1, :]
            halo[field, EAST + 17, 0:1, :] = rc[h, 3, f : f + 1, :]

    s8 = iota((8, 128), 0)
    b_at = s8 & 3
    is_b0, is_b3, first_a = b_at == 0, b_at == 3, s8 < 4
    b_scale = jnp.where(is_b0 | is_b3, 0.5, 1.0)
    scale0 = b_scale * jnp.where(first_a, 0.5, 1.0)
    scale1 = b_scale * jnp.where(first_a, 1.0, 0.5)

    def dynamics(h):
        def column(x, carry):
            fixed = isinstance(x, int)

            def inside(x, y):
                return 0 <= y < TY and not (fixed and not 0 <= x < TX)

            def locate(x, y):
                if inside(x, y):
                    return slot(x, y)
                if fixed and x == -1:
                    return WEST + y + 1
                if fixed and x == TX:
                    return EAST + y + 1
                return (SOUTH if y < 0 else NORTH) + x

            def load(f, x, y, at, v):
                if inside(x, y):
                    return st[h][f, at, v * 8 : v * 8 + 8, :]
                return halo[2 * h + f, at, v * 8 : v * 8 + 8, :]

            def along_x(y):
                found = []
                mine, west, east = locate(x, y), locate(x - 1, y), locate(x + 1, y)
                for f in range(2):
                    own0, own1 = load(f, x, y, mine, 0), load(f, x, y, mine, 1)
                    before, after = load(f, x - 1, y, west, 1), load(f, x + 1, y, east, 0)
                    found.append(own0 + jnp.where(first_a, pltpu.roll(before, 4, 0), 0.0))
                    found.append(own1 + jnp.where(first_a, 0.0, pltpu.roll(after, 4, 0)))
                return found

            south, here = along_x(-1), along_x(0)
            for y in range(TY):
                north = along_x(y + 1)
                for f in range(2):
                    parts = []
                    for v, scale in ((2 * f, scale0), (2 * f + 1, scale1)):
                        edge = jnp.where(is_b0, pltpu.roll(south[v], 5, 0), 0.0)
                        edge = jnp.where(is_b3, pltpu.roll(north[v], 3, 0), edge)
                        parts.append((here[v] + edge) * scale)
                    total = jnp.concatenate(parts, axis=0)
                    at = x * 256 + y * 16
                    dyn[2 * h + f, pl.ds(at if fixed else pl.multiple_of(at, 16), 16), :] = total
                    high = total.astype(BF16)
                    dyn_high[y * 16 : y * 16 + 16, f * 128 : f * 128 + 128] = high
                    low = (total - high.astype(F32)).astype(BF16)
                    dyn_low[y * 16 : y * 16 + 16, f * 128 : f * 128 + 128] = low
                south, here = here, north
            main = dot(coltab_ref[...], dyn_high[...])
            rest = dot(coltab_ref[0:64, :], dyn_low[...])
            total = main[0:64] + main[64:128] + rest
            cols[pl.ds(x * 64 if fixed else pl.multiple_of(x * 64, 64), 64), :] = total.astype(BF16)
            return carry

        column(0, 0)
        lax.fori_loop(1, TX - 1, column, 0)
        column(TX - 1, 0)

    wide = iota((128, 1024), 1)

    def selections():
        k_mask = iota((128, 128), 1) == (iota((128, 128), 0) & 7)

        def build(b, carry):
            found = peers.block(b, with_self=True)
            for part in range(2):
                asked = [
                    jnp.broadcast_to(req[tgx, tgy], (8, 128))
                    for tgx, tgy, _, _ in found[part * 16 : part * 16 + 16]
                ]
                asked = jnp.where(k_mask, jnp.concatenate(asked, axis=0), 0.0)
                asked = jnp.sum(asked, axis=1, keepdims=True).astype(I32)
                slot_at, piece = asked >> 2, asked & 3
                tile = jnp.zeros((128, 128), F32)
                for u in range(2):
                    names = jnp.broadcast_to(tiles(u), (128, 128))
                    tile = tile + jnp.where(slot_at == lane + 128 * u, names, 0.0)
                tile = jnp.sum(tile, axis=1, keepdims=True).astype(I32)
                at = (tile >> 4) * 64 + (piece >> 1) * 32 + (tile & 15) * 2 + (piece & 1)
                block = b * 2 + part
                rows = pl.ds(pl.multiple_of(block * 128, 128), 128)
                sel[rows, :] = jnp.where(wide == at, 1.0, 0.0).astype(BF16)
                crow[pl.ds(block, 1), :] = to_row(at.astype(F32))
            return carry

        lax.fori_loop(0, 4, build, 0)

    def transposed(row_ref, out_ref):
        def build(block, carry):
            rows = pl.ds(pl.multiple_of(block * 128, 128), 128)
            want = (sub + block * 128).astype(F32)
            for u in range(8):
                names = jnp.broadcast_to(row_ref[u : u + 1, :], (128, 128))
                out_ref[rows, u * 128 : (u + 1) * 128] = jnp.where(names == want, 1.0, 0.0).astype(BF16)
            return carry

        lax.fori_loop(0, 8, build, 0)

    def placing():
        def build(block, carry):
            rows = pl.ds(pl.multiple_of(block * 128, 128), 128)
            at = to_col(qrow[pl.ds(block, 1), :]).astype(I32)
            place[rows, :] = jnp.where(wide == at, 1.0, 0.0).astype(BF16)
            return carry

        lax.fori_loop(0, 8, build, 0)

    def permute_and_send(matrix, source, src, dst, h, send, recv, loc):
        def step(b):
            rows = pl.ds(pl.multiple_of(b * 256, 256), 256)
            moved = dot(matrix[rows, :], source[...])
            src[h, pl.ds(b * 32, 32)] = moved.reshape(32, 8, 256).astype(BF16)
            for tgx, tgy, at, back in peers.block(b):
                pltpu.make_async_remote_copy(
                    src.at[h, at], dst.at[h, back], send.at[h], recv.at[h],
                    device_id=(tgx, tgy), device_id_type=MESH,
                ).start()

        def loop_step(b, carry):
            step(b)
            return carry

        step(0)
        own = pltpu.make_async_copy(src.at[h, 0], dst.at[h, 0], loc_sem.at[loc])
        own.start()
        lax.fori_loop(1, 4, loop_step, 0)
        return own

    def wait_all(ref, h, sem):
        block = ref.at[h, pl.ds(0, ND - 1)]
        pltpu.make_async_copy(block, block, sem.at[h]).wait()

    def flatten(src, h):
        def step(block, carry):
            part = src[h, pl.ds(block * 16, 16)].astype(F32).reshape(128, 256)
            flat[pl.ds(pl.multiple_of(block * 128, 128), 128), :] = part.astype(BF16)
            return carry

        lax.fori_loop(0, 8, step, 0)

    halo_copies, forward, back_copies = [None] * NH, [None] * NH, [None] * NH
    combine(0)
    own_x.wait()
    pltpu.make_async_copy(others_x, others_x, wrecv).wait()
    lax.fori_loop(1, NY, ask_y, 0)
    own_y = pltpu.make_async_copy(mid.at[:, gy], req.at[:, gy], loc_sem.at[0])
    own_y.start()
    slot_copy.wait()
    halo_copies[0] = send_halo(0)
    combine(1)
    halo_copies[1] = send_halo(1)
    transposed(qrow, place_t)
    placing()
    grid[...] = jnp.zeros_like(grid)
    for h in range(NH):
        take_halo(h, halo_copies[h])
        dynamics(h)
        if h == 0:
            own_y.wait()
            pltpu.make_async_copy(others_y, others_y, vrecv).wait()
            selections()
        forward[h] = permute_and_send(sel, cols, outb, incb, h, fsend, frecv, 1 + h)

    transposed(crow, sel_t)
    inv_copy.wait()

    def physics(h):
        def step(block, carry):
            rows = pl.ds(pl.multiple_of(block * 256, 256), 256)
            moved = dot(place[rows, :], flat[...])
            for g in range(16):
                part = moved[g * 16 : (g + 1) * 16, :]
                stacked = jnp.concatenate([part[:, :128], part[:, 128:]], axis=0)
                smooth = dot_nt(stacked.astype(BF16), inv[block * 16 + g])
                change = smooth - stacked
                change = jnp.concatenate([change[:16], change[16:]], axis=1)
                tend[pl.ds(pl.multiple_of(block * 256 + g * 16, 16), 16), :] = change.astype(BF16)
            return carry

        lax.fori_loop(0, 4, step, 0)

    for h in range(NH):
        forward[h].wait()
        wait_all(incb, h, frecv)
        flatten(incb, h)
        physics(h)
        back_copies[h] = permute_and_send(place_t, tend, backb, rcvb, h, bsend, brecv, 3 + h)

    ring_copies = []

    def finish(h):
        def add(x, carry):
            rows = pl.ds(pl.multiple_of(x * 256, 256), 256)
            near = gridb[pl.ds(pl.multiple_of(x * RX, 16), 256), :]
            update = dot(uptab_ref[...], near)
            update = update[:256] + update[256:]
            for f in range(2):
                field = 2 * h + f
                dyn[field, rows, :] = dyn[field, rows, :] + update[:, f * LEV : (f + 1) * LEV]
            return carry

        lax.fori_loop(0, TX, add, 0)

    for h in range(NH):
        back_copies[h].wait()
        wait_all(rcvb, h, brecv)
        flatten(rcvb, h)

        def ungroup(block, carry):
            rows = pl.ds(pl.multiple_of(block * 256, 256), 256)
            moved = dot(sel_t[rows, :], flat[...])
            for x in range(4):
                for i in range(2):
                    base = pl.multiple_of((block * 4 + x + 1) * RX + i * 40, 8)
                    piece = moved[x * 64 + i * 32 : x * 64 + i * 32 + 32, :]
                    for u in range(2):
                        grid[h, u, pl.ds(base, 32), :] = piece[:, u * 128 : (u + 1) * 128]
            return carry

        lax.fori_loop(0, 4, ungroup, 0)
        for u in range(2):
            for i in range(2):
                tx[h, 0, u, i * 32 : i * 32 + 32, :] = grid[h, u, 16 * RX + i * 40 : 16 * RX + i * 40 + 32, :]
                tx[h, 1, u, i * 32 : i * 32 + 32, :] = grid[h, u, RX + i * 40 : RX + i * 40 + 32, :]
            for j in range(2):
                ty[h, 0, u, j * 32 : j * 32 + 32, :] = grid[h, u, pl.ds(RX + 30 + j, 32, stride=40), :]
                ty[h, 1, u, j * 32 : j * 32 + 32, :] = grid[h, u, pl.ds(RX + j, 32, stride=40), :]
            for at, (_, _, _, x, y, _) in enumerate(CORNERS):
                for i in range(2):
                    base = (x + 1) * RX + i * 40 + 2 * y
                    tc[h, at, u * 4 + i * 2 : u * 4 + i * 2 + 2, :] = grid[h, u, base : base + 2, :]
        copies = [
            copy_to(tx.at[h, 0], ux.at[h, 0], gsend.at[h, 0], grecv.at[h, 0], 1, 0),
            copy_to(tx.at[h, 1], ux.at[h, 1], gsend.at[h, 1], grecv.at[h, 1], -1, 0),
            copy_to(ty.at[h, 0], uy.at[h, 0], gsend.at[h, 2], grecv.at[h, 2], 0, 1),
            copy_to(ty.at[h, 1], uy.at[h, 1], gsend.at[h, 3], grecv.at[h, 3], 0, -1),
        ]
        for at, (dgx, dgy, to, _, _, _) in enumerate(CORNERS):
            copies.append(
                copy_to(tc.at[h, at], uc.at[h, at], gsend.at[h, to], grecv.at[h, to], dgx, dgy)
            )
        for copy in copies:
            copy.start()
        ring_copies.append(copies)
        for copy in copies:
            copy.wait_recv()
        for u in range(2):
            for i in range(2):
                part = slice(i * 32, i * 32 + 32)
                grid[h, u, i * 40 : i * 40 + 32, :] = ux[h, 0, u, part, :]
                grid[h, u, 17 * RX + i * 40 : 17 * RX + i * 40 + 32, :] = ux[h, 1, u, part, :]
            for j in range(2):
                part = slice(j * 32, j * 32 + 32)
                grid[h, u, pl.ds(RX + 32 + j, 32, stride=40), :] = uy[h, 0, u, part, :]
                grid[h, u, pl.ds(RX + 34 + j, 32, stride=40), :] = uy[h, 1, u, part, :]
            for at, (big_x, base) in enumerate(((0, 32), (17, 32), (0, 34), (17, 34))):
                for i in range(2):
                    to = big_x * RX + i * 40 + base
                    grid[h, u, to : to + 2, :] = uc[h, at, u * 4 + i * 2 : u * 4 + i * 2 + 2, :]
            gridb[:, u * 128 : (u + 1) * 128] = grid[h, u].astype(BF16)
        finish(h)


    pltpu.make_async_copy(others_x, others_x, wsend).wait()
    pltpu.make_async_copy(others_y, others_y, vsend).wait()
    for h in range(NH):
        wait_all(outb, h, fsend)
        wait_all(backb, h, bsend)
        for copy in halo_copies[h] + ring_copies[h]:
            copy.wait_send()


def place_kernel(cell_ref, total, out_hbm, sem):
    def step(s, carry):
        for k in range(8):
            at = s * 8 + k
            cell = cell_ref[at]
            tile = ((cell >> 7) & 15) * 16 + (cell & 15)
            pltpu.make_async_copy(total.at[:, tile], out_hbm.at[:, at], sem).start()
        return carry

    lax.fori_loop(0, NE // 8, step, 0)
    pltpu.make_async_copy(total, out_hbm, sem).wait()


def any_spec():
    return pl.BlockSpec(memory_space=pl.ANY)


def hbm_spec():
    return pl.BlockSpec(memory_space=pltpu.HBM)


def vmem_spec():
    return pl.BlockSpec(memory_space=pltpu.VMEM)


def smem_spec():
    return pl.BlockSpec(memory_space=pltpu.SMEM)


def per_device(coltab, uptab, state_in, stiffness, elem_cell, group_column, group_inverse):
    dma = pltpu.SemaphoreType.DMA
    vmem = pltpu.VMEM
    scratch = [
        vmem((64, LEV, LEV), BF16),
        vmem((2, NE, 16, LEV), F32),
        vmem((2, NE, 16, LEV), F32),
        vmem((256, 256), F32),
        vmem((NE * 16, 256), BF16),
        vmem((2, 128), I32),
        pltpu.SMEM((2, 128), I32),
        vmem((4, NHALO, 16, LEV), F32),
        vmem((128, 128), F32),
        vmem((NX, NY, 1, 128), F32),
        vmem((NX, NY, 1, 128), F32),
        vmem((NX, NY, 1, 128), F32),
        vmem((8, 128), F32),
        vmem((8, 128), F32),
        vmem((NC, NC), BF16),
        vmem((NC, NC), BF16),
        vmem((NC, NC), BF16),
        vmem((NC, NC), BF16),
        vmem((256, 256), BF16),
        vmem((256, 256), BF16),
        vmem((NC, 256), BF16),
        vmem((NH, ND, 8, 256), BF16),
        vmem((NH, ND, 8, 256), BF16),
        vmem((NH, ND, 8, 256), BF16),
        vmem((NH, ND, 8, 256), BF16),
        vmem((NC, 256), BF16),
        vmem((NC, 256), BF16),
        vmem((NH, 2, RROWS, LEV), F32),
        vmem((RROWS, 256), BF16),
        vmem((NH, 2, 2, 64, LEV), F32),
        vmem((NH, 2, 2, 64, LEV), F32),
        vmem((NH, 4, 8, LEV), F32),
        vmem((NH, 2, 2, 64, LEV), F32),
        vmem((NH, 2, 2, 64, LEV), F32),
        vmem((NH, 4, 8, LEV), F32),
        vmem((NH, 2, 2, 64, LEV), F32),
        vmem((NH, 2, 2, 64, LEV), F32),
        vmem((NH, 4, 8, LEV), F32),
        vmem((NH, 2, 2, 64, LEV), F32),
        vmem((NH, 2, 2, 64, LEV), F32),
        vmem((NH, 4, 8, LEV), F32),
        dma((NH, 4)), dma((3,)), dma, dma, dma, dma, dma((5,)),
        dma((NH,)), dma((NH,)), dma((NH,)), dma((NH,)),
        dma((NH, 8)), dma((NH, 8)), dma((NH, 8)), dma((NH, 8)),
    ]
    total = pl.pallas_call(
        exchange_kernel,
        out_shape=jax.ShapeDtypeStruct((4, NE * 16, LEV), F32),
        in_specs=[any_spec()] * 3 + [vmem_spec()] * 4,
        out_specs=vmem_spec(),
        scratch_shapes=scratch,
        compiler_params=pltpu.CompilerParams(
            collective_id=0, has_side_effects=True, vmem_limit_bytes=43 << 20
        ),
        name="exchange",
    )(
        state_in, stiffness.reshape(256, NE), group_inverse, elem_cell.reshape(2, 128),
        group_column.reshape(8, 128), coltab, uptab,
    )
    return pl.pallas_call(
        place_kernel,
        out_shape=jax.ShapeDtypeStruct((4, NE, 16, LEV), F32),
        in_specs=[smem_spec(), vmem_spec()],
        out_specs=any_spec(),
        scratch_shapes=[dma],
        compiler_params=pltpu.CompilerParams(vmem_limit_bytes=4 << 20),
        name="place",
    )(elem_cell, total.reshape(4, NE, 16, LEV))


def solution(mesh):
    coltab, uptab = constant_tables()
    placed = (
        P(None, ("gx", "gy"), None, None),
        P(None, None, ("gx", "gy")),
        P(("gx", "gy")),
        P(("gx", "gy")),
        P(("gx", "gy"), None, None),
    )

    def run(*args):
        body = functools.partial(per_device, jnp.asarray(coltab), jnp.asarray(uptab))
        return jax.shard_map(
            body,
            mesh=mesh,
            in_specs=placed,
            out_specs=P(None, ("gx", "gy"), None, None),
            check_vma=False,
        )(*args)

    return run
```

```python
import functools
import math

import jax
import jax.numpy as jnp
import ml_dtypes
import numpy as np
from jax import lax
from jax.experimental import pallas as pl
from jax.experimental.pallas import tpu as pltpu
from jax.sharding import PartitionSpec as P

F32, BF16, I32 = jnp.float32, jnp.bfloat16, jnp.int32
MESH = pl.DeviceIdType.MESH
NX, NY = 16, 8
ND = NX * NY
TX = TY = 16
NE = TX * TY
NC = 4 * NE
LEV = 128
NH = 2
WEST, EAST, SOUTH, NORTH = 0, 18, 36, 52
NHALO = 68
RX = 80
RROWS = 18 * RX + 16
CORNERS = (
    (1, 1, 4, 15, 15, 15),
    (-1, 1, 5, 0, 15, 3),
    (1, -1, 6, 15, 0, 12),
    (-1, -1, 7, 0, 0, 0),
)


def lagrange_value(node, position, nodes):
    value = 1.0
    for other in range(4):
        if other != node:
            value *= (position - nodes[other]) / (nodes[node] - nodes[other])
    return value


def tables():
    nodes = [-1.0, -1.0 / math.sqrt(5.0), 1.0 / math.sqrt(5.0), 1.0]
    halves = np.zeros((2, 4))
    for i, (low, high) in enumerate(((-1.0, 0.0), (0.0, 1.0))):
        centre, offset = 0.5 * (low + high), 0.5 * (high - low) / math.sqrt(3.0)
        for a in range(4):
            halves[i, a] = (
                0.5
                * (high - low)
                * (
                    lagrange_value(a, centre - offset, nodes)
                    + lagrange_value(a, centre + offset, nodes)
                )
            )
    spread = halves.T @ np.linalg.inv(halves @ halves.T)
    return halves.astype(np.float32).astype(np.float64), spread.astype(np.float32).astype(np.float64)


def split_bf16(table):
    high = table.astype(ml_dtypes.bfloat16)
    low = (table - high.astype(np.float64)).astype(ml_dtypes.bfloat16)
    return high, low


def constant_tables():
    halves, spread = tables()
    cols = np.einsum("ia,jb,yz->iyjzab", halves, halves, np.eye(TY)).reshape(64, 256)
    col_high, col_low = split_bf16(cols)
    along = np.zeros((4, 3, 2))
    along[:, 1, :] = spread
    along[0, 0, :] += spread[3]
    along[3, 2, :] += spread[0]
    along[0] *= 0.5
    along[3] *= 0.5
    along_y = np.zeros((TY, 4, 40))
    for y in range(TY):
        for step in range(3):
            other = y + step - 1
            base = 32 if other < 0 else 34 if other >= TY else 2 * other
            along_y[y, :, base : base + 2] += along[:, step, :]
    update = np.zeros((256, 256))
    update[:, :240] = np.einsum("asi,ybr->yabsir", along, along_y).reshape(256, 240)
    up_high, up_low = split_bf16(update)
    return np.concatenate([up_high, up_low, col_high, col_low], 0)


def iota(shape, dim):
    return lax.broadcasted_iota(I32, shape, dim)


def dot(left, right):
    return jnp.dot(left, right, preferred_element_type=F32)


def dot_nt(left, right):
    return lax.dot_general(left, right, (((1,), (1,)), ((), ())), preferred_element_type=F32)


class Peers:
    def __init__(self, gx, gy):
        self.x, self.y = lax.div(gx, 4), lax.rem(gx, 4)
        self.z, self.core = lax.div(gy, 2), lax.rem(gy, 2)
        self.xs = [lax.rem(self.x + a, 4) * 4 for a in range(4)]
        self.zs = [lax.rem(self.z + d, 4) * 2 for d in range(4)]
        self.cores = [self.core, 1 - self.core]

    def block(self, b, with_self=False):
        ys = [lax.rem(self.y + b + a, 4) for a in range(4)]
        back_b = lax.rem(4 - b, 4) if not isinstance(b, int) else -b % 4
        found = []
        for d in range(4):
            for a in range(4):
                for c in range(2):
                    if isinstance(b, int) and b == d == a == c == 0 and not with_self:
                        continue
                    tgx = self.xs[a] + ys[a]
                    tgy = self.zs[(d + a) % 4] + self.cores[c]
                    inner = d * 8 + a * 2 + c
                    back = -d % 4 * 8 + -a % 4 * 2 + c
                    found.append((tgx, tgy, b * 32 + inner, back_b * 32 + back))
        return found

    def position(self, source):
        a = ((source >> 5) - self.x) & 3
        b = (((source >> 3) & 3) - self.y - a) & 3
        d = (((source >> 1) & 3) - self.z - a) & 3
        c = ((source & 1) - self.core) & 1
        return b * 32 + d * 8 + a * 2 + c


def exchange_kernel(
    state_hbm, stiff_hbm, inv_hbm, cell_hbm, gcol_hbm, table_hbm,
    dyn,
    cell_ref, gcol_ref, table_ref, inv, st0, st1, xs, w16, slot_vmem, slots,
    halo, wv, wq, mid, req, qrow, crow,
    sel, sel_t, place, place_t,
    dyn_high, dyn_low, cols, outb, incb, backb, rcvb, flat, tend, grid, gridb,
    sx, sy, sc, rx, ry, rc,
    tx, ty, tc, ux, uy, uc,
    state_sem, in_sem, wsend, wrecv, vsend, vrecv, loc_sem,
    fsend, frecv, bsend, brecv, hsend, hrecv, gsend, grecv,
):
    st = (st0, st1)
    gx, gy = lax.axis_index("gx"), lax.axis_index("gy")
    peers = Peers(gx, gy)
    barrier = pltpu.get_barrier_semaphore()

    def other_x(k):
        return lax.rem(gx + k, NX)

    def other_y(k):
        return lax.rem(gy + k, NY)

    for dgx, dgy, _, _, _, _ in CORNERS:
        pl.semaphore_signal(
            barrier, inc=1, device_id=(other_x(NX + dgx), other_y(NY + dgy)), device_id_type=MESH
        )

    def greet_x(k, carry):
        pl.semaphore_signal(barrier, inc=1, device_id=(other_x(k), gy), device_id_type=MESH)
        return carry

    def greet_y(k, carry):
        pl.semaphore_signal(barrier, inc=1, device_id=(gx, other_y(k)), device_id_type=MESH)
        return carry

    lax.fori_loop(1, NX, greet_x, 0)
    lax.fori_loop(1, NY, greet_y, 0)


    small_copies = []
    for at, (src, dst) in enumerate(((cell_hbm, cell_ref), (gcol_hbm, gcol_ref))):
        copy = pltpu.make_async_copy(src, dst, in_sem.at[3 + at])
        copy.start()
        small_copies.append(copy)
    stiff_copy = pltpu.make_async_copy(stiff_hbm, xs, in_sem.at[0])
    stiff_copy.start()
    state_copies = []
    for h in range(NH):
        row = []
        for part in range(4):
            elems = pl.ds(part * 64, 64)
            copy = pltpu.make_async_copy(
                state_hbm.at[pl.ds(2 * h, 2), elems], st[h].at[:, elems], state_sem.at[h, part]
            )
            copy.start()
            row.append(copy)
        state_copies.append(row)

    inv_copy = pltpu.make_async_copy(inv_hbm, inv, in_sem.at[2])
    inv_copy.start()
    table_copy = pltpu.make_async_copy(table_hbm, table_ref, in_sem.at[5])
    table_copy.start()

    lane = iota((128, 128), 1)
    sub = iota((128, 128), 0)
    eye = lane == sub

    def to_col(row):
        return jnp.sum(jnp.where(eye, jnp.broadcast_to(row, (128, 128)), 0.0), axis=1, keepdims=True)

    def to_row(col):
        return jnp.sum(jnp.where(eye, jnp.broadcast_to(col, (128, 128)), 0.0), axis=0, keepdims=True)

    def tiles(u):
        cell = cell_ref[u : u + 1, :]
        return (((cell >> 7) & 15) * 16 + (cell & 15)).astype(F32)

    for copy in small_copies:
        copy.wait()
    for v in range(2):
        found = jnp.zeros((128, 128), F32)
        for u in range(2):
            at = to_col(tiles(u))
            number = (sub + 128 * u).astype(F32)
            found = jnp.maximum(found, jnp.where(at == (lane + 128 * v).astype(F32), number, 0.0))
        slot_vmem[v : v + 1, :] = jnp.max(found, axis=0, keepdims=True).astype(I32)
    slot_copy = pltpu.make_async_copy(slot_vmem, slots, in_sem.at[1])
    slot_copy.start()

    upper = jnp.where(sub < lane, 1.0, 0.0).astype(BF16)
    seen = jnp.zeros((128, 1), F32)
    want_high = jnp.zeros((128, 128), F32)
    want_low = jnp.zeros((128, 128), F32)
    for block in range(8):
        named = gcol_ref[block : block + 1, :]
        source, local = named >> 10, named & 1023
        hit = jnp.broadcast_to(source, (128, 128)) == sub
        onehot = jnp.where(hit, 1.0, 0.0)
        before = dot(onehot.astype(BF16), upper) + seen
        seen = seen + jnp.sum(onehot, axis=1, keepdims=True)
        rank = jnp.sum(jnp.where(hit, before, 0.0), axis=0, keepdims=True)
        qrow[block : block + 1, :] = peers.position(source).astype(F32) * 8.0 + rank
        ranked = jnp.broadcast_to(rank, (128, 128)) == sub.astype(F32)
        high = (local >> 5).astype(F32)
        low = (local & 31).astype(F32)
        zero = jnp.zeros((128, 128), F32)
        chosen_high = jnp.where(ranked, jnp.broadcast_to(high, (128, 128)), zero).astype(BF16)
        chosen_low = jnp.where(ranked, jnp.broadcast_to(low, (128, 128)), zero).astype(BF16)
        onehot = onehot.astype(BF16)
        want_high = want_high + dot_nt(onehot, chosen_high)
        want_low = want_low + dot_nt(onehot, chosen_low)
    wv[...] = want_high * 32.0 + want_low

    def row_out(s, carry):
        for y in range(NY):
            wq[s, y] = wv[pl.ds(s * NY + y, 1), :]
        return carry

    lax.fori_loop(0, NX, row_out, 0)
    stiff_copy.wait()
    flipped = xs[...].T.astype(BF16)
    row_i, col_i = iota((256, 256), 0), iota((256, 256), 1)
    same_m = (row_i & 15) == (col_i & 15)
    diagonal = (row_i & 15) == (col_i >> 4)
    for n in range(16):
        pick = jnp.where(same_m & ((row_i >> 4) == n), 1.0, 0.0).astype(BF16)
        block = jnp.where(diagonal, dot(flipped, pick), 0.0)
        for u in range(2):
            dyn[u, pl.ds(n, 256, stride=16), :] = block[:, u * 128 : (u + 1) * 128]

    pl.semaphore_wait(barrier, NX + NY - 2 + len(CORNERS))

    def ask_x(k, carry):
        pltpu.make_async_remote_copy(
            wq.at[other_x(k)], mid.at[gx], wsend, wrecv,
            device_id=(other_x(k), gy), device_id_type=MESH,
        ).start()
        return carry

    lax.fori_loop(1, NX, ask_x, 0)
    own_x = pltpu.make_async_copy(wq.at[gx], mid.at[gx], loc_sem.at[0])
    own_x.start()

    others_x = mid.at[pl.ds(0, NX - 1)]
    others_y = req.at[:, pl.ds(0, NY - 1)]

    def ask_y(k, carry):
        pltpu.make_async_remote_copy(
            mid.at[:, other_y(k)], req.at[:, gy], vsend, vrecv,
            device_id=(gx, other_y(k)), device_id_type=MESH,
        ).start()
        return carry

    def combine(h):
        def step(g, carry):
            rows = pl.ds(pl.multiple_of(g * 256, 256), 256)
            elems = pl.ds(g * 16, 16)
            both = jnp.concatenate([st[h][f, elems].reshape(256, LEV) for f in range(2)], axis=1)
            if h == 0:
                oper = jnp.concatenate([dyn[0, rows, :], dyn[1, rows, :]], axis=1).astype(BF16)
                w16[rows, :] = oper
            else:
                oper = w16[rows, :]
            both = both + dot(oper, both.astype(BF16))
            for f in range(2):
                st[h][f, elems] = both[:, f * LEV : (f + 1) * LEV].reshape(16, 16, LEV)
            return carry

        for part in range(4):
            state_copies[h][part].wait()
            lax.fori_loop(part * 4, part * 4 + 4, step, 0)

    def slot(x, y):
        if isinstance(x, int):
            return slots[x // 8, x % 8 * 16 + y] & (NE - 1)
        return slots[lax.div(x, 8), lax.rem(x, 8) * 16 + y] & (NE - 1)

    def copy_to(src, dst, send, recv, dgx, dgy):
        return pltpu.make_async_remote_copy(
            src, dst, send, recv,
            device_id=((gx + dgx + NX) % NX, (gy + dgy + NY) % NY),
            device_id_type=MESH,
        )

    def send_halo(h):
        for f in range(2):
            field = 2 * h + f

            for k in range(16):
                part = pl.ds(k * 4, 4)
                sx[h, 0, f, part, :] = st[h][f, slot(15, k), 8:16, :][4:8]
                sx[h, 1, f, part, :] = st[h][f, slot(0, k), 0:8, :][0:4]
                for side, y, b in ((0, 15, 3), (1, 0, 0)):
                    at = slot(k, y)
                    for v in range(2):
                        half = st[h][f, at, v * 8 : v * 8 + 8, :]
                        for a in range(2):
                            to = k * 4 + v * 2 + a
                            sy[h, side, f, to : to + 1, :] = half[a * 4 + b : a * 4 + b + 1]
            for at, (_, _, _, x, y, n) in enumerate(CORNERS):
                half = st[h][f, slot(x, y), n // 8 * 8 : n // 8 * 8 + 8, :]
                sc[h, at, f : f + 1, :] = half[n % 8 : n % 8 + 1]
        copies = [
            copy_to(sx.at[h, 0], rx.at[h, 0], hsend.at[h, 0], hrecv.at[h, 0], 1, 0),
            copy_to(sx.at[h, 1], rx.at[h, 1], hsend.at[h, 1], hrecv.at[h, 1], -1, 0),
            copy_to(sy.at[h, 0], ry.at[h, 0], hsend.at[h, 2], hrecv.at[h, 2], 0, 1),
            copy_to(sy.at[h, 1], ry.at[h, 1], hsend.at[h, 3], hrecv.at[h, 3], 0, -1),
        ]
        for at, (dgx, dgy, to, _, _, _) in enumerate(CORNERS):
            copies.append(
                copy_to(sc.at[h, at], rc.at[h, at], hsend.at[h, to], hrecv.at[h, to], dgx, dgy)
            )
        for copy in copies:
            copy.start()
        return copies

    def take_halo(h, copies):
        for copy in copies:
            copy.wait_recv()
        for f in range(2):
            field = 2 * h + f
            for k in range(16):
                part = pl.ds(k * 4, 4)
                halo[field, WEST + 1 + k, 12:16, :] = rx[h, 0, f, part, :]
                halo[field, EAST + 1 + k, 0:4, :] = rx[h, 1, f, part, :]
                halo[field, SOUTH + k, pl.ds(3, 4, stride=4), :] = ry[h, 0, f, part, :]
                halo[field, NORTH + k, pl.ds(0, 4, stride=4), :] = ry[h, 1, f, part, :]
            halo[field, WEST, 15:16, :] = rc[h, 0, f : f + 1, :]
            halo[field, EAST, 3:4, :] = rc[h, 1, f : f + 1, :]
            halo[field, WEST + 17, 12:13, :] = rc[h, 2, f : f + 1, :]
            halo[field, EAST + 17, 0:1, :] = rc[h, 3, f : f + 1, :]

    s8 = iota((8, 128), 0)
    b_at = s8 & 3
    is_b0, is_b3, first_a = b_at == 0, b_at == 3, s8 < 4
    b_scale = jnp.where(is_b0 | is_b3, 0.5, 1.0)
    scale0 = b_scale * jnp.where(first_a, 0.5, 1.0)
    scale1 = b_scale * jnp.where(first_a, 1.0, 0.5)

    def dynamics(h):
        def column(x, carry):
            fixed = isinstance(x, int)

            def inside(x, y):
                return 0 <= y < TY and not (fixed and not 0 <= x < TX)

            def locate(x, y):
                if inside(x, y):
                    return slot(x, y)
                if fixed and x == -1:
                    return WEST + y + 1
                if fixed and x == TX:
                    return EAST + y + 1
                return (SOUTH if y < 0 else NORTH) + x

            def load(f, x, y, at, v):
                if inside(x, y):
                    return st[h][f, at, v * 8 : v * 8 + 8, :]
                return halo[2 * h + f, at, v * 8 : v * 8 + 8, :]

            def along_x(y):
                found = []
                mine, west, east = locate(x, y), locate(x - 1, y), locate(x + 1, y)
                for f in range(2):
                    own0, own1 = load(f, x, y, mine, 0), load(f, x, y, mine, 1)
                    before, after = load(f, x - 1, y, west, 1), load(f, x + 1, y, east, 0)
                    found.append(own0 + jnp.where(first_a, pltpu.roll(before, 4, 0), 0.0))
                    found.append(own1 + jnp.where(first_a, 0.0, pltpu.roll(after, 4, 0)))
                return found

            south, here = along_x(-1), along_x(0)
            for y in range(TY):
                north = along_x(y + 1)
                for f in range(2):
                    parts = []
                    for v, scale in ((2 * f, scale0), (2 * f + 1, scale1)):
                        edge = jnp.where(is_b0, pltpu.roll(south[v], 5, 0), 0.0)
                        edge = jnp.where(is_b3, pltpu.roll(north[v], 3, 0), edge)
                        parts.append((here[v] + edge) * scale)
                    total = jnp.concatenate(parts, axis=0)
                    at = x * 256 + y * 16
                    dyn[2 * h + f, pl.ds(at if fixed else pl.multiple_of(at, 16), 16), :] = total
                    high = total.astype(BF16)
                    dyn_high[y * 16 : y * 16 + 16, f * 128 : f * 128 + 128] = high
                    low = (total - high.astype(F32)).astype(BF16)
                    dyn_low[y * 16 : y * 16 + 16, f * 128 : f * 128 + 128] = low
                south, here = here, north
            main = dot(table_ref[512:640, :], dyn_high[...])
            rest = dot(table_ref[512:576, :], dyn_low[...])
            total = main[0:64] + main[64:128] + rest
            cols[pl.ds(x * 64 if fixed else pl.multiple_of(x * 64, 64), 64), :] = total.astype(BF16)
            return carry

        column(0, 0)
        lax.fori_loop(1, TX - 1, column, 0)
        column(TX - 1, 0)

    wide = iota((128, 1024), 1)

    def selections():
        k_mask = iota((128, 128), 1) == (iota((128, 128), 0) & 7)

        def build(b, carry):
            found = peers.block(b, with_self=True)
            for part in range(2):
                asked = [
                    jnp.broadcast_to(req[tgx, tgy], (8, 128))
                    for tgx, tgy, _, _ in found[part * 16 : part * 16 + 16]
                ]
                asked = jnp.where(k_mask, jnp.concatenate(asked, axis=0), 0.0)
                asked = jnp.sum(asked, axis=1, keepdims=True).astype(I32)
                slot_at, piece = asked >> 2, asked & 3
                tile = jnp.zeros((128, 128), F32)
                for u in range(2):
                    names = jnp.broadcast_to(tiles(u), (128, 128))
                    tile = tile + jnp.where(slot_at == lane + 128 * u, names, 0.0)
                tile = jnp.sum(tile, axis=1, keepdims=True).astype(I32)
                at = (tile >> 4) * 64 + (piece >> 1) * 32 + (tile & 15) * 2 + (piece & 1)
                block = b * 2 + part
                rows = pl.ds(pl.multiple_of(block * 128, 128), 128)
                sel[rows, :] = jnp.where(wide == at, 1.0, 0.0).astype(BF16)
                crow[pl.ds(block, 1), :] = to_row(at.astype(F32))
            return carry

        lax.fori_loop(0, 4, build, 0)

    def transposed(row_ref, out_ref):
        def build(block, carry):
            rows = pl.ds(pl.multiple_of(block * 128, 128), 128)
            want = (sub + block * 128).astype(F32)
            for u in range(8):
                names = jnp.broadcast_to(row_ref[u : u + 1, :], (128, 128))
                out_ref[rows, u * 128 : (u + 1) * 128] = jnp.where(names == want, 1.0, 0.0).astype(BF16)
            return carry

        lax.fori_loop(0, 8, build, 0)

    def placing():
        def build(block, carry):
            rows = pl.ds(pl.multiple_of(block * 128, 128), 128)
            at = to_col(qrow[pl.ds(block, 1), :]).astype(I32)
            place[rows, :] = jnp.where(wide == at, 1.0, 0.0).astype(BF16)
            return carry

        lax.fori_loop(0, 8, build, 0)

    def permute_and_send(matrix, source, src, dst, h, send, recv, loc):
        def step(b):
            rows = pl.ds(pl.multiple_of(b * 256, 256), 256)
            moved = dot(matrix[rows, :], source[...])
            src[h, pl.ds(b * 32, 32)] = moved.reshape(32, 8, 256).astype(BF16)
            for tgx, tgy, at, back in peers.block(b):
                pltpu.make_async_remote_copy(
                    src.at[h, at], dst.at[h, back], send.at[h], recv.at[h],
                    device_id=(tgx, tgy), device_id_type=MESH,
                ).start()

        def loop_step(b, carry):
            step(b)
            return carry

        step(0)
        own = pltpu.make_async_copy(src.at[h, 0], dst.at[h, 0], loc_sem.at[loc])
        own.start()
        lax.fori_loop(1, 4, loop_step, 0)
        return own

    def wait_all(ref, h, sem):
        block = ref.at[h, pl.ds(0, ND - 1)]
        pltpu.make_async_copy(block, block, sem.at[h]).wait()

    def flatten(src, h):
        def step(block, carry):
            part = src[h, pl.ds(block * 16, 16)].astype(F32).reshape(128, 256)
            flat[pl.ds(pl.multiple_of(block * 128, 128), 128), :] = part.astype(BF16)
            return carry

        lax.fori_loop(0, 8, step, 0)

    halo_copies, forward, back_copies = [None] * NH, [None] * NH, [None] * NH
    combine(0)
    own_x.wait()
    pltpu.make_async_copy(others_x, others_x, wrecv).wait()
    lax.fori_loop(1, NY, ask_y, 0)
    own_y = pltpu.make_async_copy(mid.at[:, gy], req.at[:, gy], loc_sem.at[0])
    own_y.start()
    slot_copy.wait()
    halo_copies[0] = send_halo(0)
    transposed(qrow, place_t)
    placing()
    own_y.wait()
    pltpu.make_async_copy(others_y, others_y, vrecv).wait()
    selections()
    take_halo(0, halo_copies[0])
    table_copy.wait()
    dynamics(0)
    forward[0] = permute_and_send(sel, cols, outb, incb, 0, fsend, frecv, 1)
    combine(1)
    halo_copies[1] = send_halo(1)
    transposed(crow, sel_t)
    grid[...] = jnp.zeros_like(grid)
    take_halo(1, halo_copies[1])
    dynamics(1)
    forward[1] = permute_and_send(sel, cols, outb, incb, 1, fsend, frecv, 2)

    inv_copy.wait()

    def physics(h):
        def step(block, carry):
            rows = pl.ds(pl.multiple_of(block * 256, 256), 256)
            moved = dot(place[rows, :], flat[...])
            for g in range(16):
                part = moved[g * 16 : (g + 1) * 16, :]
                stacked = jnp.concatenate([part[:, :128], part[:, 128:]], axis=0)
                smooth = dot_nt(stacked.astype(BF16), inv[block * 16 + g])
                change = smooth - stacked
                change = jnp.concatenate([change[:16], change[16:]], axis=1)
                tend[pl.ds(pl.multiple_of(block * 256 + g * 16, 16), 16), :] = change.astype(BF16)
            return carry

        lax.fori_loop(0, 4, step, 0)

    for h in range(NH):
        forward[h].wait()
        wait_all(incb, h, frecv)
        flatten(incb, h)
        physics(h)
        back_copies[h] = permute_and_send(place_t, tend, backb, rcvb, h, bsend, brecv, 3 + h)

    ring_copies = []

    def finish(h):
        def add(x, carry):
            rows = pl.ds(pl.multiple_of(x * 256, 256), 256)
            near = gridb[pl.ds(pl.multiple_of(x * RX, 16), 256), :]
            update = dot(table_ref[0:512, :], near)
            update = update[:256] + update[256:]
            for f in range(2):
                field = 2 * h + f
                dyn[field, rows, :] = dyn[field, rows, :] + update[:, f * LEV : (f + 1) * LEV]
            return carry

        lax.fori_loop(0, TX, add, 0)

    for h in range(NH):
        back_copies[h].wait()
        wait_all(rcvb, h, brecv)
        flatten(rcvb, h)

        def ungroup(block, carry):
            rows = pl.ds(pl.multiple_of(block * 256, 256), 256)
            moved = dot(sel_t[rows, :], flat[...])
            for x in range(4):
                for i in range(2):
                    base = pl.multiple_of((block * 4 + x + 1) * RX + i * 40, 8)
                    piece = moved[x * 64 + i * 32 : x * 64 + i * 32 + 32, :]
                    for u in range(2):
                        grid[h, u, pl.ds(base, 32), :] = piece[:, u * 128 : (u + 1) * 128]
            return carry

        lax.fori_loop(0, 4, ungroup, 0)
        for u in range(2):
            for i in range(2):
                tx[h, 0, u, i * 32 : i * 32 + 32, :] = grid[h, u, 16 * RX + i * 40 : 16 * RX + i * 40 + 32, :]
                tx[h, 1, u, i * 32 : i * 32 + 32, :] = grid[h, u, RX + i * 40 : RX + i * 40 + 32, :]
            for j in range(2):
                ty[h, 0, u, j * 32 : j * 32 + 32, :] = grid[h, u, pl.ds(RX + 30 + j, 32, stride=40), :]
                ty[h, 1, u, j * 32 : j * 32 + 32, :] = grid[h, u, pl.ds(RX + j, 32, stride=40), :]
            for at, (_, _, _, x, y, _) in enumerate(CORNERS):
                for i in range(2):
                    base = (x + 1) * RX + i * 40 + 2 * y
                    tc[h, at, u * 4 + i * 2 : u * 4 + i * 2 + 2, :] = grid[h, u, base : base + 2, :]
        copies = [
            copy_to(tx.at[h, 0], ux.at[h, 0], gsend.at[h, 0], grecv.at[h, 0], 1, 0),
            copy_to(tx.at[h, 1], ux.at[h, 1], gsend.at[h, 1], grecv.at[h, 1], -1, 0),
            copy_to(ty.at[h, 0], uy.at[h, 0], gsend.at[h, 2], grecv.at[h, 2], 0, 1),
            copy_to(ty.at[h, 1], uy.at[h, 1], gsend.at[h, 3], grecv.at[h, 3], 0, -1),
        ]
        for at, (dgx, dgy, to, _, _, _) in enumerate(CORNERS):
            copies.append(
                copy_to(tc.at[h, at], uc.at[h, at], gsend.at[h, to], grecv.at[h, to], dgx, dgy)
            )
        for copy in copies:
            copy.start()
        ring_copies.append(copies)
        for copy in copies:
            copy.wait_recv()
        for u in range(2):
            for i in range(2):
                part = slice(i * 32, i * 32 + 32)
                grid[h, u, i * 40 : i * 40 + 32, :] = ux[h, 0, u, part, :]
                grid[h, u, 17 * RX + i * 40 : 17 * RX + i * 40 + 32, :] = ux[h, 1, u, part, :]
            for j in range(2):
                part = slice(j * 32, j * 32 + 32)
                grid[h, u, pl.ds(RX + 32 + j, 32, stride=40), :] = uy[h, 0, u, part, :]
                grid[h, u, pl.ds(RX + 34 + j, 32, stride=40), :] = uy[h, 1, u, part, :]
            for at, (big_x, base) in enumerate(((0, 32), (17, 32), (0, 34), (17, 34))):
                for i in range(2):
                    to = big_x * RX + i * 40 + base
                    grid[h, u, to : to + 2, :] = uc[h, at, u * 4 + i * 2 : u * 4 + i * 2 + 2, :]
            gridb[:, u * 128 : (u + 1) * 128] = grid[h, u].astype(BF16)
        finish(h)


    pltpu.make_async_copy(others_x, others_x, wsend).wait()
    pltpu.make_async_copy(others_y, others_y, vsend).wait()
    for h in range(NH):
        wait_all(outb, h, fsend)
        wait_all(backb, h, bsend)
        for copy in halo_copies[h] + ring_copies[h]:
            copy.wait_send()


def place_kernel(cell_ref, total, out_hbm, sem):
    def step(s, carry):
        for k in range(8):
            at = s * 8 + k
            cell = cell_ref[at]
            tile = ((cell >> 7) & 15) * 16 + (cell & 15)
            pltpu.make_async_copy(total.at[:, tile], out_hbm.at[:, at], sem).start()
        return carry

    lax.fori_loop(0, NE // 8, step, 0)
    pltpu.make_async_copy(total, out_hbm, sem).wait()


def any_spec():
    return pl.BlockSpec(memory_space=pl.ANY)


def in_hbm(array):
    return pltpu.with_memory_space_constraint(array, pltpu.HBM)


def hbm_spec():
    return pl.BlockSpec(memory_space=pltpu.HBM)


def vmem_spec():
    return pl.BlockSpec(memory_space=pltpu.VMEM)


def smem_spec():
    return pl.BlockSpec(memory_space=pltpu.SMEM)


def per_device(table, state_in, stiffness, elem_cell, group_column, group_inverse):
    dma = pltpu.SemaphoreType.DMA
    vmem = pltpu.VMEM
    scratch = [
        vmem((2, 128), I32),
        vmem((8, 128), I32),
        vmem((640, 256), BF16),
        vmem((64, LEV, LEV), BF16),
        vmem((2, NE, 16, LEV), F32),
        vmem((2, NE, 16, LEV), F32),
        vmem((256, 256), F32),
        vmem((NE * 16, 256), BF16),
        vmem((2, 128), I32),
        pltpu.SMEM((2, 128), I32),
        vmem((4, NHALO, 16, LEV), F32),
        vmem((128, 128), F32),
        vmem((NX, NY, 1, 128), F32),
        vmem((NX, NY, 1, 128), F32),
        vmem((NX, NY, 1, 128), F32),
        vmem((8, 128), F32),
        vmem((8, 128), F32),
        vmem((NC, NC), BF16),
        vmem((NC, NC), BF16),
        vmem((NC, NC), BF16),
        vmem((NC, NC), BF16),
        vmem((256, 256), BF16),
        vmem((256, 256), BF16),
        vmem((NC, 256), BF16),
        vmem((NH, ND, 8, 256), BF16),
        vmem((NH, ND, 8, 256), BF16),
        vmem((NH, ND, 8, 256), BF16),
        vmem((NH, ND, 8, 256), BF16),
        vmem((NC, 256), BF16),
        vmem((NC, 256), BF16),
        vmem((NH, 2, RROWS, LEV), F32),
        vmem((RROWS, 256), BF16),
        vmem((NH, 2, 2, 64, LEV), F32),
        vmem((NH, 2, 2, 64, LEV), F32),
        vmem((NH, 4, 8, LEV), F32),
        vmem((NH, 2, 2, 64, LEV), F32),
        vmem((NH, 2, 2, 64, LEV), F32),
        vmem((NH, 4, 8, LEV), F32),
        vmem((NH, 2, 2, 64, LEV), F32),
        vmem((NH, 2, 2, 64, LEV), F32),
        vmem((NH, 4, 8, LEV), F32),
        vmem((NH, 2, 2, 64, LEV), F32),
        vmem((NH, 2, 2, 64, LEV), F32),
        vmem((NH, 4, 8, LEV), F32),
        dma((NH, 4)), dma((6,)), dma, dma, dma, dma, dma((5,)),
        dma((NH,)), dma((NH,)), dma((NH,)), dma((NH,)),
        dma((NH, 8)), dma((NH, 8)), dma((NH, 8)), dma((NH, 8)),
    ]
    total = pl.pallas_call(
        exchange_kernel,
        out_shape=jax.ShapeDtypeStruct((4, NE * 16, LEV), F32),
        in_specs=[any_spec()] * 6,
        out_specs=vmem_spec(),
        scratch_shapes=scratch,
        compiler_params=pltpu.CompilerParams(
            collective_id=0, has_side_effects=True, vmem_limit_bytes=44 << 20
        ),
        name="exchange",
    )(
        state_in, in_hbm(stiffness.reshape(256, NE)), in_hbm(group_inverse),
        in_hbm(elem_cell.reshape(2, 128)), in_hbm(group_column.reshape(8, 128)), in_hbm(table),
    )
    return pl.pallas_call(
        place_kernel,
        out_shape=jax.ShapeDtypeStruct((4, NE, 16, LEV), F32),
        in_specs=[smem_spec(), vmem_spec()],
        out_specs=any_spec(),
        scratch_shapes=[dma],
        compiler_params=pltpu.CompilerParams(vmem_limit_bytes=4 << 20),
        name="place",
    )(elem_cell, total.reshape(4, NE, 16, LEV))


def solution(mesh):
    table = constant_tables()
    placed = (
        P(None, ("gx", "gy"), None, None),
        P(None, None, ("gx", "gy")),
        P(("gx", "gy")),
        P(("gx", "gy")),
        P(("gx", "gy"), None, None),
    )

    def run(*args):
        body = functools.partial(per_device, jnp.asarray(table))
        return jax.shard_map(
            body,
            mesh=mesh,
            in_specs=placed,
            out_specs=P(None, ("gx", "gy"), None, None),
            check_vma=False,
        )(*args)

    return run
```

```python
import functools
import math

import jax
import jax.numpy as jnp
import ml_dtypes
import numpy as np
from jax import lax
from jax.experimental import pallas as pl
from jax.experimental.pallas import tpu as pltpu
from jax.sharding import PartitionSpec as P

F32, BF16, I32 = jnp.float32, jnp.bfloat16, jnp.int32
MESH = pl.DeviceIdType.MESH
NX, NY = 16, 8
ND = NX * NY
TX = TY = 16
NE = TX * TY
NC = 4 * NE
LEV = 128
NH = 2
WEST, EAST, SOUTH, NORTH = 0, 18, 36, 52
NHALO = 68
RX = 80
RROWS = 18 * RX + 16
CORNERS = (
    (1, 1, 4, 15, 15, 15),
    (-1, 1, 5, 0, 15, 3),
    (1, -1, 6, 15, 0, 12),
    (-1, -1, 7, 0, 0, 0),
)


def lagrange_value(node, position, nodes):
    value = 1.0
    for other in range(4):
        if other != node:
            value *= (position - nodes[other]) / (nodes[node] - nodes[other])
    return value


def tables():
    nodes = [-1.0, -1.0 / math.sqrt(5.0), 1.0 / math.sqrt(5.0), 1.0]
    halves = np.zeros((2, 4))
    for i, (low, high) in enumerate(((-1.0, 0.0), (0.0, 1.0))):
        centre, offset = 0.5 * (low + high), 0.5 * (high - low) / math.sqrt(3.0)
        for a in range(4):
            halves[i, a] = (
                0.5
                * (high - low)
                * (
                    lagrange_value(a, centre - offset, nodes)
                    + lagrange_value(a, centre + offset, nodes)
                )
            )
    spread = halves.T @ np.linalg.inv(halves @ halves.T)
    return halves.astype(np.float32).astype(np.float64), spread.astype(np.float32).astype(np.float64)


def split_bf16(table):
    high = table.astype(ml_dtypes.bfloat16)
    low = (table - high.astype(np.float64)).astype(ml_dtypes.bfloat16)
    return high, low


def constant_tables():
    halves, spread = tables()
    cols = np.einsum("ia,jb,yz->iyjzab", halves, halves, np.eye(TY)).reshape(64, 256)
    col_high, col_low = split_bf16(cols)
    along = np.zeros((4, 3, 2))
    along[:, 1, :] = spread
    along[0, 0, :] += spread[3]
    along[3, 2, :] += spread[0]
    along[0] *= 0.5
    along[3] *= 0.5
    along_y = np.zeros((TY, 4, 40))
    for y in range(TY):
        for step in range(3):
            other = y + step - 1
            base = 32 if other < 0 else 34 if other >= TY else 2 * other
            along_y[y, :, base : base + 2] += along[:, step, :]
    update = np.zeros((256, 256))
    update[:, :240] = np.einsum("asi,ybr->yabsir", along, along_y).reshape(256, 240)
    up_high, up_low = split_bf16(update)
    return np.concatenate([up_high, up_low, col_high, col_low], 0)


def iota(shape, dim):
    return lax.broadcasted_iota(I32, shape, dim)


def dot(left, right):
    return jnp.dot(left, right, preferred_element_type=F32)


def dot_nt(left, right):
    return lax.dot_general(left, right, (((1,), (1,)), ((), ())), preferred_element_type=F32)


class Peers:
    def __init__(self, gx, gy):
        self.x, self.y = lax.div(gx, 4), lax.rem(gx, 4)
        self.z, self.core = lax.div(gy, 2), lax.rem(gy, 2)
        self.xs = [lax.rem(self.x + a, 4) * 4 for a in range(4)]
        self.zs = [lax.rem(self.z + d, 4) * 2 for d in range(4)]
        self.cores = [self.core, 1 - self.core]

    def block(self, b, with_self=False):
        ys = [lax.rem(self.y + b + a, 4) for a in range(4)]
        back_b = lax.rem(4 - b, 4) if not isinstance(b, int) else -b % 4
        found = []
        for d in range(4):
            for a in range(4):
                for c in range(2):
                    if isinstance(b, int) and b == d == a == c == 0 and not with_self:
                        continue
                    tgx = self.xs[a] + ys[a]
                    tgy = self.zs[(d + a) % 4] + self.cores[c]
                    inner = d * 8 + a * 2 + c
                    back = -d % 4 * 8 + -a % 4 * 2 + c
                    found.append((tgx, tgy, b * 32 + inner, back_b * 32 + back))
        return found

    def position(self, source):
        a = ((source >> 5) - self.x) & 3
        b = (((source >> 3) & 3) - self.y - a) & 3
        d = (((source >> 1) & 3) - self.z - a) & 3
        c = ((source & 1) - self.core) & 1
        return b * 32 + d * 8 + a * 2 + c


def combine_kernel(cell_ref, state_hbm, stiff_hbm, out_ref, st, xs, w, stiff_sem, state_sem):
    stiff_copy = pltpu.make_async_copy(stiff_hbm, xs, stiff_sem)
    stiff_copy.start()
    loads = []
    for part in range(8):
        rows = pl.ds(part * 512, 512)
        copy = pltpu.make_async_copy(state_hbm.at[:, rows], st.at[:, rows], state_sem.at[part])
        copy.start()
        loads.append(copy)
    stiff_copy.wait()
    flipped = xs[...].T.astype(BF16)
    row_i, col_i = iota((256, 256), 0), iota((256, 256), 1)
    same_m = (row_i & 15) == (col_i & 15)
    diagonal = (row_i & 15) == (col_i >> 4)
    for n in range(16):
        pick = jnp.where(same_m & ((row_i >> 4) == n), 1.0, 0.0).astype(BF16)
        block = jnp.where(diagonal, dot(flipped, pick), 0.0)
        for u in range(2):
            w[u, pl.ds(n, 256, stride=16), :] = block[:, u * 128 : (u + 1) * 128]

    def step(g, carry):
        rows = pl.ds(pl.multiple_of(g * 256, 256), 256)
        state = jnp.concatenate([st[f, rows, :] for f in range(4)], axis=1)
        oper = jnp.concatenate([w[0, rows, :], w[1, rows, :]], axis=1).astype(BF16)
        state = state + dot(oper, state.astype(BF16))
        for e in range(16):
            cell = cell_ref[g * 16 + e]
            tile = ((cell >> 7) & 15) * 16 + (cell & 15)
            target = pl.ds(pl.multiple_of(tile * 16, 16), 16)
            for f in range(4):
                out_ref[f, target, :] = state[e * 16 : e * 16 + 16, f * 128 : f * 128 + 128]
        return carry

    for part in range(8):
        loads[part].wait()
        lax.fori_loop(part * 2, part * 2 + 2, step, 0)


def exchange_kernel(
    st, cell_ref, gcol_ref, inv, table_ref,
    dyn,
    halo, wv, wq, mid, req, qrow, crow,
    sel, sel_t, place, place_t,
    dyn_high, dyn_low, cols, outb, incb, backb, rcvb, flat, tend, grid, gridb,
    sx, sy, sc, rx, ry, rc,
    tx, ty, tc, ux, uy, uc,
    wsend, wrecv, vsend, vrecv, loc_sem,
    fsend, frecv, bsend, brecv, hsend, hrecv, gsend, grecv,
):
    gx, gy = lax.axis_index("gx"), lax.axis_index("gy")
    peers = Peers(gx, gy)
    barrier = pltpu.get_barrier_semaphore()

    def other_x(k):
        return lax.rem(gx + k, NX)

    def other_y(k):
        return lax.rem(gy + k, NY)

    for dgx, dgy, _, _, _, _ in CORNERS:
        pl.semaphore_signal(
            barrier, inc=1, device_id=(other_x(NX + dgx), other_y(NY + dgy)), device_id_type=MESH
        )

    def greet_x(k, carry):
        pl.semaphore_signal(barrier, inc=1, device_id=(other_x(k), gy), device_id_type=MESH)
        return carry

    def greet_y(k, carry):
        pl.semaphore_signal(barrier, inc=1, device_id=(gx, other_y(k)), device_id_type=MESH)
        return carry

    lax.fori_loop(1, NX, greet_x, 0)
    lax.fori_loop(1, NY, greet_y, 0)


    lane = iota((128, 128), 1)
    sub = iota((128, 128), 0)
    eye = lane == sub

    def to_col(row):
        return jnp.sum(jnp.where(eye, jnp.broadcast_to(row, (128, 128)), 0.0), axis=1, keepdims=True)

    def to_row(col):
        return jnp.sum(jnp.where(eye, jnp.broadcast_to(col, (128, 128)), 0.0), axis=0, keepdims=True)

    upper = jnp.where(sub < lane, 1.0, 0.0).astype(BF16)
    seen = jnp.zeros((128, 1), F32)
    want_high = jnp.zeros((128, 128), F32)
    want_low = jnp.zeros((128, 128), F32)
    for block in range(8):
        named = gcol_ref[block : block + 1, :]
        source, local = named >> 10, named & 1023
        hit = jnp.broadcast_to(source, (128, 128)) == sub
        onehot = jnp.where(hit, 1.0, 0.0)
        before = dot(onehot.astype(BF16), upper) + seen
        seen = seen + jnp.sum(onehot, axis=1, keepdims=True)
        rank = jnp.sum(jnp.where(hit, before, 0.0), axis=0, keepdims=True)
        qrow[block : block + 1, :] = peers.position(source).astype(F32) * 8.0 + rank
        ranked = jnp.broadcast_to(rank, (128, 128)) == sub.astype(F32)
        high = (local >> 5).astype(F32)
        low = (local & 31).astype(F32)
        zero = jnp.zeros((128, 128), F32)
        chosen_high = jnp.where(ranked, jnp.broadcast_to(high, (128, 128)), zero).astype(BF16)
        chosen_low = jnp.where(ranked, jnp.broadcast_to(low, (128, 128)), zero).astype(BF16)
        onehot = onehot.astype(BF16)
        want_high = want_high + dot_nt(onehot, chosen_high)
        want_low = want_low + dot_nt(onehot, chosen_low)
    wv[...] = want_high * 32.0 + want_low

    def row_out(s, carry):
        for y in range(NY):
            wq[s, y] = wv[pl.ds(s * NY + y, 1), :]
        return carry

    lax.fori_loop(0, NX, row_out, 0)
    pl.semaphore_wait(barrier, NX + NY - 2 + len(CORNERS))

    def ask_x(k, carry):
        pltpu.make_async_remote_copy(
            wq.at[other_x(k)], mid.at[gx], wsend, wrecv,
            device_id=(other_x(k), gy), device_id_type=MESH,
        ).start()
        return carry

    lax.fori_loop(1, NX, ask_x, 0)
    own_x = pltpu.make_async_copy(wq.at[gx], mid.at[gx], loc_sem.at[0])
    own_x.start()

    others_x = mid.at[pl.ds(0, NX - 1)]
    others_y = req.at[:, pl.ds(0, NY - 1)]

    def ask_y(k, carry):
        pltpu.make_async_remote_copy(
            mid.at[:, other_y(k)], req.at[:, gy], vsend, vrecv,
            device_id=(gx, other_y(k)), device_id_type=MESH,
        ).start()
        return carry

    def copy_to(src, dst, send, recv, dgx, dgy):
        return pltpu.make_async_remote_copy(
            src, dst, send, recv,
            device_id=((gx + dgx + NX) % NX, (gy + dgy + NY) % NY),
            device_id_type=MESH,
        )

    def send_halo(h):
        for f in range(2):
            field = 2 * h + f

            for k in range(16):
                part = pl.ds(k * 4, 4)
                sx[h, 0, f, part, :] = st[field, pl.ds((15 * 16 + k) * 16 + 12, 4), :]
                sx[h, 1, f, part, :] = st[field, pl.ds(k * 16, 4), :]
                sy[h, 0, f, part, :] = st[field, pl.ds((k * 16 + 15) * 16 + 3, 4, stride=4), :]
                sy[h, 1, f, part, :] = st[field, pl.ds(k * 256, 4, stride=4), :]
            for at, (_, _, _, x, y, n) in enumerate(CORNERS):
                sc[h, at, f : f + 1, :] = st[field, pl.ds((x * 16 + y) * 16 + n, 1), :]
        copies = [
            copy_to(sx.at[h, 0], rx.at[h, 0], hsend.at[h, 0], hrecv.at[h, 0], 1, 0),
            copy_to(sx.at[h, 1], rx.at[h, 1], hsend.at[h, 1], hrecv.at[h, 1], -1, 0),
            copy_to(sy.at[h, 0], ry.at[h, 0], hsend.at[h, 2], hrecv.at[h, 2], 0, 1),
            copy_to(sy.at[h, 1], ry.at[h, 1], hsend.at[h, 3], hrecv.at[h, 3], 0, -1),
        ]
        for at, (dgx, dgy, to, _, _, _) in enumerate(CORNERS):
            copies.append(
                copy_to(sc.at[h, at], rc.at[h, at], hsend.at[h, to], hrecv.at[h, to], dgx, dgy)
            )
        for copy in copies:
            copy.start()
        return copies

    def take_halo(h, copies):
        for copy in copies:
            copy.wait_recv()
        for f in range(2):
            field = 2 * h + f
            for k in range(16):
                part = pl.ds(k * 4, 4)
                halo[field, pl.ds((WEST + 1 + k) * 16 + 12, 4), :] = rx[h, 0, f, part, :]
                halo[field, pl.ds((EAST + 1 + k) * 16, 4), :] = rx[h, 1, f, part, :]
                halo[field, pl.ds((SOUTH + k) * 16 + 3, 4, stride=4), :] = ry[h, 0, f, part, :]
                halo[field, pl.ds((NORTH + k) * 16, 4, stride=4), :] = ry[h, 1, f, part, :]
            halo[field, pl.ds(WEST * 16 + 15, 1), :] = rc[h, 0, f : f + 1, :]
            halo[field, pl.ds(EAST * 16 + 3, 1), :] = rc[h, 1, f : f + 1, :]
            halo[field, pl.ds((WEST + 17) * 16 + 12, 1), :] = rc[h, 2, f : f + 1, :]
            halo[field, pl.ds((EAST + 17) * 16, 1), :] = rc[h, 3, f : f + 1, :]

    s8 = iota((8, 128), 0)
    b_at = s8 & 3
    is_b0, is_b3, first_a = b_at == 0, b_at == 3, s8 < 4
    b_scale = jnp.where(is_b0 | is_b3, 0.5, 1.0)
    scale0 = b_scale * jnp.where(first_a, 0.5, 1.0)
    scale1 = b_scale * jnp.where(first_a, 1.0, 0.5)

    def dynamics(h):
        def column(x, carry):
            fixed = isinstance(x, int)

            def rows(x, y, v):
                inside = 0 <= y < TY
                if fixed and x == -1:
                    return halo, (WEST + y + 1) * 16 + v * 8
                if fixed and x == TX:
                    return halo, (EAST + y + 1) * 16 + v * 8
                if not inside:
                    return halo, ((SOUTH if y < 0 else NORTH) + x) * 16 + v * 8
                return st, x * 256 + y * 16 + v * 8

            def load(field, x, y, v):
                ref, at = rows(x, y, v)
                return ref[field, pl.ds(at if fixed else pl.multiple_of(at, 8), 8), :]

            def along_x(y):
                found = []
                for f in range(2):
                    field = 2 * h + f
                    own0, own1 = load(field, x, y, 0), load(field, x, y, 1)
                    before, after = load(field, x - 1, y, 1), load(field, x + 1, y, 0)
                    found.append(own0 + jnp.where(first_a, pltpu.roll(before, 4, 0), 0.0))
                    found.append(own1 + jnp.where(first_a, 0.0, pltpu.roll(after, 4, 0)))
                return found

            south, here = along_x(-1), along_x(0)
            for y in range(TY):
                north = along_x(y + 1)
                for f in range(2):
                    parts = []
                    for v, scale in ((2 * f, scale0), (2 * f + 1, scale1)):
                        edge = jnp.where(is_b0, pltpu.roll(south[v], 5, 0), 0.0)
                        edge = jnp.where(is_b3, pltpu.roll(north[v], 3, 0), edge)
                        parts.append((here[v] + edge) * scale)
                    total = jnp.concatenate(parts, axis=0)
                    at = x * 256 + y * 16
                    dyn[2 * h + f, pl.ds(at if fixed else pl.multiple_of(at, 16), 16), :] = total
                    high = total.astype(BF16)
                    dyn_high[y * 16 : y * 16 + 16, f * 128 : f * 128 + 128] = high
                    low = (total - high.astype(F32)).astype(BF16)
                    dyn_low[y * 16 : y * 16 + 16, f * 128 : f * 128 + 128] = low
                south, here = here, north
            main = dot(table_ref[512:640, :], dyn_high[...])
            rest = dot(table_ref[512:576, :], dyn_low[...])
            total = main[0:64] + main[64:128] + rest
            cols[pl.ds(x * 64 if fixed else pl.multiple_of(x * 64, 64), 64), :] = total.astype(BF16)
            return carry

        column(0, 0)
        lax.fori_loop(1, TX - 1, column, 0)
        column(TX - 1, 0)

    wide = iota((128, 1024), 1)

    def selections():
        k_mask = iota((128, 128), 1) == (iota((128, 128), 0) & 7)

        def build(b, carry):
            found = peers.block(b, with_self=True)
            for part in range(2):
                asked = [
                    jnp.broadcast_to(req[tgx, tgy], (8, 128))
                    for tgx, tgy, _, _ in found[part * 16 : part * 16 + 16]
                ]
                asked = jnp.where(k_mask, jnp.concatenate(asked, axis=0), 0.0)
                asked = jnp.sum(asked, axis=1, keepdims=True).astype(I32)
                slot_at, piece = asked >> 2, asked & 3
                tile = jnp.zeros((128, 128), F32)
                for u in range(2):
                    cell = cell_ref[u : u + 1, :]
                    names = (((cell >> 7) & 15) * 16 + (cell & 15)).astype(F32)
                    names = jnp.broadcast_to(names, (128, 128))
                    tile = tile + jnp.where(slot_at == lane + 128 * u, names, 0.0)
                tile = jnp.sum(tile, axis=1, keepdims=True).astype(I32)
                at = (tile >> 4) * 64 + (piece >> 1) * 32 + (tile & 15) * 2 + (piece & 1)
                block = b * 2 + part
                rows = pl.ds(pl.multiple_of(block * 128, 128), 128)
                sel[rows, :] = jnp.where(wide == at, 1.0, 0.0).astype(BF16)
                crow[pl.ds(block, 1), :] = to_row(at.astype(F32))
            return carry

        lax.fori_loop(0, 4, build, 0)

    def transposed(row_ref, out_ref):
        def build(block, carry):
            rows = pl.ds(pl.multiple_of(block * 128, 128), 128)
            want = (sub + block * 128).astype(F32)
            for u in range(8):
                names = jnp.broadcast_to(row_ref[u : u + 1, :], (128, 128))
                out_ref[rows, u * 128 : (u + 1) * 128] = jnp.where(names == want, 1.0, 0.0).astype(BF16)
            return carry

        lax.fori_loop(0, 8, build, 0)

    def placing():
        def build(block, carry):
            rows = pl.ds(pl.multiple_of(block * 128, 128), 128)
            at = to_col(qrow[pl.ds(block, 1), :]).astype(I32)
            place[rows, :] = jnp.where(wide == at, 1.0, 0.0).astype(BF16)
            return carry

        lax.fori_loop(0, 8, build, 0)

    def permute_and_send(matrix, source, src, dst, h, send, recv, loc):
        def step(b):
            rows = pl.ds(pl.multiple_of(b * 256, 256), 256)
            moved = dot(matrix[rows, :], source[...])
            src[h, pl.ds(b * 32, 32)] = moved.reshape(32, 8, 256).astype(BF16)
            for tgx, tgy, at, back in peers.block(b):
                pltpu.make_async_remote_copy(
                    src.at[h, at], dst.at[h, back], send.at[h], recv.at[h],
                    device_id=(tgx, tgy), device_id_type=MESH,
                ).start()

        def loop_step(b, carry):
            step(b)
            return carry

        step(0)
        own = pltpu.make_async_copy(src.at[h, 0], dst.at[h, 0], loc_sem.at[loc])
        own.start()
        lax.fori_loop(1, 4, loop_step, 0)
        return own

    def wait_all(ref, h, sem):
        block = ref.at[h, pl.ds(0, ND - 1)]
        pltpu.make_async_copy(block, block, sem.at[h]).wait()

    def flatten(src, h):
        def step(block, carry):
            part = src[h, pl.ds(block * 16, 16)].astype(F32).reshape(128, 256)
            flat[pl.ds(pl.multiple_of(block * 128, 128), 128), :] = part.astype(BF16)
            return carry

        lax.fori_loop(0, 8, step, 0)

    halo_copies, forward, back_copies = [None] * NH, [None] * NH, [None] * NH
    for h in range(NH):
        halo_copies[h] = send_halo(h)
    transposed(qrow, place_t)
    placing()
    grid[...] = jnp.zeros_like(grid)
    own_x.wait()
    pltpu.make_async_copy(others_x, others_x, wrecv).wait()
    lax.fori_loop(1, NY, ask_y, 0)
    own_y = pltpu.make_async_copy(mid.at[:, gy], req.at[:, gy], loc_sem.at[0])
    own_y.start()
    for h in range(NH):
        take_halo(h, halo_copies[h])
        dynamics(h)
        if h == 0:
            own_y.wait()
            pltpu.make_async_copy(others_y, others_y, vrecv).wait()
            selections()
        forward[h] = permute_and_send(sel, cols, outb, incb, h, fsend, frecv, 1 + h)

    transposed(crow, sel_t)

    def physics(h):
        def step(block, carry):
            rows = pl.ds(pl.multiple_of(block * 256, 256), 256)
            moved = dot(place[rows, :], flat[...])
            for g in range(16):
                part = moved[g * 16 : (g + 1) * 16, :]
                stacked = jnp.concatenate([part[:, :128], part[:, 128:]], axis=0)
                smooth = dot_nt(stacked.astype(BF16), inv[block * 16 + g])
                change = smooth - stacked
                change = jnp.concatenate([change[:16], change[16:]], axis=1)
                tend[pl.ds(pl.multiple_of(block * 256 + g * 16, 16), 16), :] = change.astype(BF16)
            return carry

        lax.fori_loop(0, 4, step, 0)

    for h in range(NH):
        forward[h].wait()
        wait_all(incb, h, frecv)
        flatten(incb, h)
        physics(h)
        back_copies[h] = permute_and_send(place_t, tend, backb, rcvb, h, bsend, brecv, 3 + h)

    ring_copies = []

    def finish(h):
        def add(x, carry):
            rows = pl.ds(pl.multiple_of(x * 256, 256), 256)
            near = gridb[pl.ds(pl.multiple_of(x * RX, 16), 256), :]
            update = dot(table_ref[0:512, :], near)
            update = update[:256] + update[256:]
            for f in range(2):
                field = 2 * h + f
                dyn[field, rows, :] = dyn[field, rows, :] + update[:, f * LEV : (f + 1) * LEV]
            return carry

        lax.fori_loop(0, TX, add, 0)

    for h in range(NH):
        back_copies[h].wait()
        wait_all(rcvb, h, brecv)
        flatten(rcvb, h)

        def ungroup(block, carry):
            rows = pl.ds(pl.multiple_of(block * 256, 256), 256)
            moved = dot(sel_t[rows, :], flat[...])
            for x in range(4):
                for i in range(2):
                    base = pl.multiple_of((block * 4 + x + 1) * RX + i * 40, 8)
                    piece = moved[x * 64 + i * 32 : x * 64 + i * 32 + 32, :]
                    for u in range(2):
                        grid[h, u, pl.ds(base, 32), :] = piece[:, u * 128 : (u + 1) * 128]
            return carry

        lax.fori_loop(0, 4, ungroup, 0)
        for u in range(2):
            for i in range(2):
                tx[h, 0, u, i * 32 : i * 32 + 32, :] = grid[h, u, 16 * RX + i * 40 : 16 * RX + i * 40 + 32, :]
                tx[h, 1, u, i * 32 : i * 32 + 32, :] = grid[h, u, RX + i * 40 : RX + i * 40 + 32, :]
            for j in range(2):
                ty[h, 0, u, j * 32 : j * 32 + 32, :] = grid[h, u, pl.ds(RX + 30 + j, 32, stride=40), :]
                ty[h, 1, u, j * 32 : j * 32 + 32, :] = grid[h, u, pl.ds(RX + j, 32, stride=40), :]
            for at, (_, _, _, x, y, _) in enumerate(CORNERS):
                for i in range(2):
                    base = (x + 1) * RX + i * 40 + 2 * y
                    tc[h, at, u * 4 + i * 2 : u * 4 + i * 2 + 2, :] = grid[h, u, base : base + 2, :]
        copies = [
            copy_to(tx.at[h, 0], ux.at[h, 0], gsend.at[h, 0], grecv.at[h, 0], 1, 0),
            copy_to(tx.at[h, 1], ux.at[h, 1], gsend.at[h, 1], grecv.at[h, 1], -1, 0),
            copy_to(ty.at[h, 0], uy.at[h, 0], gsend.at[h, 2], grecv.at[h, 2], 0, 1),
            copy_to(ty.at[h, 1], uy.at[h, 1], gsend.at[h, 3], grecv.at[h, 3], 0, -1),
        ]
        for at, (dgx, dgy, to, _, _, _) in enumerate(CORNERS):
            copies.append(
                copy_to(tc.at[h, at], uc.at[h, at], gsend.at[h, to], grecv.at[h, to], dgx, dgy)
            )
        for copy in copies:
            copy.start()
        ring_copies.append(copies)
        for copy in copies:
            copy.wait_recv()
        for u in range(2):
            for i in range(2):
                part = slice(i * 32, i * 32 + 32)
                grid[h, u, i * 40 : i * 40 + 32, :] = ux[h, 0, u, part, :]
                grid[h, u, 17 * RX + i * 40 : 17 * RX + i * 40 + 32, :] = ux[h, 1, u, part, :]
            for j in range(2):
                part = slice(j * 32, j * 32 + 32)
                grid[h, u, pl.ds(RX + 32 + j, 32, stride=40), :] = uy[h, 0, u, part, :]
                grid[h, u, pl.ds(RX + 34 + j, 32, stride=40), :] = uy[h, 1, u, part, :]
            for at, (big_x, base) in enumerate(((0, 32), (17, 32), (0, 34), (17, 34))):
                for i in range(2):
                    to = big_x * RX + i * 40 + base
                    grid[h, u, to : to + 2, :] = uc[h, at, u * 4 + i * 2 : u * 4 + i * 2 + 2, :]
            gridb[:, u * 128 : (u + 1) * 128] = grid[h, u].astype(BF16)
        finish(h)


    pltpu.make_async_copy(others_x, others_x, wsend).wait()
    pltpu.make_async_copy(others_y, others_y, vsend).wait()
    for h in range(NH):
        wait_all(outb, h, fsend)
        wait_all(backb, h, bsend)
        for copy in halo_copies[h] + ring_copies[h]:
            copy.wait_send()


def place_kernel(cell_ref, total, out_hbm, sem):
    def step(s, carry):
        for k in range(8):
            at = s * 8 + k
            cell = cell_ref[at]
            tile = ((cell >> 7) & 15) * 16 + (cell & 15)
            pltpu.make_async_copy(total.at[:, tile], out_hbm.at[:, at], sem).start()
        return carry

    lax.fori_loop(0, NE // 8, step, 0)
    pltpu.make_async_copy(total, out_hbm, sem).wait()


def any_spec():
    return pl.BlockSpec(memory_space=pl.ANY)


def in_hbm(array):
    return pltpu.with_memory_space_constraint(array, pltpu.HBM)


def vmem_spec():
    return pl.BlockSpec(memory_space=pltpu.VMEM)


def smem_spec():
    return pl.BlockSpec(memory_space=pltpu.SMEM)


def per_device(table, state_in, stiffness, elem_cell, group_column, group_inverse):
    state = state_in.reshape(4, NE * 16, LEV)
    dma = pltpu.SemaphoreType.DMA
    vmem = pltpu.VMEM
    whole = jax.ShapeDtypeStruct((4, NE * 16, LEV), F32)
    combined = pl.pallas_call(
        combine_kernel,
        out_shape=whole,
        in_specs=[smem_spec(), any_spec(), any_spec()],
        out_specs=vmem_spec(),
        scratch_shapes=[
            vmem((4, NE * 16, LEV), F32),
            vmem((256, 256), F32),
            vmem((2, NE * 16, LEV), F32),
            dma,
            dma((8,)),
        ],
        compiler_params=pltpu.CompilerParams(vmem_limit_bytes=30 << 20),
        name="combine",
    )(elem_cell, in_hbm(state), in_hbm(stiffness.reshape(256, NE)))
    scratch = [
        vmem((4, NHALO * 16, LEV), F32),
        vmem((128, 128), F32),
        vmem((NX, NY, 1, 128), F32),
        vmem((NX, NY, 1, 128), F32),
        vmem((NX, NY, 1, 128), F32),
        vmem((8, 128), F32),
        vmem((8, 128), F32),
        vmem((NC, NC), BF16),
        vmem((NC, NC), BF16),
        vmem((NC, NC), BF16),
        vmem((NC, NC), BF16),
        vmem((256, 256), BF16),
        vmem((256, 256), BF16),
        vmem((NC, 256), BF16),
        vmem((NH, ND, 8, 256), BF16),
        vmem((NH, ND, 8, 256), BF16),
        vmem((NH, ND, 8, 256), BF16),
        vmem((NH, ND, 8, 256), BF16),
        vmem((NC, 256), BF16),
        vmem((NC, 256), BF16),
        vmem((NH, 2, RROWS, LEV), F32),
        vmem((RROWS, 256), BF16),
        vmem((NH, 2, 2, 64, LEV), F32),
        vmem((NH, 2, 2, 64, LEV), F32),
        vmem((NH, 4, 8, LEV), F32),
        vmem((NH, 2, 2, 64, LEV), F32),
        vmem((NH, 2, 2, 64, LEV), F32),
        vmem((NH, 4, 8, LEV), F32),
        vmem((NH, 2, 2, 64, LEV), F32),
        vmem((NH, 2, 2, 64, LEV), F32),
        vmem((NH, 4, 8, LEV), F32),
        vmem((NH, 2, 2, 64, LEV), F32),
        vmem((NH, 2, 2, 64, LEV), F32),
        vmem((NH, 4, 8, LEV), F32),
        dma, dma, dma, dma, dma((5,)),
        dma((NH,)), dma((NH,)), dma((NH,)), dma((NH,)),
        dma((NH, 8)), dma((NH, 8)), dma((NH, 8)), dma((NH, 8)),
    ]
    total = pl.pallas_call(
        exchange_kernel,
        out_shape=whole,
        in_specs=[vmem_spec()] * 5,
        out_specs=vmem_spec(),
        scratch_shapes=scratch,
        compiler_params=pltpu.CompilerParams(
            collective_id=0, has_side_effects=True, vmem_limit_bytes=28 << 20
        ),
        name="exchange",
    )(combined, elem_cell.reshape(2, 128), group_column.reshape(8, 128), group_inverse, table)
    return pl.pallas_call(
        place_kernel,
        out_shape=jax.ShapeDtypeStruct((4, NE, 16, LEV), F32),
        in_specs=[smem_spec(), vmem_spec()],
        out_specs=any_spec(),
        scratch_shapes=[dma],
        compiler_params=pltpu.CompilerParams(vmem_limit_bytes=4 << 20),
        name="place",
    )(elem_cell, total.reshape(4, NE, 16, LEV))


def solution(mesh):
    table = constant_tables()
    placed = (
        P(None, ("gx", "gy"), None, None),
        P(None, None, ("gx", "gy")),
        P(("gx", "gy")),
        P(("gx", "gy")),
        P(("gx", "gy"), None, None),
    )

    def run(*args):
        body = functools.partial(per_device, jnp.asarray(table))
        return jax.shard_map(
            body,
            mesh=mesh,
            in_specs=placed,
            out_specs=P(None, ("gx", "gy"), None, None),
            check_vma=False,
        )(*args)

    return run
```

```python
import functools
import math

import jax
import jax.numpy as jnp
import ml_dtypes
import numpy as np
from jax import lax
from jax.experimental import pallas as pl
from jax.experimental.pallas import tpu as pltpu
from jax.sharding import PartitionSpec as P

F32, BF16, I32 = jnp.float32, jnp.bfloat16, jnp.int32
MESH = pl.DeviceIdType.MESH
NX, NY = 16, 8
ND = NX * NY
TX = TY = 16
NE = TX * TY
NC = 4 * NE
LEV = 128
NH = 2
WEST, EAST, SOUTH, NORTH = 0, 18, 36, 52
NHALO = 68
RX = 80
RROWS = 18 * RX + 16
CORNERS = (
    (1, 1, 4, 15, 15, 15),
    (-1, 1, 5, 0, 15, 3),
    (1, -1, 6, 15, 0, 12),
    (-1, -1, 7, 0, 0, 0),
)


def lagrange_value(node, position, nodes):
    value = 1.0
    for other in range(4):
        if other != node:
            value *= (position - nodes[other]) / (nodes[node] - nodes[other])
    return value


def tables():
    nodes = [-1.0, -1.0 / math.sqrt(5.0), 1.0 / math.sqrt(5.0), 1.0]
    halves = np.zeros((2, 4))
    for i, (low, high) in enumerate(((-1.0, 0.0), (0.0, 1.0))):
        centre, offset = 0.5 * (low + high), 0.5 * (high - low) / math.sqrt(3.0)
        for a in range(4):
            halves[i, a] = (
                0.5
                * (high - low)
                * (
                    lagrange_value(a, centre - offset, nodes)
                    + lagrange_value(a, centre + offset, nodes)
                )
            )
    spread = halves.T @ np.linalg.inv(halves @ halves.T)
    return halves.astype(np.float32).astype(np.float64), spread.astype(np.float32).astype(np.float64)


def split_bf16(table):
    high = table.astype(ml_dtypes.bfloat16)
    low = (table - high.astype(np.float64)).astype(ml_dtypes.bfloat16)
    return high, low


def constant_tables():
    halves, spread = tables()
    cols = np.einsum("ia,jb,yz->iyjzab", halves, halves, np.eye(TY)).reshape(64, 256)
    col_high, col_low = split_bf16(cols)
    along = np.zeros((4, 3, 2))
    along[:, 1, :] = spread
    along[0, 0, :] += spread[3]
    along[3, 2, :] += spread[0]
    along[0] *= 0.5
    along[3] *= 0.5
    along_y = np.zeros((TY, 4, 40))
    for y in range(TY):
        for step in range(3):
            other = y + step - 1
            base = 32 if other < 0 else 34 if other >= TY else 2 * other
            along_y[y, :, base : base + 2] += along[:, step, :]
    update = np.zeros((256, 256))
    update[:, :240] = np.einsum("asi,ybr->yabsir", along, along_y).reshape(256, 240)
    up_high, up_low = split_bf16(update)
    return np.concatenate([up_high, up_low, col_high, col_low], 0)


def iota(shape, dim):
    return lax.broadcasted_iota(I32, shape, dim)


def dot(left, right):
    return jnp.dot(left, right, preferred_element_type=F32)


def dot_nt(left, right):
    return lax.dot_general(left, right, (((1,), (1,)), ((), ())), preferred_element_type=F32)


class Peers:
    def __init__(self, gx, gy):
        self.x, self.y = lax.div(gx, 4), lax.rem(gx, 4)
        self.z, self.core = lax.div(gy, 2), lax.rem(gy, 2)
        self.xs = [lax.rem(self.x + a, 4) * 4 for a in range(4)]
        self.zs = [lax.rem(self.z + d, 4) * 2 for d in range(4)]
        self.cores = [self.core, 1 - self.core]

    def block(self, b, with_self=False):
        ys = [lax.rem(self.y + b + a, 4) for a in range(4)]
        back_b = lax.rem(4 - b, 4) if not isinstance(b, int) else -b % 4
        found = []
        for d in range(4):
            for a in range(4):
                for c in range(2):
                    if isinstance(b, int) and b == d == a == c == 0 and not with_self:
                        continue
                    tgx = self.xs[a] + ys[a]
                    tgy = self.zs[(d + a) % 4] + self.cores[c]
                    inner = d * 8 + a * 2 + c
                    back = -d % 4 * 8 + -a % 4 * 2 + c
                    found.append((tgx, tgy, b * 32 + inner, back_b * 32 + back))
        return found

    def position(self, source):
        a = ((source >> 5) - self.x) & 3
        b = (((source >> 3) & 3) - self.y - a) & 3
        d = (((source >> 1) & 3) - self.z - a) & 3
        c = ((source & 1) - self.core) & 1
        return b * 32 + d * 8 + a * 2 + c


def combine_kernel(cell_ref, state_hbm, stiff_hbm, out_ref, st, xs, w, stiff_sem, state_sem):
    stiff_copy = pltpu.make_async_copy(stiff_hbm, xs, stiff_sem)
    stiff_copy.start()
    loads = []
    for part in range(8):
        rows = pl.ds(part * 512, 512)
        copy = pltpu.make_async_copy(state_hbm.at[:, rows], st.at[:, rows], state_sem.at[part])
        copy.start()
        loads.append(copy)
    stiff_copy.wait()
    flipped = xs[...].T.astype(BF16)
    row_i, col_i = iota((256, 256), 0), iota((256, 256), 1)
    same_m = (row_i & 15) == (col_i & 15)
    diagonal = (row_i & 15) == (col_i >> 4)
    for n in range(16):
        pick = jnp.where(same_m & ((row_i >> 4) == n), 1.0, 0.0).astype(BF16)
        block = jnp.where(diagonal, dot(flipped, pick), 0.0)
        for u in range(2):
            w[u, pl.ds(n, 256, stride=16), :] = block[:, u * 128 : (u + 1) * 128]

    def step(g, carry):
        rows = pl.ds(pl.multiple_of(g * 256, 256), 256)
        state = jnp.concatenate([st[f, rows, :] for f in range(4)], axis=1)
        oper = jnp.concatenate([w[0, rows, :], w[1, rows, :]], axis=1).astype(BF16)
        state = state + dot(oper, state.astype(BF16))
        for e in range(16):
            cell = cell_ref[g * 16 + e]
            tile = ((cell >> 7) & 15) * 16 + (cell & 15)
            target = pl.ds(pl.multiple_of(tile * 16, 16), 16)
            for f in range(4):
                out_ref[f, target, :] = state[e * 16 : e * 16 + 16, f * 128 : f * 128 + 128]
        return carry

    for part in range(8):
        loads[part].wait()
        lax.fori_loop(part * 2, part * 2 + 2, step, 0)


def exchange_kernel(
    st, cell_ref, gcol_ref, inv, table_ref,
    dyn,
    halo, wv, wq, mid, req, qrow, crow,
    sel, sel_t, place, place_t,
    dyn_high, dyn_low, cols, outb, incb, backb, rcvb, flat, tend, grid, gridb,
    sx, sy, sc, rx, ry, rc,
    tx, ty, tc, ux, uy, uc,
    wsend, wrecv, vsend, vrecv, loc_sem,
    fsend, frecv, bsend, brecv, hsend, hrecv, gsend, grecv,
):
    gx, gy = lax.axis_index("gx"), lax.axis_index("gy")
    peers = Peers(gx, gy)
    barrier = pltpu.get_barrier_semaphore()

    def other_x(k):
        return lax.rem(gx + k, NX)

    def other_y(k):
        return lax.rem(gy + k, NY)

    for dgx, dgy, _, _, _, _ in CORNERS:
        pl.semaphore_signal(
            barrier, inc=1, device_id=(other_x(NX + dgx), other_y(NY + dgy)), device_id_type=MESH
        )

    def greet_x(k, carry):
        pl.semaphore_signal(barrier, inc=1, device_id=(other_x(k), gy), device_id_type=MESH)
        return carry

    def greet_y(k, carry):
        pl.semaphore_signal(barrier, inc=1, device_id=(gx, other_y(k)), device_id_type=MESH)
        return carry

    lax.fori_loop(1, NX, greet_x, 0)
    lax.fori_loop(1, NY, greet_y, 0)


    lane = iota((128, 128), 1)
    sub = iota((128, 128), 0)
    eye = lane == sub

    def to_col(row):
        return jnp.sum(jnp.where(eye, jnp.broadcast_to(row, (128, 128)), 0.0), axis=1, keepdims=True)

    def to_row(col):
        return jnp.sum(jnp.where(eye, jnp.broadcast_to(col, (128, 128)), 0.0), axis=0, keepdims=True)

    upper = jnp.where(sub < lane, 1.0, 0.0).astype(BF16)
    seen = jnp.zeros((128, 1), F32)
    want_high = jnp.zeros((128, 128), F32)
    want_low = jnp.zeros((128, 128), F32)
    for block in range(8):
        named = gcol_ref[block : block + 1, :]
        source, local = named >> 10, named & 1023
        hit = jnp.broadcast_to(source, (128, 128)) == sub
        onehot = jnp.where(hit, 1.0, 0.0)
        before = dot(onehot.astype(BF16), upper) + seen
        seen = seen + jnp.sum(onehot, axis=1, keepdims=True)
        rank = jnp.sum(jnp.where(hit, before, 0.0), axis=0, keepdims=True)
        qrow[block : block + 1, :] = peers.position(source).astype(F32) * 8.0 + rank
        ranked = jnp.broadcast_to(rank, (128, 128)) == sub.astype(F32)
        high = (local >> 5).astype(F32)
        low = (local & 31).astype(F32)
        zero = jnp.zeros((128, 128), F32)
        chosen_high = jnp.where(ranked, jnp.broadcast_to(high, (128, 128)), zero).astype(BF16)
        chosen_low = jnp.where(ranked, jnp.broadcast_to(low, (128, 128)), zero).astype(BF16)
        onehot = onehot.astype(BF16)
        want_high = want_high + dot_nt(onehot, chosen_high)
        want_low = want_low + dot_nt(onehot, chosen_low)
    wv[...] = want_high * 32.0 + want_low

    def row_out(s, carry):
        for y in range(NY):
            wq[s, y] = wv[pl.ds(s * NY + y, 1), :]
        return carry

    lax.fori_loop(0, NX, row_out, 0)
    pl.semaphore_wait(barrier, NX + NY - 2 + len(CORNERS))

    def ask_x(k, carry):
        pltpu.make_async_remote_copy(
            wq.at[other_x(k)], mid.at[gx], wsend, wrecv,
            device_id=(other_x(k), gy), device_id_type=MESH,
        ).start()
        return carry

    lax.fori_loop(1, NX, ask_x, 0)
    own_x = pltpu.make_async_copy(wq.at[gx], mid.at[gx], loc_sem.at[0])
    own_x.start()

    others_x = mid.at[pl.ds(0, NX - 1)]
    others_y = req.at[:, pl.ds(0, NY - 1)]

    def ask_y(k, carry):
        pltpu.make_async_remote_copy(
            mid.at[:, other_y(k)], req.at[:, gy], vsend, vrecv,
            device_id=(gx, other_y(k)), device_id_type=MESH,
        ).start()
        return carry

    def copy_to(src, dst, send, recv, dgx, dgy):
        return pltpu.make_async_remote_copy(
            src, dst, send, recv,
            device_id=((gx + dgx + NX) % NX, (gy + dgy + NY) % NY),
            device_id_type=MESH,
        )

    def send_halo(h):
        for f in range(2):
            field = 2 * h + f

            for k in range(16):
                part = pl.ds(k * 4, 4)
                sx[h, 0, f, part, :] = st[field, pl.ds((15 * 16 + k) * 16 + 12, 4), :]
                sx[h, 1, f, part, :] = st[field, pl.ds(k * 16, 4), :]
                sy[h, 0, f, part, :] = st[field, pl.ds((k * 16 + 15) * 16 + 3, 4, stride=4), :]
                sy[h, 1, f, part, :] = st[field, pl.ds(k * 256, 4, stride=4), :]
            for at, (_, _, _, x, y, n) in enumerate(CORNERS):
                sc[h, at, f : f + 1, :] = st[field, pl.ds((x * 16 + y) * 16 + n, 1), :]
        copies = [
            copy_to(sx.at[h, 0], rx.at[h, 0], hsend.at[h, 0], hrecv.at[h, 0], 1, 0),
            copy_to(sx.at[h, 1], rx.at[h, 1], hsend.at[h, 1], hrecv.at[h, 1], -1, 0),
            copy_to(sy.at[h, 0], ry.at[h, 0], hsend.at[h, 2], hrecv.at[h, 2], 0, 1),
            copy_to(sy.at[h, 1], ry.at[h, 1], hsend.at[h, 3], hrecv.at[h, 3], 0, -1),
        ]
        for at, (dgx, dgy, to, _, _, _) in enumerate(CORNERS):
            copies.append(
                copy_to(sc.at[h, at], rc.at[h, at], hsend.at[h, to], hrecv.at[h, to], dgx, dgy)
            )
        for copy in copies:
            copy.start()
        return copies

    def take_halo(h, copies):
        for copy in copies:
            copy.wait_recv()
        for f in range(2):
            field = 2 * h + f
            for k in range(16):
                part = pl.ds(k * 4, 4)
                halo[field, pl.ds((WEST + 1 + k) * 16 + 12, 4), :] = rx[h, 0, f, part, :]
                halo[field, pl.ds((EAST + 1 + k) * 16, 4), :] = rx[h, 1, f, part, :]
                halo[field, pl.ds((SOUTH + k) * 16 + 3, 4, stride=4), :] = ry[h, 0, f, part, :]
                halo[field, pl.ds((NORTH + k) * 16, 4, stride=4), :] = ry[h, 1, f, part, :]
            halo[field, pl.ds(WEST * 16 + 15, 1), :] = rc[h, 0, f : f + 1, :]
            halo[field, pl.ds(EAST * 16 + 3, 1), :] = rc[h, 1, f : f + 1, :]
            halo[field, pl.ds((WEST + 17) * 16 + 12, 1), :] = rc[h, 2, f : f + 1, :]
            halo[field, pl.ds((EAST + 17) * 16, 1), :] = rc[h, 3, f : f + 1, :]

    s8 = iota((8, 128), 0)
    b_at = s8 & 3
    is_b0, is_b3, first_a = b_at == 0, b_at == 3, s8 < 4
    b_scale = jnp.where(is_b0 | is_b3, 0.5, 1.0)
    scale0 = b_scale * jnp.where(first_a, 0.5, 1.0)
    scale1 = b_scale * jnp.where(first_a, 1.0, 0.5)

    def dynamics(h):
        def column(x, carry):
            fixed = isinstance(x, int)

            def rows(x, y, v):
                inside = 0 <= y < TY
                if fixed and x == -1:
                    return halo, (WEST + y + 1) * 16 + v * 8
                if fixed and x == TX:
                    return halo, (EAST + y + 1) * 16 + v * 8
                if not inside:
                    return halo, ((SOUTH if y < 0 else NORTH) + x) * 16 + v * 8
                return st, x * 256 + y * 16 + v * 8

            def load(field, x, y, v):
                ref, at = rows(x, y, v)
                return ref[field, pl.ds(at if fixed else pl.multiple_of(at, 8), 8), :]

            def along_x(y):
                found = []
                for f in range(2):
                    field = 2 * h + f
                    own0, own1 = load(field, x, y, 0), load(field, x, y, 1)
                    before, after = load(field, x - 1, y, 1), load(field, x + 1, y, 0)
                    found.append(own0 + jnp.where(first_a, pltpu.roll(before, 4, 0), 0.0))
                    found.append(own1 + jnp.where(first_a, 0.0, pltpu.roll(after, 4, 0)))
                return found

            south, here = along_x(-1), along_x(0)
            for y in range(TY):
                north = along_x(y + 1)
                for f in range(2):
                    parts = []
                    for v, scale in ((2 * f, scale0), (2 * f + 1, scale1)):
                        edge = jnp.where(is_b0, pltpu.roll(south[v], 5, 0), 0.0)
                        edge = jnp.where(is_b3, pltpu.roll(north[v], 3, 0), edge)
                        parts.append((here[v] + edge) * scale)
                    total = jnp.concatenate(parts, axis=0)
                    at = x * 256 + y * 16
                    dyn[2 * h + f, pl.ds(at if fixed else pl.multiple_of(at, 16), 16), :] = total
                    high = total.astype(BF16)
                    dyn_high[y * 16 : y * 16 + 16, f * 128 : f * 128 + 128] = high
                    low = (total - high.astype(F32)).astype(BF16)
                    dyn_low[y * 16 : y * 16 + 16, f * 128 : f * 128 + 128] = low
                south, here = here, north
            main = dot(table_ref[512:640, :], dyn_high[...])
            rest = dot(table_ref[512:576, :], dyn_low[...])
            total = main[0:64] + main[64:128] + rest
            cols[pl.ds(x * 64 if fixed else pl.multiple_of(x * 64, 64), 64), :] = total.astype(BF16)
            return carry

        column(0, 0)
        lax.fori_loop(1, TX - 1, column, 0)
        column(TX - 1, 0)

    wide = iota((128, 1024), 1)

    def selections():
        k_mask = iota((128, 128), 1) == (iota((128, 128), 0) & 7)

        def build(b, carry):
            found = peers.block(b, with_self=True)
            for part in range(2):
                asked = [
                    jnp.broadcast_to(req[tgx, tgy], (8, 128))
                    for tgx, tgy, _, _ in found[part * 16 : part * 16 + 16]
                ]
                asked = jnp.where(k_mask, jnp.concatenate(asked, axis=0), 0.0)
                asked = jnp.sum(asked, axis=1, keepdims=True).astype(I32)
                slot_at, piece = asked >> 2, asked & 3
                tile = jnp.zeros((128, 128), F32)
                for u in range(2):
                    cell = cell_ref[u : u + 1, :]
                    names = (((cell >> 7) & 15) * 16 + (cell & 15)).astype(F32)
                    names = jnp.broadcast_to(names, (128, 128))
                    tile = tile + jnp.where(slot_at == lane + 128 * u, names, 0.0)
                tile = jnp.sum(tile, axis=1, keepdims=True).astype(I32)
                at = (tile >> 4) * 64 + (piece >> 1) * 32 + (tile & 15) * 2 + (piece & 1)
                block = b * 2 + part
                rows = pl.ds(pl.multiple_of(block * 128, 128), 128)
                sel[rows, :] = jnp.where(wide == at, 1.0, 0.0).astype(BF16)
                crow[pl.ds(block, 1), :] = to_row(at.astype(F32))
            return carry

        lax.fori_loop(0, 4, build, 0)

    def transposed(row_ref, out_ref):
        def build(block, carry):
            rows = pl.ds(pl.multiple_of(block * 128, 128), 128)
            want = (sub + block * 128).astype(F32)
            for u in range(8):
                names = jnp.broadcast_to(row_ref[u : u + 1, :], (128, 128))
                out_ref[rows, u * 128 : (u + 1) * 128] = jnp.where(names == want, 1.0, 0.0).astype(BF16)
            return carry

        lax.fori_loop(0, 8, build, 0)

    def placing():
        def build(block, carry):
            rows = pl.ds(pl.multiple_of(block * 128, 128), 128)
            at = to_col(qrow[pl.ds(block, 1), :]).astype(I32)
            place[rows, :] = jnp.where(wide == at, 1.0, 0.0).astype(BF16)
            return carry

        lax.fori_loop(0, 8, build, 0)

    def permute_and_send(matrix, source, src, dst, h, send, recv, loc):
        def step(b):
            rows = pl.ds(pl.multiple_of(b * 256, 256), 256)
            moved = dot(matrix[rows, :], source[...])
            src[h, pl.ds(b * 32, 32)] = moved.reshape(32, 8, 256).astype(BF16)
            for tgx, tgy, at, back in peers.block(b):
                pltpu.make_async_remote_copy(
                    src.at[h, at], dst.at[h, back], send.at[h], recv.at[h],
                    device_id=(tgx, tgy), device_id_type=MESH,
                ).start()

        def loop_step(b, carry):
            step(b)
            return carry

        step(0)
        own = pltpu.make_async_copy(src.at[h, 0], dst.at[h, 0], loc_sem.at[loc])
        own.start()
        lax.fori_loop(1, 4, loop_step, 0)
        return own

    def wait_all(ref, h, sem):
        block = ref.at[h, pl.ds(0, ND - 1)]
        pltpu.make_async_copy(block, block, sem.at[h]).wait()

    def flatten(src, h):
        def step(block, carry):
            part = src[h, pl.ds(block * 16, 16)].astype(F32).reshape(128, 256)
            flat[pl.ds(pl.multiple_of(block * 128, 128), 128), :] = part.astype(BF16)
            return carry

        lax.fori_loop(0, 8, step, 0)

    halo_copies, forward, back_copies = [None] * NH, [None] * NH, [None] * NH
    for h in range(NH):
        halo_copies[h] = send_halo(h)
    transposed(qrow, place_t)
    placing()
    grid[...] = jnp.zeros_like(grid)
    own_x.wait()
    pltpu.make_async_copy(others_x, others_x, wrecv).wait()
    lax.fori_loop(1, NY, ask_y, 0)
    own_y = pltpu.make_async_copy(mid.at[:, gy], req.at[:, gy], loc_sem.at[0])
    own_y.start()
    for h in range(NH):
        take_halo(h, halo_copies[h])
        dynamics(h)
        if h == 0:
            own_y.wait()
            pltpu.make_async_copy(others_y, others_y, vrecv).wait()
            selections()
        forward[h] = permute_and_send(sel, cols, outb, incb, h, fsend, frecv, 1 + h)

    transposed(crow, sel_t)

    def physics(h):
        def step(block, carry):
            rows = pl.ds(pl.multiple_of(block * 256, 256), 256)
            moved = dot(place[rows, :], flat[...])
            for g in range(16):
                part = moved[g * 16 : (g + 1) * 16, :]
                stacked = jnp.concatenate([part[:, :128], part[:, 128:]], axis=0)
                smooth = dot_nt(stacked.astype(BF16), inv[block * 16 + g])
                change = smooth - stacked
                change = jnp.concatenate([change[:16], change[16:]], axis=1)
                tend[pl.ds(pl.multiple_of(block * 256 + g * 16, 16), 16), :] = change.astype(BF16)
            return carry

        lax.fori_loop(0, 4, step, 0)

    for h in range(NH):
        forward[h].wait()
        wait_all(incb, h, frecv)
        flatten(incb, h)
        physics(h)
        back_copies[h] = permute_and_send(place_t, tend, backb, rcvb, h, bsend, brecv, 3 + h)

    ring_copies = []

    def finish(h):
        def add(x, carry):
            rows = pl.ds(pl.multiple_of(x * 256, 256), 256)
            near = gridb[pl.ds(pl.multiple_of(x * RX, 16), 256), :]
            update = dot(table_ref[0:512, :], near)
            update = update[:256] + update[256:]
            for f in range(2):
                field = 2 * h + f
                dyn[field, rows, :] = dyn[field, rows, :] + update[:, f * LEV : (f + 1) * LEV]
            return carry

        lax.fori_loop(0, TX, add, 0)

    for h in range(NH):
        back_copies[h].wait()
        wait_all(rcvb, h, brecv)
        flatten(rcvb, h)

        def ungroup(block, carry):
            rows = pl.ds(pl.multiple_of(block * 256, 256), 256)
            moved = dot(sel_t[rows, :], flat[...])
            for x in range(4):
                for i in range(2):
                    base = pl.multiple_of((block * 4 + x + 1) * RX + i * 40, 8)
                    piece = moved[x * 64 + i * 32 : x * 64 + i * 32 + 32, :]
                    for u in range(2):
                        grid[h, u, pl.ds(base, 32), :] = piece[:, u * 128 : (u + 1) * 128]
            return carry

        lax.fori_loop(0, 4, ungroup, 0)
        for u in range(2):
            for i in range(2):
                tx[h, 0, u, i * 32 : i * 32 + 32, :] = grid[h, u, 16 * RX + i * 40 : 16 * RX + i * 40 + 32, :]
                tx[h, 1, u, i * 32 : i * 32 + 32, :] = grid[h, u, RX + i * 40 : RX + i * 40 + 32, :]
            for j in range(2):
                ty[h, 0, u, j * 32 : j * 32 + 32, :] = grid[h, u, pl.ds(RX + 30 + j, 32, stride=40), :]
                ty[h, 1, u, j * 32 : j * 32 + 32, :] = grid[h, u, pl.ds(RX + j, 32, stride=40), :]
            for at, (_, _, _, x, y, _) in enumerate(CORNERS):
                for i in range(2):
                    base = (x + 1) * RX + i * 40 + 2 * y
                    tc[h, at, u * 4 + i * 2 : u * 4 + i * 2 + 2, :] = grid[h, u, base : base + 2, :]
        copies = [
            copy_to(tx.at[h, 0], ux.at[h, 0], gsend.at[h, 0], grecv.at[h, 0], 1, 0),
            copy_to(tx.at[h, 1], ux.at[h, 1], gsend.at[h, 1], grecv.at[h, 1], -1, 0),
            copy_to(ty.at[h, 0], uy.at[h, 0], gsend.at[h, 2], grecv.at[h, 2], 0, 1),
            copy_to(ty.at[h, 1], uy.at[h, 1], gsend.at[h, 3], grecv.at[h, 3], 0, -1),
        ]
        for at, (dgx, dgy, to, _, _, _) in enumerate(CORNERS):
            copies.append(
                copy_to(tc.at[h, at], uc.at[h, at], gsend.at[h, to], grecv.at[h, to], dgx, dgy)
            )
        for copy in copies:
            copy.start()
        ring_copies.append(copies)

    for h in range(NH):
        for copy in ring_copies[h]:
            copy.wait_recv()
        for u in range(2):
            for i in range(2):
                part = slice(i * 32, i * 32 + 32)
                grid[h, u, i * 40 : i * 40 + 32, :] = ux[h, 0, u, part, :]
                grid[h, u, 17 * RX + i * 40 : 17 * RX + i * 40 + 32, :] = ux[h, 1, u, part, :]
            for j in range(2):
                part = slice(j * 32, j * 32 + 32)
                grid[h, u, pl.ds(RX + 32 + j, 32, stride=40), :] = uy[h, 0, u, part, :]
                grid[h, u, pl.ds(RX + 34 + j, 32, stride=40), :] = uy[h, 1, u, part, :]
            for at, (big_x, base) in enumerate(((0, 32), (17, 32), (0, 34), (17, 34))):
                for i in range(2):
                    to = big_x * RX + i * 40 + base
                    grid[h, u, to : to + 2, :] = uc[h, at, u * 4 + i * 2 : u * 4 + i * 2 + 2, :]
            gridb[:, u * 128 : (u + 1) * 128] = grid[h, u].astype(BF16)
        finish(h)


    pltpu.make_async_copy(others_x, others_x, wsend).wait()
    pltpu.make_async_copy(others_y, others_y, vsend).wait()
    for h in range(NH):
        wait_all(outb, h, fsend)
        wait_all(backb, h, bsend)
        for copy in halo_copies[h] + ring_copies[h]:
            copy.wait_send()


def place_kernel(cell_ref, total, out_hbm, sem):
    def step(s, carry):
        for k in range(8):
            at = s * 8 + k
            cell = cell_ref[at]
            tile = ((cell >> 7) & 15) * 16 + (cell & 15)
            pltpu.make_async_copy(total.at[:, tile], out_hbm.at[:, at], sem).start()
        return carry

    lax.fori_loop(0, NE // 8, step, 0)
    pltpu.make_async_copy(total, out_hbm, sem).wait()


def any_spec():
    return pl.BlockSpec(memory_space=pl.ANY)


def in_hbm(array):
    return pltpu.with_memory_space_constraint(array, pltpu.HBM)


def vmem_spec():
    return pl.BlockSpec(memory_space=pltpu.VMEM)


def smem_spec():
    return pl.BlockSpec(memory_space=pltpu.SMEM)


def per_device(table, state_in, stiffness, elem_cell, group_column, group_inverse):
    state = state_in.reshape(4, NE * 16, LEV)
    dma = pltpu.SemaphoreType.DMA
    vmem = pltpu.VMEM
    whole = jax.ShapeDtypeStruct((4, NE * 16, LEV), F32)
    combined = pl.pallas_call(
        combine_kernel,
        out_shape=whole,
        in_specs=[smem_spec(), any_spec(), any_spec()],
        out_specs=vmem_spec(),
        scratch_shapes=[
            vmem((4, NE * 16, LEV), F32),
            vmem((256, 256), F32),
            vmem((2, NE * 16, LEV), F32),
            dma,
            dma((8,)),
        ],
        compiler_params=pltpu.CompilerParams(vmem_limit_bytes=30 << 20),
        name="combine",
    )(elem_cell, in_hbm(state), stiffness.reshape(256, NE))
    scratch = [
        vmem((4, NHALO * 16, LEV), F32),
        vmem((128, 128), F32),
        vmem((NX, NY, 1, 128), F32),
        vmem((NX, NY, 1, 128), F32),
        vmem((NX, NY, 1, 128), F32),
        vmem((8, 128), F32),
        vmem((8, 128), F32),
        vmem((NC, NC), BF16),
        vmem((NC, NC), BF16),
        vmem((NC, NC), BF16),
        vmem((NC, NC), BF16),
        vmem((256, 256), BF16),
        vmem((256, 256), BF16),
        vmem((NC, 256), BF16),
        vmem((NH, ND, 8, 256), BF16),
        vmem((NH, ND, 8, 256), BF16),
        vmem((NH, ND, 8, 256), BF16),
        vmem((NH, ND, 8, 256), BF16),
        vmem((NC, 256), BF16),
        vmem((NC, 256), BF16),
        vmem((NH, 2, RROWS, LEV), F32),
        vmem((RROWS, 256), BF16),
        vmem((NH, 2, 2, 64, LEV), F32),
        vmem((NH, 2, 2, 64, LEV), F32),
        vmem((NH, 4, 8, LEV), F32),
        vmem((NH, 2, 2, 64, LEV), F32),
        vmem((NH, 2, 2, 64, LEV), F32),
        vmem((NH, 4, 8, LEV), F32),
        vmem((NH, 2, 2, 64, LEV), F32),
        vmem((NH, 2, 2, 64, LEV), F32),
        vmem((NH, 4, 8, LEV), F32),
        vmem((NH, 2, 2, 64, LEV), F32),
        vmem((NH, 2, 2, 64, LEV), F32),
        vmem((NH, 4, 8, LEV), F32),
        dma, dma, dma, dma, dma((5,)),
        dma((NH,)), dma((NH,)), dma((NH,)), dma((NH,)),
        dma((NH, 8)), dma((NH, 8)), dma((NH, 8)), dma((NH, 8)),
    ]
    total = pl.pallas_call(
        exchange_kernel,
        out_shape=whole,
        in_specs=[vmem_spec()] * 5,
        out_specs=vmem_spec(),
        scratch_shapes=scratch,
        compiler_params=pltpu.CompilerParams(
            collective_id=0, has_side_effects=True, vmem_limit_bytes=28 << 20
        ),
        name="exchange",
    )(combined, elem_cell.reshape(2, 128), group_column.reshape(8, 128), group_inverse, table)
    return pl.pallas_call(
        place_kernel,
        out_shape=jax.ShapeDtypeStruct((4, NE, 16, LEV), F32),
        in_specs=[smem_spec(), vmem_spec()],
        out_specs=any_spec(),
        scratch_shapes=[dma],
        compiler_params=pltpu.CompilerParams(vmem_limit_bytes=4 << 20),
        name="place",
    )(elem_cell, total.reshape(4, NE, 16, LEV))


def solution(mesh):
    table = constant_tables()
    placed = (
        P(None, ("gx", "gy"), None, None),
        P(None, None, ("gx", "gy")),
        P(("gx", "gy")),
        P(("gx", "gy")),
        P(("gx", "gy"), None, None),
    )

    def run(*args):
        body = functools.partial(per_device, jnp.asarray(table))
        return jax.shard_map(
            body,
            mesh=mesh,
            in_specs=placed,
            out_specs=P(None, ("gx", "gy"), None, None),
            check_vma=False,
        )(*args)

    return run
```

```python
import functools
import math

import jax
import jax.numpy as jnp
import ml_dtypes
import numpy as np
from jax import lax
from jax.experimental import pallas as pl
from jax.experimental.pallas import tpu as pltpu
from jax.sharding import PartitionSpec as P

F32, BF16, I32 = jnp.float32, jnp.bfloat16, jnp.int32
MESH = pl.DeviceIdType.MESH
NX, NY = 16, 8
ND = NX * NY
TX = TY = 16
NE = TX * TY
NC = 4 * NE
LEV = 128
NH = 2
WEST, EAST, SOUTH, NORTH = 0, 18, 36, 52
NHALO = 68
RX = 80
RROWS = 18 * RX + 16
CORNERS = (
    (1, 1, 4, 15, 15, 15),
    (-1, 1, 5, 0, 15, 3),
    (1, -1, 6, 15, 0, 12),
    (-1, -1, 7, 0, 0, 0),
)


def lagrange_value(node, position, nodes):
    value = 1.0
    for other in range(4):
        if other != node:
            value *= (position - nodes[other]) / (nodes[node] - nodes[other])
    return value


def tables():
    nodes = [-1.0, -1.0 / math.sqrt(5.0), 1.0 / math.sqrt(5.0), 1.0]
    halves = np.zeros((2, 4))
    for i, (low, high) in enumerate(((-1.0, 0.0), (0.0, 1.0))):
        centre, offset = 0.5 * (low + high), 0.5 * (high - low) / math.sqrt(3.0)
        for a in range(4):
            halves[i, a] = (
                0.5
                * (high - low)
                * (
                    lagrange_value(a, centre - offset, nodes)
                    + lagrange_value(a, centre + offset, nodes)
                )
            )
    spread = halves.T @ np.linalg.inv(halves @ halves.T)
    return halves.astype(np.float32).astype(np.float64), spread.astype(np.float32).astype(np.float64)


def split_bf16(table):
    high = table.astype(ml_dtypes.bfloat16)
    low = (table - high.astype(np.float64)).astype(ml_dtypes.bfloat16)
    return high, low


def constant_tables():
    halves, spread = tables()
    cols = np.einsum("ia,jb,yz->iyjzab", halves, halves, np.eye(TY)).reshape(64, 256)
    col_high, col_low = split_bf16(cols)
    along = np.zeros((4, 3, 2))
    along[:, 1, :] = spread
    along[0, 0, :] += spread[3]
    along[3, 2, :] += spread[0]
    along[0] *= 0.5
    along[3] *= 0.5
    along_y = np.zeros((TY, 4, 40))
    for y in range(TY):
        for step in range(3):
            other = y + step - 1
            base = 32 if other < 0 else 34 if other >= TY else 2 * other
            along_y[y, :, base : base + 2] += along[:, step, :]
    update = np.zeros((256, 256))
    update[:, :240] = np.einsum("asi,ybr->yabsir", along, along_y).reshape(256, 240)
    up_high, up_low = split_bf16(update)
    return np.concatenate([up_high, up_low, col_high, col_low], 0)


def iota(shape, dim):
    return lax.broadcasted_iota(I32, shape, dim)


def dot(left, right):
    return jnp.dot(left, right, preferred_element_type=F32)


def dot_nt(left, right):
    return lax.dot_general(left, right, (((1,), (1,)), ((), ())), preferred_element_type=F32)


class Peers:
    def __init__(self, gx, gy):
        self.x, self.y = lax.div(gx, 4), lax.rem(gx, 4)
        self.z, self.core = lax.div(gy, 2), lax.rem(gy, 2)
        self.xs = [lax.rem(self.x + a, 4) * 4 for a in range(4)]
        self.zs = [lax.rem(self.z + d, 4) * 2 for d in range(4)]
        self.cores = [self.core, 1 - self.core]

    def block(self, b, with_self=False):
        ys = [lax.rem(self.y + b + a, 4) for a in range(4)]
        back_b = lax.rem(4 - b, 4) if not isinstance(b, int) else -b % 4
        found = []
        for d in range(4):
            for a in range(4):
                for c in range(2):
                    if isinstance(b, int) and b == d == a == c == 0 and not with_self:
                        continue
                    tgx = self.xs[a] + ys[a]
                    tgy = self.zs[(d + a) % 4] + self.cores[c]
                    inner = d * 8 + a * 2 + c
                    back = -d % 4 * 8 + -a % 4 * 2 + c
                    found.append((tgx, tgy, b * 32 + inner, back_b * 32 + back))
        return found

    def position(self, source):
        a = ((source >> 5) - self.x) & 3
        b = (((source >> 3) & 3) - self.y - a) & 3
        d = (((source >> 1) & 3) - self.z - a) & 3
        c = ((source & 1) - self.core) & 1
        return b * 32 + d * 8 + a * 2 + c


def combine_kernel(
    cell_ref, gcol_hbm, state_hbm, stiff_hbm,
    out_ref, wq, rank_ref,
    st, xs, w, wv, gcol_ref, stiff_sem, gcol_sem, state_sem,
):
    gcol_copy = pltpu.make_async_copy(gcol_hbm, gcol_ref, gcol_sem)
    gcol_copy.start()
    stiff_copy = pltpu.make_async_copy(stiff_hbm, xs, stiff_sem)
    stiff_copy.start()
    loads = []
    for part in range(8):
        rows = pl.ds(part * 512, 512)
        copy = pltpu.make_async_copy(state_hbm.at[:, rows], st.at[:, rows], state_sem.at[part])
        copy.start()
        loads.append(copy)
    stiff_copy.wait()
    flipped = xs[...].T.astype(BF16)
    row_i, col_i = iota((256, 256), 0), iota((256, 256), 1)
    same_m = (row_i & 15) == (col_i & 15)
    diagonal = (row_i & 15) == (col_i >> 4)
    for n in range(16):
        pick = jnp.where(same_m & ((row_i >> 4) == n), 1.0, 0.0).astype(BF16)
        block = jnp.where(diagonal, dot(flipped, pick), 0.0)
        for u in range(2):
            w[u, pl.ds(n, 256, stride=16), :] = block[:, u * 128 : (u + 1) * 128]

    lane, sub = iota((128, 128), 1), iota((128, 128), 0)
    gcol_copy.wait()

    upper = jnp.where(sub < lane, 1.0, 0.0).astype(BF16)
    seen = jnp.zeros((128, 1), F32)
    want_high = jnp.zeros((128, 128), F32)
    want_low = jnp.zeros((128, 128), F32)
    for block in range(8):
        named = gcol_ref[block : block + 1, :]
        source, local = named >> 10, named & 1023
        hit = jnp.broadcast_to(source, (128, 128)) == sub
        onehot = jnp.where(hit, 1.0, 0.0)
        before = dot(onehot.astype(BF16), upper) + seen
        seen = seen + jnp.sum(onehot, axis=1, keepdims=True)
        rank = jnp.sum(jnp.where(hit, before, 0.0), axis=0, keepdims=True)
        rank_ref[block : block + 1, :] = rank
        ranked = jnp.broadcast_to(rank, (128, 128)) == sub.astype(F32)
        high = (local >> 5).astype(F32)
        low = (local & 31).astype(F32)
        zero = jnp.zeros((128, 128), F32)
        chosen_high = jnp.where(ranked, jnp.broadcast_to(high, (128, 128)), zero).astype(BF16)
        chosen_low = jnp.where(ranked, jnp.broadcast_to(low, (128, 128)), zero).astype(BF16)
        onehot = onehot.astype(BF16)
        want_high = want_high + dot_nt(onehot, chosen_high)
        want_low = want_low + dot_nt(onehot, chosen_low)
    wv[...] = want_high * 32.0 + want_low

    def row_out(s, carry):
        for y in range(NY):
            wq[s, y] = wv[pl.ds(s * NY + y, 1), :]
        return carry

    lax.fori_loop(0, NX, row_out, 0)
    def step(g, carry):
        rows = pl.ds(pl.multiple_of(g * 256, 256), 256)
        state = jnp.concatenate([st[f, rows, :] for f in range(4)], axis=1)
        oper = jnp.concatenate([w[0, rows, :], w[1, rows, :]], axis=1).astype(BF16)
        state = state + dot(oper, state.astype(BF16))
        for e in range(16):
            cell = cell_ref[g * 16 + e]
            tile = ((cell >> 7) & 15) * 16 + (cell & 15)
            target = pl.ds(pl.multiple_of(tile * 16, 16), 16)
            for f in range(4):
                out_ref[f, target, :] = state[e * 16 : e * 16 + 16, f * 128 : f * 128 + 128]
        return carry

    for part in range(8):
        loads[part].wait()
        lax.fori_loop(part * 2, part * 2 + 2, step, 0)


def exchange_kernel(
    st, cell_ref, gcol_ref, rank_ref, wq, inv, table_ref,
    dyn,
    halo, mid, req, qrow, crow,
    sel, sel_t, place, place_t,
    dyn_high, dyn_low, cols, outb, incb, backb, rcvb, flat, tend, grid, gridb,
    sx, sy, sc, rx, ry, rc,
    tx, ty, tc, ux, uy, uc,
    wsend, wrecv, vsend, vrecv, loc_sem,
    fsend, frecv, bsend, brecv, hsend, hrecv, gsend, grecv,
):
    gx, gy = lax.axis_index("gx"), lax.axis_index("gy")
    peers = Peers(gx, gy)
    barrier = pltpu.get_barrier_semaphore()

    def other_x(k):
        return lax.rem(gx + k, NX)

    def other_y(k):
        return lax.rem(gy + k, NY)

    for dgx, dgy, _, _, _, _ in CORNERS:
        pl.semaphore_signal(
            barrier, inc=1, device_id=(other_x(NX + dgx), other_y(NY + dgy)), device_id_type=MESH
        )

    def greet_x(k, carry):
        pl.semaphore_signal(barrier, inc=1, device_id=(other_x(k), gy), device_id_type=MESH)
        return carry

    def greet_y(k, carry):
        pl.semaphore_signal(barrier, inc=1, device_id=(gx, other_y(k)), device_id_type=MESH)
        return carry

    lax.fori_loop(1, NX, greet_x, 0)
    lax.fori_loop(1, NY, greet_y, 0)


    lane = iota((128, 128), 1)
    sub = iota((128, 128), 0)
    eye = lane == sub

    def to_col(row):
        return jnp.sum(jnp.where(eye, jnp.broadcast_to(row, (128, 128)), 0.0), axis=1, keepdims=True)

    def to_row(col):
        return jnp.sum(jnp.where(eye, jnp.broadcast_to(col, (128, 128)), 0.0), axis=0, keepdims=True)

    source = gcol_ref[...] >> 10
    qrow[...] = peers.position(source).astype(F32) * 8.0 + rank_ref[...]
    pl.semaphore_wait(barrier, NX + NY - 2 + len(CORNERS))

    def ask_x(k, carry):
        pltpu.make_async_remote_copy(
            wq.at[other_x(k)], mid.at[gx], wsend, wrecv,
            device_id=(other_x(k), gy), device_id_type=MESH,
        ).start()
        return carry

    lax.fori_loop(1, NX, ask_x, 0)
    own_x = pltpu.make_async_copy(wq.at[gx], mid.at[gx], loc_sem.at[0])
    own_x.start()

    others_x = mid.at[pl.ds(0, NX - 1)]
    others_y = req.at[:, pl.ds(0, NY - 1)]

    def ask_y(k, carry):
        pltpu.make_async_remote_copy(
            mid.at[:, other_y(k)], req.at[:, gy], vsend, vrecv,
            device_id=(gx, other_y(k)), device_id_type=MESH,
        ).start()
        return carry

    def copy_to(src, dst, send, recv, dgx, dgy):
        return pltpu.make_async_remote_copy(
            src, dst, send, recv,
            device_id=((gx + dgx + NX) % NX, (gy + dgy + NY) % NY),
            device_id_type=MESH,
        )

    def send_halo(h):
        for f in range(2):
            field = 2 * h + f

            for k in range(16):
                part = pl.ds(k * 4, 4)
                sx[h, 0, f, part, :] = st[field, pl.ds((15 * 16 + k) * 16 + 12, 4), :]
                sx[h, 1, f, part, :] = st[field, pl.ds(k * 16, 4), :]
                sy[h, 0, f, part, :] = st[field, pl.ds((k * 16 + 15) * 16 + 3, 4, stride=4), :]
                sy[h, 1, f, part, :] = st[field, pl.ds(k * 256, 4, stride=4), :]
            for at, (_, _, _, x, y, n) in enumerate(CORNERS):
                sc[h, at, f : f + 1, :] = st[field, pl.ds((x * 16 + y) * 16 + n, 1), :]
        copies = [
            copy_to(sx.at[h, 0], rx.at[h, 0], hsend.at[h, 0], hrecv.at[h, 0], 1, 0),
            copy_to(sx.at[h, 1], rx.at[h, 1], hsend.at[h, 1], hrecv.at[h, 1], -1, 0),
            copy_to(sy.at[h, 0], ry.at[h, 0], hsend.at[h, 2], hrecv.at[h, 2], 0, 1),
            copy_to(sy.at[h, 1], ry.at[h, 1], hsend.at[h, 3], hrecv.at[h, 3], 0, -1),
        ]
        for at, (dgx, dgy, to, _, _, _) in enumerate(CORNERS):
            copies.append(
                copy_to(sc.at[h, at], rc.at[h, at], hsend.at[h, to], hrecv.at[h, to], dgx, dgy)
            )
        for copy in copies:
            copy.start()
        return copies

    def take_halo(h, copies):
        for copy in copies:
            copy.wait_recv()
        for f in range(2):
            field = 2 * h + f
            for k in range(16):
                part = pl.ds(k * 4, 4)
                halo[field, pl.ds((WEST + 1 + k) * 16 + 12, 4), :] = rx[h, 0, f, part, :]
                halo[field, pl.ds((EAST + 1 + k) * 16, 4), :] = rx[h, 1, f, part, :]
                halo[field, pl.ds((SOUTH + k) * 16 + 3, 4, stride=4), :] = ry[h, 0, f, part, :]
                halo[field, pl.ds((NORTH + k) * 16, 4, stride=4), :] = ry[h, 1, f, part, :]
            halo[field, pl.ds(WEST * 16 + 15, 1), :] = rc[h, 0, f : f + 1, :]
            halo[field, pl.ds(EAST * 16 + 3, 1), :] = rc[h, 1, f : f + 1, :]
            halo[field, pl.ds((WEST + 17) * 16 + 12, 1), :] = rc[h, 2, f : f + 1, :]
            halo[field, pl.ds((EAST + 17) * 16, 1), :] = rc[h, 3, f : f + 1, :]

    s8 = iota((8, 128), 0)
    b_at = s8 & 3
    is_b0, is_b3, first_a = b_at == 0, b_at == 3, s8 < 4
    b_scale = jnp.where(is_b0 | is_b3, 0.5, 1.0)
    scale0 = b_scale * jnp.where(first_a, 0.5, 1.0)
    scale1 = b_scale * jnp.where(first_a, 1.0, 0.5)

    def dynamics(h):
        def column(x, carry):
            fixed = isinstance(x, int)

            def rows(x, y, v):
                inside = 0 <= y < TY
                if fixed and x == -1:
                    return halo, (WEST + y + 1) * 16 + v * 8
                if fixed and x == TX:
                    return halo, (EAST + y + 1) * 16 + v * 8
                if not inside:
                    return halo, ((SOUTH if y < 0 else NORTH) + x) * 16 + v * 8
                return st, x * 256 + y * 16 + v * 8

            def load(field, x, y, v):
                ref, at = rows(x, y, v)
                return ref[field, pl.ds(at if fixed else pl.multiple_of(at, 8), 8), :]

            def along_x(y):
                found = []
                for f in range(2):
                    field = 2 * h + f
                    own0, own1 = load(field, x, y, 0), load(field, x, y, 1)
                    before, after = load(field, x - 1, y, 1), load(field, x + 1, y, 0)
                    found.append(own0 + jnp.where(first_a, pltpu.roll(before, 4, 0), 0.0))
                    found.append(own1 + jnp.where(first_a, 0.0, pltpu.roll(after, 4, 0)))
                return found

            south, here = along_x(-1), along_x(0)
            for y in range(TY):
                north = along_x(y + 1)
                for f in range(2):
                    parts = []
                    for v, scale in ((2 * f, scale0), (2 * f + 1, scale1)):
                        edge = jnp.where(is_b0, pltpu.roll(south[v], 5, 0), 0.0)
                        edge = jnp.where(is_b3, pltpu.roll(north[v], 3, 0), edge)
                        parts.append((here[v] + edge) * scale)
                    total = jnp.concatenate(parts, axis=0)
                    at = x * 256 + y * 16
                    dyn[2 * h + f, pl.ds(at if fixed else pl.multiple_of(at, 16), 16), :] = total
                    high = total.astype(BF16)
                    dyn_high[y * 16 : y * 16 + 16, f * 128 : f * 128 + 128] = high
                    low = (total - high.astype(F32)).astype(BF16)
                    dyn_low[y * 16 : y * 16 + 16, f * 128 : f * 128 + 128] = low
                south, here = here, north
            main = dot(table_ref[512:640, :], dyn_high[...])
            rest = dot(table_ref[512:576, :], dyn_low[...])
            total = main[0:64] + main[64:128] + rest
            cols[pl.ds(x * 64 if fixed else pl.multiple_of(x * 64, 64), 64), :] = total.astype(BF16)
            return carry

        column(0, 0)
        lax.fori_loop(1, TX - 1, column, 0)
        column(TX - 1, 0)

    wide = iota((128, 1024), 1)

    def selections():
        k_mask = iota((128, 128), 1) == (iota((128, 128), 0) & 7)

        def build(b, carry):
            found = peers.block(b, with_self=True)
            for part in range(2):
                asked = [
                    jnp.broadcast_to(req[tgx, tgy], (8, 128))
                    for tgx, tgy, _, _ in found[part * 16 : part * 16 + 16]
                ]
                asked = jnp.where(k_mask, jnp.concatenate(asked, axis=0), 0.0)
                asked = jnp.sum(asked, axis=1, keepdims=True).astype(I32)
                slot_at, piece = asked >> 2, asked & 3
                tile = jnp.zeros((128, 128), F32)
                for u in range(2):
                    cell = cell_ref[u : u + 1, :]
                    names = (((cell >> 7) & 15) * 16 + (cell & 15)).astype(F32)
                    names = jnp.broadcast_to(names, (128, 128))
                    tile = tile + jnp.where(slot_at == lane + 128 * u, names, 0.0)
                tile = jnp.sum(tile, axis=1, keepdims=True).astype(I32)
                at = (tile >> 4) * 64 + (piece >> 1) * 32 + (tile & 15) * 2 + (piece & 1)
                block = b * 2 + part
                rows = pl.ds(pl.multiple_of(block * 128, 128), 128)
                sel[rows, :] = jnp.where(wide == at, 1.0, 0.0).astype(BF16)
                crow[pl.ds(block, 1), :] = to_row(at.astype(F32))
            return carry

        lax.fori_loop(0, 4, build, 0)

    def transposed(row_ref, out_ref):
        def build(block, carry):
            rows = pl.ds(pl.multiple_of(block * 128, 128), 128)
            want = (sub + block * 128).astype(F32)
            for u in range(8):
                names = jnp.broadcast_to(row_ref[u : u + 1, :], (128, 128))
                out_ref[rows, u * 128 : (u + 1) * 128] = jnp.where(names == want, 1.0, 0.0).astype(BF16)
            return carry

        lax.fori_loop(0, 8, build, 0)

    def placing():
        def build(block, carry):
            rows = pl.ds(pl.multiple_of(block * 128, 128), 128)
            at = to_col(qrow[pl.ds(block, 1), :]).astype(I32)
            place[rows, :] = jnp.where(wide == at, 1.0, 0.0).astype(BF16)
            return carry

        lax.fori_loop(0, 8, build, 0)

    def permute_and_send(matrix, source, src, dst, h, send, recv, loc):
        def step(b):
            rows = pl.ds(pl.multiple_of(b * 256, 256), 256)
            moved = dot(matrix[rows, :], source[...])
            src[h, pl.ds(b * 32, 32)] = moved.reshape(32, 8, 256).astype(BF16)
            for tgx, tgy, at, back in peers.block(b):
                pltpu.make_async_remote_copy(
                    src.at[h, at], dst.at[h, back], send.at[h], recv.at[h],
                    device_id=(tgx, tgy), device_id_type=MESH,
                ).start()

        def loop_step(b, carry):
            step(b)
            return carry

        step(0)
        own = pltpu.make_async_copy(src.at[h, 0], dst.at[h, 0], loc_sem.at[loc])
        own.start()
        lax.fori_loop(1, 4, loop_step, 0)
        return own

    def wait_all(ref, h, sem):
        block = ref.at[h, pl.ds(0, ND - 1)]
        pltpu.make_async_copy(block, block, sem.at[h]).wait()

    def flatten(src, h):
        def step(block, carry):
            part = src[h, pl.ds(block * 16, 16)].astype(F32).reshape(128, 256)
            flat[pl.ds(pl.multiple_of(block * 128, 128), 128), :] = part.astype(BF16)
            return carry

        lax.fori_loop(0, 8, step, 0)

    halo_copies, forward, back_copies = [None] * NH, [None] * NH, [None] * NH
    for h in range(NH):
        halo_copies[h] = send_halo(h)
    transposed(qrow, place_t)
    placing()
    grid[...] = jnp.zeros_like(grid)
    own_x.wait()
    pltpu.make_async_copy(others_x, others_x, wrecv).wait()
    lax.fori_loop(1, NY, ask_y, 0)
    own_y = pltpu.make_async_copy(mid.at[:, gy], req.at[:, gy], loc_sem.at[0])
    own_y.start()
    for h in range(NH):
        take_halo(h, halo_copies[h])
        dynamics(h)
        if h == 0:
            own_y.wait()
            pltpu.make_async_copy(others_y, others_y, vrecv).wait()
            selections()
        forward[h] = permute_and_send(sel, cols, outb, incb, h, fsend, frecv, 1 + h)

    transposed(crow, sel_t)

    def physics(h):
        def step(block, carry):
            rows = pl.ds(pl.multiple_of(block * 256, 256), 256)
            moved = dot(place[rows, :], flat[...])
            for g in range(16):
                part = moved[g * 16 : (g + 1) * 16, :]
                stacked = jnp.concatenate([part[:, :128], part[:, 128:]], axis=0)
                smooth = dot_nt(stacked.astype(BF16), inv[block * 16 + g])
                change = smooth - stacked
                change = jnp.concatenate([change[:16], change[16:]], axis=1)
                tend[pl.ds(pl.multiple_of(block * 256 + g * 16, 16), 16), :] = change.astype(BF16)
            return carry

        lax.fori_loop(0, 4, step, 0)

    for h in range(NH):
        forward[h].wait()
        wait_all(incb, h, frecv)
        flatten(incb, h)
        physics(h)
        back_copies[h] = permute_and_send(place_t, tend, backb, rcvb, h, bsend, brecv, 3 + h)

    ring_copies = []

    def finish(h):
        def add(x, carry):
            rows = pl.ds(pl.multiple_of(x * 256, 256), 256)
            near = gridb[pl.ds(pl.multiple_of(x * RX, 16), 256), :]
            update = dot(table_ref[0:512, :], near)
            update = update[:256] + update[256:]
            for f in range(2):
                field = 2 * h + f
                dyn[field, rows, :] = dyn[field, rows, :] + update[:, f * LEV : (f + 1) * LEV]
            return carry

        lax.fori_loop(0, TX, add, 0)

    for h in range(NH):
        back_copies[h].wait()
        wait_all(rcvb, h, brecv)
        flatten(rcvb, h)

        def ungroup(block, carry):
            rows = pl.ds(pl.multiple_of(block * 256, 256), 256)
            moved = dot(sel_t[rows, :], flat[...])
            for x in range(4):
                for i in range(2):
                    base = pl.multiple_of((block * 4 + x + 1) * RX + i * 40, 8)
                    piece = moved[x * 64 + i * 32 : x * 64 + i * 32 + 32, :]
                    for u in range(2):
                        grid[h, u, pl.ds(base, 32), :] = piece[:, u * 128 : (u + 1) * 128]
            return carry

        lax.fori_loop(0, 4, ungroup, 0)
        for u in range(2):
            for i in range(2):
                tx[h, 0, u, i * 32 : i * 32 + 32, :] = grid[h, u, 16 * RX + i * 40 : 16 * RX + i * 40 + 32, :]
                tx[h, 1, u, i * 32 : i * 32 + 32, :] = grid[h, u, RX + i * 40 : RX + i * 40 + 32, :]
            for j in range(2):
                ty[h, 0, u, j * 32 : j * 32 + 32, :] = grid[h, u, pl.ds(RX + 30 + j, 32, stride=40), :]
                ty[h, 1, u, j * 32 : j * 32 + 32, :] = grid[h, u, pl.ds(RX + j, 32, stride=40), :]
            for at, (_, _, _, x, y, _) in enumerate(CORNERS):
                for i in range(2):
                    base = (x + 1) * RX + i * 40 + 2 * y
                    tc[h, at, u * 4 + i * 2 : u * 4 + i * 2 + 2, :] = grid[h, u, base : base + 2, :]
        copies = [
            copy_to(tx.at[h, 0], ux.at[h, 0], gsend.at[h, 0], grecv.at[h, 0], 1, 0),
            copy_to(tx.at[h, 1], ux.at[h, 1], gsend.at[h, 1], grecv.at[h, 1], -1, 0),
            copy_to(ty.at[h, 0], uy.at[h, 0], gsend.at[h, 2], grecv.at[h, 2], 0, 1),
            copy_to(ty.at[h, 1], uy.at[h, 1], gsend.at[h, 3], grecv.at[h, 3], 0, -1),
        ]
        for at, (dgx, dgy, to, _, _, _) in enumerate(CORNERS):
            copies.append(
                copy_to(tc.at[h, at], uc.at[h, at], gsend.at[h, to], grecv.at[h, to], dgx, dgy)
            )
        for copy in copies:
            copy.start()
        ring_copies.append(copies)

    for h in range(NH):
        for copy in ring_copies[h]:
            copy.wait_recv()
        for u in range(2):
            for i in range(2):
                part = slice(i * 32, i * 32 + 32)
                grid[h, u, i * 40 : i * 40 + 32, :] = ux[h, 0, u, part, :]
                grid[h, u, 17 * RX + i * 40 : 17 * RX + i * 40 + 32, :] = ux[h, 1, u, part, :]
            for j in range(2):
                part = slice(j * 32, j * 32 + 32)
                grid[h, u, pl.ds(RX + 32 + j, 32, stride=40), :] = uy[h, 0, u, part, :]
                grid[h, u, pl.ds(RX + 34 + j, 32, stride=40), :] = uy[h, 1, u, part, :]
            for at, (big_x, base) in enumerate(((0, 32), (17, 32), (0, 34), (17, 34))):
                for i in range(2):
                    to = big_x * RX + i * 40 + base
                    grid[h, u, to : to + 2, :] = uc[h, at, u * 4 + i * 2 : u * 4 + i * 2 + 2, :]
            gridb[:, u * 128 : (u + 1) * 128] = grid[h, u].astype(BF16)
        finish(h)


    pltpu.make_async_copy(others_x, others_x, wsend).wait()
    pltpu.make_async_copy(others_y, others_y, vsend).wait()
    for h in range(NH):
        wait_all(outb, h, fsend)
        wait_all(backb, h, bsend)
        for copy in halo_copies[h] + ring_copies[h]:
            copy.wait_send()


def place_kernel(cell_ref, total, out_hbm, sem):
    def step(s, carry):
        for k in range(8):
            at = s * 8 + k
            cell = cell_ref[at]
            tile = ((cell >> 7) & 15) * 16 + (cell & 15)
            pltpu.make_async_copy(total.at[:, tile], out_hbm.at[:, at], sem).start()
        return carry

    lax.fori_loop(0, NE // 8, step, 0)
    pltpu.make_async_copy(total, out_hbm, sem).wait()


def any_spec():
    return pl.BlockSpec(memory_space=pl.ANY)


def in_hbm(array):
    return pltpu.with_memory_space_constraint(array, pltpu.HBM)


def vmem_spec():
    return pl.BlockSpec(memory_space=pltpu.VMEM)


def smem_spec():
    return pl.BlockSpec(memory_space=pltpu.SMEM)


def per_device(table, state_in, stiffness, elem_cell, group_column, group_inverse):
    state = state_in.reshape(4, NE * 16, LEV)
    dma = pltpu.SemaphoreType.DMA
    vmem = pltpu.VMEM
    whole = jax.ShapeDtypeStruct((4, NE * 16, LEV), F32)
    named = group_column.reshape(8, 128)
    combined, wanted, rank = pl.pallas_call(
        combine_kernel,
        out_shape=(
            whole,
            jax.ShapeDtypeStruct((NX, NY, 1, 128), F32),
            jax.ShapeDtypeStruct((8, 128), F32),
        ),
        in_specs=[smem_spec(), any_spec(), any_spec(), any_spec()],
        out_specs=(vmem_spec(), vmem_spec(), vmem_spec()),
        scratch_shapes=[
            vmem((4, NE * 16, LEV), F32),
            vmem((256, 256), F32),
            vmem((2, NE * 16, LEV), F32),
            vmem((128, 128), F32),
            vmem((8, 128), I32),
            dma,
            dma,
            dma((8,)),
        ],
        compiler_params=pltpu.CompilerParams(vmem_limit_bytes=30 << 20),
        name="combine",
    )(elem_cell, in_hbm(named), in_hbm(state), stiffness.reshape(256, NE))
    scratch = [
        vmem((4, NHALO * 16, LEV), F32),
        vmem((NX, NY, 1, 128), F32),
        vmem((NX, NY, 1, 128), F32),
        vmem((8, 128), F32),
        vmem((8, 128), F32),
        vmem((NC, NC), BF16),
        vmem((NC, NC), BF16),
        vmem((NC, NC), BF16),
        vmem((NC, NC), BF16),
        vmem((256, 256), BF16),
        vmem((256, 256), BF16),
        vmem((NC, 256), BF16),
        vmem((NH, ND, 8, 256), BF16),
        vmem((NH, ND, 8, 256), BF16),
        vmem((NH, ND, 8, 256), BF16),
        vmem((NH, ND, 8, 256), BF16),
        vmem((NC, 256), BF16),
        vmem((NC, 256), BF16),
        vmem((NH, 2, RROWS, LEV), F32),
        vmem((RROWS, 256), BF16),
        vmem((NH, 2, 2, 64, LEV), F32),
        vmem((NH, 2, 2, 64, LEV), F32),
        vmem((NH, 4, 8, LEV), F32),
        vmem((NH, 2, 2, 64, LEV), F32),
        vmem((NH, 2, 2, 64, LEV), F32),
        vmem((NH, 4, 8, LEV), F32),
        vmem((NH, 2, 2, 64, LEV), F32),
        vmem((NH, 2, 2, 64, LEV), F32),
        vmem((NH, 4, 8, LEV), F32),
        vmem((NH, 2, 2, 64, LEV), F32),
        vmem((NH, 2, 2, 64, LEV), F32),
        vmem((NH, 4, 8, LEV), F32),
        dma, dma, dma, dma, dma((5,)),
        dma((NH,)), dma((NH,)), dma((NH,)), dma((NH,)),
        dma((NH, 8)), dma((NH, 8)), dma((NH, 8)), dma((NH, 8)),
    ]
    total = pl.pallas_call(
        exchange_kernel,
        out_shape=whole,
        in_specs=[vmem_spec()] * 7,
        out_specs=vmem_spec(),
        scratch_shapes=scratch,
        compiler_params=pltpu.CompilerParams(
            collective_id=0, has_side_effects=True, vmem_limit_bytes=28 << 20
        ),
        name="exchange",
    )(combined, elem_cell.reshape(2, 128), named, rank, wanted, group_inverse, table)
    return pl.pallas_call(
        place_kernel,
        out_shape=jax.ShapeDtypeStruct((4, NE, 16, LEV), F32),
        in_specs=[smem_spec(), vmem_spec()],
        out_specs=any_spec(),
        scratch_shapes=[dma],
        compiler_params=pltpu.CompilerParams(vmem_limit_bytes=4 << 20),
        name="place",
    )(elem_cell, total.reshape(4, NE, 16, LEV))


def solution(mesh):
    table = constant_tables()
    placed = (
        P(None, ("gx", "gy"), None, None),
        P(None, None, ("gx", "gy")),
        P(("gx", "gy")),
        P(("gx", "gy")),
        P(("gx", "gy"), None, None),
    )

    def run(*args):
        body = functools.partial(per_device, jnp.asarray(table))
        return jax.shard_map(
            body,
            mesh=mesh,
            in_specs=placed,
            out_specs=P(None, ("gx", "gy"), None, None),
            check_vma=False,
        )(*args)

    return run
```

```python
import functools
import math

import jax
import jax.numpy as jnp
import ml_dtypes
import numpy as np
from jax import lax
from jax.experimental import pallas as pl
from jax.experimental.pallas import tpu as pltpu
from jax.sharding import PartitionSpec as P

F32, BF16, I32 = jnp.float32, jnp.bfloat16, jnp.int32
MESH = pl.DeviceIdType.MESH
NX, NY = 16, 8
ND = NX * NY
TX = TY = 16
NE = TX * TY
NC = 4 * NE
LEV = 128
NH = 2
WEST, EAST, SOUTH, NORTH = 0, 18, 36, 52
NHALO = 68
RX = 80
RROWS = 18 * RX + 16
CORNERS = (
    (1, 1, 4, 15, 15, 15),
    (-1, 1, 5, 0, 15, 3),
    (1, -1, 6, 15, 0, 12),
    (-1, -1, 7, 0, 0, 0),
)


def lagrange_value(node, position, nodes):
    value = 1.0
    for other in range(4):
        if other != node:
            value *= (position - nodes[other]) / (nodes[node] - nodes[other])
    return value


def tables():
    nodes = [-1.0, -1.0 / math.sqrt(5.0), 1.0 / math.sqrt(5.0), 1.0]
    halves = np.zeros((2, 4))
    for i, (low, high) in enumerate(((-1.0, 0.0), (0.0, 1.0))):
        centre, offset = 0.5 * (low + high), 0.5 * (high - low) / math.sqrt(3.0)
        for a in range(4):
            halves[i, a] = (
                0.5
                * (high - low)
                * (
                    lagrange_value(a, centre - offset, nodes)
                    + lagrange_value(a, centre + offset, nodes)
                )
            )
    spread = halves.T @ np.linalg.inv(halves @ halves.T)
    return halves.astype(np.float32).astype(np.float64), spread.astype(np.float32).astype(np.float64)


def split_bf16(table):
    high = table.astype(ml_dtypes.bfloat16)
    low = (table - high.astype(np.float64)).astype(ml_dtypes.bfloat16)
    return high, low


def constant_tables():
    halves, spread = tables()
    cols = np.einsum("ia,jb,yz->iyjzab", halves, halves, np.eye(TY)).reshape(64, 256)
    col_high, col_low = split_bf16(cols)
    along = np.zeros((4, 3, 2))
    along[:, 1, :] = spread
    along[0, 0, :] += spread[3]
    along[3, 2, :] += spread[0]
    along[0] *= 0.5
    along[3] *= 0.5
    along_y = np.zeros((TY, 4, 40))
    for y in range(TY):
        for step in range(3):
            other = y + step - 1
            base = 32 if other < 0 else 34 if other >= TY else 2 * other
            along_y[y, :, base : base + 2] += along[:, step, :]
    update = np.zeros((256, 256))
    update[:, :240] = np.einsum("asi,ybr->yabsir", along, along_y).reshape(256, 240)
    up_high, up_low = split_bf16(update)
    return np.concatenate([up_high, up_low, col_high, col_low], 0)


def iota(shape, dim):
    return lax.broadcasted_iota(I32, shape, dim)


def dot(left, right):
    return jnp.dot(left, right, preferred_element_type=F32)


def dot_nt(left, right):
    return lax.dot_general(left, right, (((1,), (1,)), ((), ())), preferred_element_type=F32)


class Peers:
    def __init__(self, gx, gy):
        self.x, self.y = lax.div(gx, 4), lax.rem(gx, 4)
        self.z, self.core = lax.div(gy, 2), lax.rem(gy, 2)
        self.xs = [lax.rem(self.x + a, 4) * 4 for a in range(4)]
        self.zs = [lax.rem(self.z + d, 4) * 2 for d in range(4)]
        self.cores = [self.core, 1 - self.core]

    def block(self, b, with_self=False):
        ys = [lax.rem(self.y + b + a, 4) for a in range(4)]
        back_b = lax.rem(4 - b, 4) if not isinstance(b, int) else -b % 4
        found = []
        for d in range(4):
            for a in range(4):
                for c in range(2):
                    if isinstance(b, int) and b == d == a == c == 0 and not with_self:
                        continue
                    tgx = self.xs[a] + ys[a]
                    tgy = self.zs[(d + a) % 4] + self.cores[c]
                    inner = d * 8 + a * 2 + c
                    back = -d % 4 * 8 + -a % 4 * 2 + c
                    found.append((tgx, tgy, b * 32 + inner, back_b * 32 + back))
        return found

    def position(self, source):
        a = ((source >> 5) - self.x) & 3
        b = (((source >> 3) & 3) - self.y - a) & 3
        d = (((source >> 1) & 3) - self.z - a) & 3
        c = ((source & 1) - self.core) & 1
        return b * 32 + d * 8 + a * 2 + c


def combine_kernel(cell_ref, state_hbm, stiff_hbm, out_ref, st, xs, w, stiff_sem, state_sem):
    stiff_copy = pltpu.make_async_copy(stiff_hbm, xs, stiff_sem)
    stiff_copy.start()
    loads = []
    for part in range(8):
        rows = pl.ds(part * 512, 512)
        copy = pltpu.make_async_copy(state_hbm.at[:, rows], st.at[:, rows], state_sem.at[part])
        copy.start()
        loads.append(copy)
    stiff_copy.wait()
    flipped = xs[...].T.astype(BF16)
    row_i, col_i = iota((256, 256), 0), iota((256, 256), 1)
    same_m = (row_i & 15) == (col_i & 15)
    diagonal = (row_i & 15) == (col_i >> 4)
    for n in range(16):
        pick = jnp.where(same_m & ((row_i >> 4) == n), 1.0, 0.0).astype(BF16)
        block = jnp.where(diagonal, dot(flipped, pick), 0.0)
        for u in range(2):
            w[u, pl.ds(n, 256, stride=16), :] = block[:, u * 128 : (u + 1) * 128]

    def step(g, carry):
        rows = pl.ds(pl.multiple_of(g * 256, 256), 256)
        state = jnp.concatenate([st[f, rows, :] for f in range(4)], axis=1)
        oper = jnp.concatenate([w[0, rows, :], w[1, rows, :]], axis=1).astype(BF16)
        state = state + dot(oper, state.astype(BF16))
        for e in range(16):
            cell = cell_ref[g * 16 + e]
            tile = ((cell >> 7) & 15) * 16 + (cell & 15)
            target = pl.ds(pl.multiple_of(tile * 16, 16), 16)
            for f in range(4):
                out_ref[f, target, :] = state[e * 16 : e * 16 + 16, f * 128 : f * 128 + 128]
        return carry

    for part in range(8):
        loads[part].wait()
        lax.fori_loop(part * 2, part * 2 + 2, step, 0)


def exchange_kernel(
    st, cell_ref, gcol_ref, inv, table_ref,
    dyn,
    halo, wv, wq, req, qrow, crow,
    sel, sel_t, place, place_t,
    dyn_high, dyn_low, cols, outb, incb, backb, rcvb, flat, tend, grid, gridb,
    sx, sy, sc, rx, ry, rc,
    tx, ty, tc, ux, uy, uc,
    wsend, wrecv, loc_sem,
    fsend, frecv, bsend, brecv, hsend, hrecv, gsend, grecv,
):
    gx, gy = lax.axis_index("gx"), lax.axis_index("gy")
    me = gx * NY + gy
    peers = Peers(gx, gy)
    barrier = pltpu.get_barrier_semaphore()

    def to_peers(act):
        def step(b, carry):
            for tgx, tgy, _, _ in peers.block(b):
                act(tgx, tgy)
            return carry

        step(0, 0)
        lax.fori_loop(1, 4, step, 0)

    def greet(tgx, tgy):
        pl.semaphore_signal(barrier, inc=1, device_id=(tgx, tgy), device_id_type=MESH)

    to_peers(greet)

    lane = iota((128, 128), 1)
    sub = iota((128, 128), 0)
    eye = lane == sub

    def to_col(row):
        return jnp.sum(jnp.where(eye, jnp.broadcast_to(row, (128, 128)), 0.0), axis=1, keepdims=True)

    def to_row(col):
        return jnp.sum(jnp.where(eye, jnp.broadcast_to(col, (128, 128)), 0.0), axis=0, keepdims=True)

    upper = jnp.where(sub < lane, 1.0, 0.0).astype(BF16)
    seen = jnp.zeros((128, 1), F32)
    want_high = jnp.zeros((128, 128), F32)
    want_low = jnp.zeros((128, 128), F32)
    for block in range(8):
        named = gcol_ref[block : block + 1, :]
        source, local = named >> 10, named & 1023
        hit = jnp.broadcast_to(source, (128, 128)) == sub
        onehot = jnp.where(hit, 1.0, 0.0)
        before = dot(onehot.astype(BF16), upper) + seen
        seen = seen + jnp.sum(onehot, axis=1, keepdims=True)
        rank = jnp.sum(jnp.where(hit, before, 0.0), axis=0, keepdims=True)
        qrow[block : block + 1, :] = peers.position(source).astype(F32) * 8.0 + rank
        ranked = jnp.broadcast_to(rank, (128, 128)) == sub.astype(F32)
        high = (local >> 5).astype(F32)
        low = (local & 31).astype(F32)
        zero = jnp.zeros((128, 128), F32)
        chosen_high = jnp.where(ranked, jnp.broadcast_to(high, (128, 128)), zero).astype(BF16)
        chosen_low = jnp.where(ranked, jnp.broadcast_to(low, (128, 128)), zero).astype(BF16)
        onehot = onehot.astype(BF16)
        want_high = want_high + dot_nt(onehot, chosen_high)
        want_low = want_low + dot_nt(onehot, chosen_low)
    wv[...] = want_high * 32.0 + want_low

    def row_out(s, carry):
        for y in range(NY):
            wq[s * NY + y] = wv[pl.ds(s * NY + y, 1), :]
        return carry

    lax.fori_loop(0, NX, row_out, 0)
    pl.semaphore_wait(barrier, ND - 1)

    def ask(tgx, tgy):
        pltpu.make_async_remote_copy(
            wq.at[tgx * NY + tgy], req.at[me], wsend, wrecv,
            device_id=(tgx, tgy), device_id_type=MESH,
        ).start()

    to_peers(ask)
    own_ask = pltpu.make_async_copy(wq.at[me], req.at[me], loc_sem.at[0])
    own_ask.start()
    others = req.at[pl.ds(0, ND - 1)]

    def copy_to(src, dst, send, recv, dgx, dgy):
        return pltpu.make_async_remote_copy(
            src, dst, send, recv,
            device_id=((gx + dgx + NX) % NX, (gy + dgy + NY) % NY),
            device_id_type=MESH,
        )

    def send_halo(h):
        for f in range(2):
            field = 2 * h + f

            for k in range(16):
                part = pl.ds(k * 4, 4)
                sx[h, 0, f, part, :] = st[field, pl.ds((15 * 16 + k) * 16 + 12, 4), :]
                sx[h, 1, f, part, :] = st[field, pl.ds(k * 16, 4), :]
                sy[h, 0, f, part, :] = st[field, pl.ds((k * 16 + 15) * 16 + 3, 4, stride=4), :]
                sy[h, 1, f, part, :] = st[field, pl.ds(k * 256, 4, stride=4), :]
            for at, (_, _, _, x, y, n) in enumerate(CORNERS):
                sc[h, at, f : f + 1, :] = st[field, pl.ds((x * 16 + y) * 16 + n, 1), :]
        copies = [
            copy_to(sx.at[h, 0], rx.at[h, 0], hsend.at[h, 0], hrecv.at[h, 0], 1, 0),
            copy_to(sx.at[h, 1], rx.at[h, 1], hsend.at[h, 1], hrecv.at[h, 1], -1, 0),
            copy_to(sy.at[h, 0], ry.at[h, 0], hsend.at[h, 2], hrecv.at[h, 2], 0, 1),
            copy_to(sy.at[h, 1], ry.at[h, 1], hsend.at[h, 3], hrecv.at[h, 3], 0, -1),
        ]
        for at, (dgx, dgy, to, _, _, _) in enumerate(CORNERS):
            copies.append(
                copy_to(sc.at[h, at], rc.at[h, at], hsend.at[h, to], hrecv.at[h, to], dgx, dgy)
            )
        for copy in copies:
            copy.start()
        return copies

    def take_halo(h, copies):
        for copy in copies:
            copy.wait_recv()
        for f in range(2):
            field = 2 * h + f
            for k in range(16):
                part = pl.ds(k * 4, 4)
                halo[field, pl.ds((WEST + 1 + k) * 16 + 12, 4), :] = rx[h, 0, f, part, :]
                halo[field, pl.ds((EAST + 1 + k) * 16, 4), :] = rx[h, 1, f, part, :]
                halo[field, pl.ds((SOUTH + k) * 16 + 3, 4, stride=4), :] = ry[h, 0, f, part, :]
                halo[field, pl.ds((NORTH + k) * 16, 4, stride=4), :] = ry[h, 1, f, part, :]
            halo[field, pl.ds(WEST * 16 + 15, 1), :] = rc[h, 0, f : f + 1, :]
            halo[field, pl.ds(EAST * 16 + 3, 1), :] = rc[h, 1, f : f + 1, :]
            halo[field, pl.ds((WEST + 17) * 16 + 12, 1), :] = rc[h, 2, f : f + 1, :]
            halo[field, pl.ds((EAST + 17) * 16, 1), :] = rc[h, 3, f : f + 1, :]

    s8 = iota((8, 128), 0)
    b_at = s8 & 3
    is_b0, is_b3, first_a = b_at == 0, b_at == 3, s8 < 4
    b_scale = jnp.where(is_b0 | is_b3, 0.5, 1.0)
    scale0 = b_scale * jnp.where(first_a, 0.5, 1.0)
    scale1 = b_scale * jnp.where(first_a, 1.0, 0.5)

    def dynamics(h):
        def column(x, carry):
            fixed = isinstance(x, int)

            def rows(x, y, v):
                inside = 0 <= y < TY
                if fixed and x == -1:
                    return halo, (WEST + y + 1) * 16 + v * 8
                if fixed and x == TX:
                    return halo, (EAST + y + 1) * 16 + v * 8
                if not inside:
                    return halo, ((SOUTH if y < 0 else NORTH) + x) * 16 + v * 8
                return st, x * 256 + y * 16 + v * 8

            def load(field, x, y, v):
                ref, at = rows(x, y, v)
                return ref[field, pl.ds(at if fixed else pl.multiple_of(at, 8), 8), :]

            def along_x(y):
                found = []
                for f in range(2):
                    field = 2 * h + f
                    own0, own1 = load(field, x, y, 0), load(field, x, y, 1)
                    before, after = load(field, x - 1, y, 1), load(field, x + 1, y, 0)
                    found.append(own0 + jnp.where(first_a, pltpu.roll(before, 4, 0), 0.0))
                    found.append(own1 + jnp.where(first_a, 0.0, pltpu.roll(after, 4, 0)))
                return found

            south, here = along_x(-1), along_x(0)
            for y in range(TY):
                north = along_x(y + 1)
                for f in range(2):
                    parts = []
                    for v, scale in ((2 * f, scale0), (2 * f + 1, scale1)):
                        edge = jnp.where(is_b0, pltpu.roll(south[v], 5, 0), 0.0)
                        edge = jnp.where(is_b3, pltpu.roll(north[v], 3, 0), edge)
                        parts.append((here[v] + edge) * scale)
                    total = jnp.concatenate(parts, axis=0)
                    at = x * 256 + y * 16
                    dyn[2 * h + f, pl.ds(at if fixed else pl.multiple_of(at, 16), 16), :] = total
                    high = total.astype(BF16)
                    dyn_high[y * 16 : y * 16 + 16, f * 128 : f * 128 + 128] = high
                    low = (total - high.astype(F32)).astype(BF16)
                    dyn_low[y * 16 : y * 16 + 16, f * 128 : f * 128 + 128] = low
                south, here = here, north
            main = dot(table_ref[512:640, :], dyn_high[...])
            rest = dot(table_ref[512:576, :], dyn_low[...])
            total = main[0:64] + main[64:128] + rest
            cols[pl.ds(x * 64 if fixed else pl.multiple_of(x * 64, 64), 64), :] = total.astype(BF16)
            return carry

        column(0, 0)
        lax.fori_loop(1, TX - 1, column, 0)
        column(TX - 1, 0)

    wide = iota((128, 1024), 1)

    def selections():
        k_mask = iota((128, 128), 1) == (iota((128, 128), 0) & 7)

        def build(b, carry):
            found = peers.block(b, with_self=True)
            for part in range(2):
                asked = [
                    jnp.broadcast_to(req[tgx * NY + tgy], (8, 128))
                    for tgx, tgy, _, _ in found[part * 16 : part * 16 + 16]
                ]
                asked = jnp.where(k_mask, jnp.concatenate(asked, axis=0), 0.0)
                asked = jnp.sum(asked, axis=1, keepdims=True).astype(I32)
                slot_at, piece = asked >> 2, asked & 3
                tile = jnp.zeros((128, 128), F32)
                for u in range(2):
                    cell = cell_ref[u : u + 1, :]
                    names = (((cell >> 7) & 15) * 16 + (cell & 15)).astype(F32)
                    names = jnp.broadcast_to(names, (128, 128))
                    tile = tile + jnp.where(slot_at == lane + 128 * u, names, 0.0)
                tile = jnp.sum(tile, axis=1, keepdims=True).astype(I32)
                at = (tile >> 4) * 64 + (piece >> 1) * 32 + (tile & 15) * 2 + (piece & 1)
                block = b * 2 + part
                rows = pl.ds(pl.multiple_of(block * 128, 128), 128)
                sel[rows, :] = jnp.where(wide == at, 1.0, 0.0).astype(BF16)
                crow[pl.ds(block, 1), :] = to_row(at.astype(F32))
            return carry

        lax.fori_loop(0, 4, build, 0)

    def transposed(row_ref, out_ref):
        def build(block, carry):
            rows = pl.ds(pl.multiple_of(block * 128, 128), 128)
            want = (sub + block * 128).astype(F32)
            for u in range(8):
                names = jnp.broadcast_to(row_ref[u : u + 1, :], (128, 128))
                out_ref[rows, u * 128 : (u + 1) * 128] = jnp.where(names == want, 1.0, 0.0).astype(BF16)
            return carry

        lax.fori_loop(0, 8, build, 0)

    def placing():
        def build(block, carry):
            rows = pl.ds(pl.multiple_of(block * 128, 128), 128)
            at = to_col(qrow[pl.ds(block, 1), :]).astype(I32)
            place[rows, :] = jnp.where(wide == at, 1.0, 0.0).astype(BF16)
            return carry

        lax.fori_loop(0, 8, build, 0)

    def permute_and_send(matrix, source, src, dst, h, send, recv, loc):
        def step(b):
            rows = pl.ds(pl.multiple_of(b * 256, 256), 256)
            moved = dot(matrix[rows, :], source[...])
            src[h, pl.ds(b * 32, 32)] = moved.reshape(32, 8, 256).astype(BF16)
            for tgx, tgy, at, back in peers.block(b):
                pltpu.make_async_remote_copy(
                    src.at[h, at], dst.at[h, back], send.at[h], recv.at[h],
                    device_id=(tgx, tgy), device_id_type=MESH,
                ).start()

        def loop_step(b, carry):
            step(b)
            return carry

        step(0)
        own = pltpu.make_async_copy(src.at[h, 0], dst.at[h, 0], loc_sem.at[loc])
        own.start()
        lax.fori_loop(1, 4, loop_step, 0)
        return own

    def wait_all(ref, h, sem):
        block = ref.at[h, pl.ds(0, ND - 1)]
        pltpu.make_async_copy(block, block, sem.at[h]).wait()

    def flatten(src, h):
        def step(block, carry):
            part = src[h, pl.ds(block * 16, 16)].astype(F32).reshape(128, 256)
            flat[pl.ds(pl.multiple_of(block * 128, 128), 128), :] = part.astype(BF16)
            return carry

        lax.fori_loop(0, 8, step, 0)

    halo_copies, forward, back_copies = [None] * NH, [None] * NH, [None] * NH
    for h in range(NH):
        halo_copies[h] = send_halo(h)
    transposed(qrow, place_t)
    placing()
    grid[...] = jnp.zeros_like(grid)
    for h in range(NH):
        take_halo(h, halo_copies[h])
        dynamics(h)
        if h == 0:
            own_ask.wait()
            pltpu.make_async_copy(others, others, wrecv).wait()
            selections()
        forward[h] = permute_and_send(sel, cols, outb, incb, h, fsend, frecv, 1 + h)

    transposed(crow, sel_t)

    def physics(h):
        def step(block, carry):
            rows = pl.ds(pl.multiple_of(block * 256, 256), 256)
            moved = dot(place[rows, :], flat[...])
            for g in range(16):
                part = moved[g * 16 : (g + 1) * 16, :]
                stacked = jnp.concatenate([part[:, :128], part[:, 128:]], axis=0)
                smooth = dot_nt(stacked.astype(BF16), inv[block * 16 + g])
                change = smooth - stacked
                change = jnp.concatenate([change[:16], change[16:]], axis=1)
                tend[pl.ds(pl.multiple_of(block * 256 + g * 16, 16), 16), :] = change.astype(BF16)
            return carry

        lax.fori_loop(0, 4, step, 0)

    for h in range(NH):
        forward[h].wait()
        wait_all(incb, h, frecv)
        flatten(incb, h)
        physics(h)
        back_copies[h] = permute_and_send(place_t, tend, backb, rcvb, h, bsend, brecv, 3 + h)

    ring_copies = []

    def finish(h):
        def add(x, carry):
            rows = pl.ds(pl.multiple_of(x * 256, 256), 256)
            near = gridb[pl.ds(pl.multiple_of(x * RX, 16), 256), :]
            update = dot(table_ref[0:512, :], near)
            update = update[:256] + update[256:]
            for f in range(2):
                field = 2 * h + f
                dyn[field, rows, :] = dyn[field, rows, :] + update[:, f * LEV : (f + 1) * LEV]
            return carry

        lax.fori_loop(0, TX, add, 0)

    for h in range(NH):
        back_copies[h].wait()
        wait_all(rcvb, h, brecv)
        flatten(rcvb, h)

        def ungroup(block, carry):
            rows = pl.ds(pl.multiple_of(block * 256, 256), 256)
            moved = dot(sel_t[rows, :], flat[...])
            for x in range(4):
                for i in range(2):
                    base = pl.multiple_of((block * 4 + x + 1) * RX + i * 40, 8)
                    piece = moved[x * 64 + i * 32 : x * 64 + i * 32 + 32, :]
                    for u in range(2):
                        grid[h, u, pl.ds(base, 32), :] = piece[:, u * 128 : (u + 1) * 128]
            return carry

        lax.fori_loop(0, 4, ungroup, 0)
        for u in range(2):
            for i in range(2):
                tx[h, 0, u, i * 32 : i * 32 + 32, :] = grid[h, u, 16 * RX + i * 40 : 16 * RX + i * 40 + 32, :]
                tx[h, 1, u, i * 32 : i * 32 + 32, :] = grid[h, u, RX + i * 40 : RX + i * 40 + 32, :]
            for j in range(2):
                ty[h, 0, u, j * 32 : j * 32 + 32, :] = grid[h, u, pl.ds(RX + 30 + j, 32, stride=40), :]
                ty[h, 1, u, j * 32 : j * 32 + 32, :] = grid[h, u, pl.ds(RX + j, 32, stride=40), :]
            for at, (_, _, _, x, y, _) in enumerate(CORNERS):
                for i in range(2):
                    base = (x + 1) * RX + i * 40 + 2 * y
                    tc[h, at, u * 4 + i * 2 : u * 4 + i * 2 + 2, :] = grid[h, u, base : base + 2, :]
        copies = [
            copy_to(tx.at[h, 0], ux.at[h, 0], gsend.at[h, 0], grecv.at[h, 0], 1, 0),
            copy_to(tx.at[h, 1], ux.at[h, 1], gsend.at[h, 1], grecv.at[h, 1], -1, 0),
            copy_to(ty.at[h, 0], uy.at[h, 0], gsend.at[h, 2], grecv.at[h, 2], 0, 1),
            copy_to(ty.at[h, 1], uy.at[h, 1], gsend.at[h, 3], grecv.at[h, 3], 0, -1),
        ]
        for at, (dgx, dgy, to, _, _, _) in enumerate(CORNERS):
            copies.append(
                copy_to(tc.at[h, at], uc.at[h, at], gsend.at[h, to], grecv.at[h, to], dgx, dgy)
            )
        for copy in copies:
            copy.start()
        ring_copies.append(copies)

    for h in range(NH):
        for copy in ring_copies[h]:
            copy.wait_recv()
        for u in range(2):
            for i in range(2):
                part = slice(i * 32, i * 32 + 32)
                grid[h, u, i * 40 : i * 40 + 32, :] = ux[h, 0, u, part, :]
                grid[h, u, 17 * RX + i * 40 : 17 * RX + i * 40 + 32, :] = ux[h, 1, u, part, :]
            for j in range(2):
                part = slice(j * 32, j * 32 + 32)
                grid[h, u, pl.ds(RX + 32 + j, 32, stride=40), :] = uy[h, 0, u, part, :]
                grid[h, u, pl.ds(RX + 34 + j, 32, stride=40), :] = uy[h, 1, u, part, :]
            for at, (big_x, base) in enumerate(((0, 32), (17, 32), (0, 34), (17, 34))):
                for i in range(2):
                    to = big_x * RX + i * 40 + base
                    grid[h, u, to : to + 2, :] = uc[h, at, u * 4 + i * 2 : u * 4 + i * 2 + 2, :]
            gridb[:, u * 128 : (u + 1) * 128] = grid[h, u].astype(BF16)
        finish(h)


    pltpu.make_async_copy(others, others, wsend).wait()
    for h in range(NH):
        wait_all(outb, h, fsend)
        wait_all(backb, h, bsend)
        for copy in halo_copies[h] + ring_copies[h]:
            copy.wait_send()


def place_kernel(cell_ref, total, out_hbm, sem):
    def step(s, carry):
        for k in range(8):
            at = s * 8 + k
            cell = cell_ref[at]
            tile = ((cell >> 7) & 15) * 16 + (cell & 15)
            pltpu.make_async_copy(total.at[:, tile], out_hbm.at[:, at], sem).start()
        return carry

    lax.fori_loop(0, NE // 8, step, 0)
    pltpu.make_async_copy(total, out_hbm, sem).wait()


def any_spec():
    return pl.BlockSpec(memory_space=pl.ANY)


def in_hbm(array):
    return pltpu.with_memory_space_constraint(array, pltpu.HBM)


def vmem_spec():
    return pl.BlockSpec(memory_space=pltpu.VMEM)


def smem_spec():
    return pl.BlockSpec(memory_space=pltpu.SMEM)


def per_device(table, state_in, stiffness, elem_cell, group_column, group_inverse):
    state = state_in.reshape(4, NE * 16, LEV)
    dma = pltpu.SemaphoreType.DMA
    vmem = pltpu.VMEM
    whole = jax.ShapeDtypeStruct((4, NE * 16, LEV), F32)
    combined = pl.pallas_call(
        combine_kernel,
        out_shape=whole,
        in_specs=[smem_spec(), any_spec(), any_spec()],
        out_specs=vmem_spec(),
        scratch_shapes=[
            vmem((4, NE * 16, LEV), F32),
            vmem((256, 256), F32),
            vmem((2, NE * 16, LEV), F32),
            dma,
            dma((8,)),
        ],
        compiler_params=pltpu.CompilerParams(vmem_limit_bytes=30 << 20),
        name="combine",
    )(elem_cell, in_hbm(state), stiffness.reshape(256, NE))
    scratch = [
        vmem((4, NHALO * 16, LEV), F32),
        vmem((128, 128), F32),
        vmem((ND, 1, 128), F32),
        vmem((ND, 1, 128), F32),
        vmem((8, 128), F32),
        vmem((8, 128), F32),
        vmem((NC, NC), BF16),
        vmem((NC, NC), BF16),
        vmem((NC, NC), BF16),
        vmem((NC, NC), BF16),
        vmem((256, 256), BF16),
        vmem((256, 256), BF16),
        vmem((NC, 256), BF16),
        vmem((NH, ND, 8, 256), BF16),
        vmem((NH, ND, 8, 256), BF16),
        vmem((NH, ND, 8, 256), BF16),
        vmem((NH, ND, 8, 256), BF16),
        vmem((NC, 256), BF16),
        vmem((NC, 256), BF16),
        vmem((NH, 2, RROWS, LEV), F32),
        vmem((RROWS, 256), BF16),
        vmem((NH, 2, 2, 64, LEV), F32),
        vmem((NH, 2, 2, 64, LEV), F32),
        vmem((NH, 4, 8, LEV), F32),
        vmem((NH, 2, 2, 64, LEV), F32),
        vmem((NH, 2, 2, 64, LEV), F32),
        vmem((NH, 4, 8, LEV), F32),
        vmem((NH, 2, 2, 64, LEV), F32),
        vmem((NH, 2, 2, 64, LEV), F32),
        vmem((NH, 4, 8, LEV), F32),
        vmem((NH, 2, 2, 64, LEV), F32),
        vmem((NH, 2, 2, 64, LEV), F32),
        vmem((NH, 4, 8, LEV), F32),
        dma, dma, dma((5,)),
        dma((NH,)), dma((NH,)), dma((NH,)), dma((NH,)),
        dma((NH, 8)), dma((NH, 8)), dma((NH, 8)), dma((NH, 8)),
    ]
    total = pl.pallas_call(
        exchange_kernel,
        out_shape=whole,
        in_specs=[vmem_spec()] * 5,
        out_specs=vmem_spec(),
        scratch_shapes=scratch,
        compiler_params=pltpu.CompilerParams(
            collective_id=0, has_side_effects=True, vmem_limit_bytes=28 << 20
        ),
        name="exchange",
    )(combined, elem_cell.reshape(2, 128), group_column.reshape(8, 128), group_inverse, table)
    return pl.pallas_call(
        place_kernel,
        out_shape=jax.ShapeDtypeStruct((4, NE, 16, LEV), F32),
        in_specs=[smem_spec(), vmem_spec()],
        out_specs=any_spec(),
        scratch_shapes=[dma],
        compiler_params=pltpu.CompilerParams(vmem_limit_bytes=4 << 20),
        name="place",
    )(elem_cell, total.reshape(4, NE, 16, LEV))


def solution(mesh):
    table = constant_tables()
    placed = (
        P(None, ("gx", "gy"), None, None),
        P(None, None, ("gx", "gy")),
        P(("gx", "gy")),
        P(("gx", "gy")),
        P(("gx", "gy"), None, None),
    )

    def run(*args):
        body = functools.partial(per_device, jnp.asarray(table))
        return jax.shard_map(
            body,
            mesh=mesh,
            in_specs=placed,
            out_specs=P(None, ("gx", "gy"), None, None),
            check_vma=False,
        )(*args)

    return run
```
